32 devices in a mesh: dp: 8 (over z, y), mp: 4 (over x, core).
Axes of the slice: x: 2, y: 2, z: 4, core: 2. Of those that a mesh axis runs over, the one named last changes fastest.
Arguments:
- sentence_entry_words: bfloat16 [16384, 768], P(('dp', 'mp')), may hold values from -6 to 6
- sentence_present_marks: int32 [1024], P(('dp', 'mp')), may hold values 0 or 1
- picture_present_marks: int32 [1024], P(('dp', 'mp')), may hold values 0 or 1
- matched_picture_positions: int32 [1024], replicated, may hold values from 0 to 1023, each once
- stored_picture_patches: bfloat16 [51200, 768], P(('dp', 'mp')), may hold values from -6 to 6
- log_logit_multiplier: float32 [1], replicated, may hold values from 3.6 to 4.3
- leading_standardizer_stretch: float32 [768], replicated, may hold values from 0.5 to 1.5
- leading_standardizer_shift: float32 [768], replicated, may hold values from -1 to 1
- lookup_coefficients: bfloat16 [768, 768], P(None, 'mp'), may hold values from -0.21875 to 0.21875
- lookup_offset: float32 [768], P('mp'), may hold values from -1 to 1
- address_coefficients: bfloat16 [768, 768], P(None, 'mp'), may hold values from -0.21875 to 0.21875
- content_coefficients: bfloat16 [768, 768], P(None, 'mp'), may hold values from -0.21875 to 0.21875
- content_offset: float32 [768], P('mp'), may hold values from -1 to 1
- mixer_exit_coefficients: bfloat16 [768, 768], P('mp'), may hold values from -0.625 to 0.625
- mixer_exit_offset: float32 [768], replicated, may hold values from -1 to 1
- trailing_standardizer_stretch: float32 [768], replicated, may hold values from 0.5 to 1.5
- trailing_standardizer_shift: float32 [768], replicated, may hold values from -1 to 1
- perceptron_entry_coefficients: bfloat16 [768, 3072], P(None, 'mp'), may hold values from -0.21875 to 0.21875
- perceptron_inner_offset: float32 [3072], P('mp'), may hold values from -1 to 1
- perceptron_exit_coefficients: bfloat16 [3072, 768], P('mp'), may hold values from -0.109375 to 0.109375
- perceptron_exit_offset: float32 [768], replicated, may hold values from -1 to 1
- picture_lookup_coefficients: bfloat16 [768, 768], replicated, may hold values from -0.21875 to 0.21875
- picture_address_coefficients: bfloat16 [768, 768], replicated, may hold values from -0.21875 to 0.21875
- picture_content_coefficients: bfloat16 [768, 768], replicated, may hold values from -0.21875 to 0.21875
- picture_mixer_exit: bfloat16 [768, 768], replicated, may hold values from -0.625 to 0.625
- picture_perceptron_entry: bfloat16 [768, 3072], replicated, may hold values from -0.21875 to 0.21875
- picture_perceptron_exit: bfloat16 [3072, 768], replicated, may hold values from -0.109375 to 0.109375
Outputs:
- loss: float32 [1], replicated
- text_out: bfloat16 [16384, 768], P(('dp', 'mp'))
- text_in_grad: float32 [16384, 768], P(('dp', 'mp'))
- temperature_grad: float32 [1], replicated
- ln1_gain_grad: float32 [768], replicated
- ln1_bias_grad: float32 [768], replicated
- w_query_grad: float32 [768, 768], P(None, 'mp')
- query_bias_grad: float32 [768], P('mp')
- w_key_grad: float32 [768, 768], P(None, 'mp')
- w_value_grad: float32 [768, 768], P(None, 'mp')
- value_bias_grad: float32 [768], P('mp')
- w_attn_out_grad: float32 [768, 768], P('mp')
- attn_out_bias_grad: float32 [768], replicated
- ln2_gain_grad: float32 [768], replicated
- ln2_bias_grad: float32 [768], replicated
- w_hidden_grad: float32 [768, 3072], P(None, 'mp')
- hidden_bias_grad: float32 [3072], P('mp')
- w_proj_grad: float32 [3072, 768], P('mp')
- proj_bias_grad: float32 [768], replicated
The draws below stay inside these ranges and needn't reach their ends.
Inputs may be any that keep to these rules, and one draw needn't show every extreme that they name: `matched_picture_positions`: each index appears exactly once.
All inputs are finite; a program needn't handle non-finite values. No bound on the sum of `sentence_present_marks` or of `picture_present_marks` on one device may be relied on, other than what follows from the above.
Results may differ from the reference program's by a relative error of at most 0.012.
Values may be sent and summed in bfloat16 or wider, within the bound.
A program may use at most 192 MiB of HBM per device.

```python
from functools import partial
import jax
import jax.numpy as jnp
from jax import lax

D = 768
HEADS = 12
HD = 64
FF = 3072
LEN = 16
PATCHES = 50
EXAMPLES = 1024
TEXT_TOKENS = 16384
IMAGE_TOKENS = 51200
N_DP = 8


def plant(values, stream_key, low, largest):
    index_at = [jax.random.randint(jax.random.fold_in(stream_key, axis), (), 0, length) for axis, length in enumerate(values.shape)]
    main_axis = values.shape.index(max(values.shape))
    next_to = index_at[:main_axis] + [(index_at[main_axis] + 1) % values.shape[main_axis]] + index_at[main_axis + 1:]
    return values.at[tuple(index_at)].set(low).at[tuple(next_to)].set(largest)


def block_scale(own_key, extent, cuts, least, top_value):
    def one(position, parts):
        draws = jax.random.uniform(jax.random.fold_in(jax.random.fold_in(own_key, 6), position), (parts,), jnp.float32, least / len(cuts), top_value / len(cuts))
        return jnp.repeat(jnp.exp(draws), extent[position] // parts).reshape((-1,) + (1,) * (len(extent) - position - 1))

    loudness = one(*cuts[0])
    for cut in cuts[1:]:
        loudness = loudness * one(*cut)
    return loudness


def gaussian(own_key, extent, spread, reach, shards=(), kind=jnp.bfloat16):
    gain = block_scale(own_key, extent, shards, -0.22, 0.18) if shards else 1.0
    values = jax.random.normal(own_key, extent, jnp.float32) * spread * gain
    return jnp.minimum(jnp.maximum(values, -reach), reach).astype(kind)


def setup_inputs(seed: int = 0) -> dict:
    seeds = jax.random.split(jax.random.key(seed), 28)
    return {
        "sentence_entry_words": gaussian(seeds[0], (TEXT_TOKENS, D), 1.0, 6.0, ((0, 32),)),
        "sentence_present_marks": plant((jax.random.randint(seeds[1], (EXAMPLES,), 0, 4) < 3).astype(jnp.int32), jax.random.fold_in(seeds[1], 1), 0, 1),
        "picture_present_marks": plant((jax.random.randint(seeds[2], (EXAMPLES,), 0, 4) < 3).astype(jnp.int32), jax.random.fold_in(seeds[2], 1), 0, 1),
        "matched_picture_positions": jax.random.permutation(seeds[3], EXAMPLES).astype(jnp.int32),
        "stored_picture_patches": gaussian(seeds[4], (IMAGE_TOKENS, D), 1.0, 6.0, ((0, 32),)),
        "log_logit_multiplier": jnp.clip(jax.random.uniform(seeds[5], (1,), jnp.float32, 3.6, 4.3), 3.6, 4.3),
        "leading_standardizer_stretch": jnp.clip(1.0 + 0.1 * jax.random.normal(seeds[6], (D,), jnp.float32), 0.5, 1.5),
        "leading_standardizer_shift": gaussian(seeds[7], (D,), 0.2, 1.0, (), jnp.float32),
        "lookup_coefficients": gaussian(seeds[8], (D, D), D ** -0.5, 0.21875, ((1, 4),)),
        "lookup_offset": gaussian(seeds[9], (D,), 0.2, 1.0, ((0, 4),), jnp.float32),
        "address_coefficients": gaussian(seeds[10], (D, D), D ** -0.5, 0.21875, ((1, 4),)),
        "content_coefficients": gaussian(seeds[11], (D, D), D ** -0.5, 0.21875, ((1, 4),)),
        "content_offset": gaussian(seeds[12], (D,), 0.2, 1.0, ((0, 4),), jnp.float32),
        "mixer_exit_coefficients": gaussian(seeds[13], (D, D), (D // 8) ** -0.5, 0.625, ((0, 4),)),
        "mixer_exit_offset": gaussian(seeds[14], (D,), 0.2, 1.0, (), jnp.float32),
        "trailing_standardizer_stretch": jnp.clip(1.0 + 0.1 * jax.random.normal(seeds[15], (D,), jnp.float32), 0.5, 1.5),
        "trailing_standardizer_shift": gaussian(seeds[16], (D,), 0.2, 1.0, (), jnp.float32),
        "perceptron_entry_coefficients": gaussian(seeds[17], (D, FF), D ** -0.5, 0.21875, ((1, 4),)),
        "perceptron_inner_offset": gaussian(seeds[18], (FF,), 0.2, 1.0, ((0, 4),), jnp.float32),
        "perceptron_exit_coefficients": gaussian(seeds[19], (FF, D), FF ** -0.5, 0.109375, ((0, 4),)),
        "perceptron_exit_offset": gaussian(seeds[20], (D,), 0.2, 1.0, (), jnp.float32),
        "picture_lookup_coefficients": gaussian(seeds[21], (D, D), D ** -0.5, 0.21875),
        "picture_address_coefficients": gaussian(seeds[22], (D, D), D ** -0.5, 0.21875),
        "picture_content_coefficients": gaussian(seeds[23], (D, D), D ** -0.5, 0.21875),
        "picture_mixer_exit": gaussian(seeds[24], (D, D), (D // 8) ** -0.5, 0.625),
        "picture_perceptron_entry": gaussian(seeds[25], (D, FF), D ** -0.5, 0.21875),
        "picture_perceptron_exit": gaussian(seeds[26], (FF, D), FF ** -0.5, 0.109375),
    }


@jax.custom_vjp
def low(v):
    return lax.optimization_barrier(v.astype(jnp.bfloat16)).astype(jnp.float32)

@jax.custom_vjp
def low_back(v):
    return v

def low_keep(v):
    return (low(v), None)

def low_pass(kept, grad):
    return (grad,)

def back_keep(v):
    return (v, None)

def back_low(kept, grad):
    return (low(grad),)
low.defvjp(low_keep, low_pass)
low_back.defvjp(back_keep, back_low)

def matmul(left, right):
    return jnp.dot(left, right, precision=lax.Precision.HIGHEST, preferred_element_type=jnp.float32)

def layer_norm(tensor, norm_gain, norm_shift):
    centred = tensor - lax.optimization_barrier(jnp.mean(tensor, axis=-1, keepdims=True))
    variance = lax.optimization_barrier(jnp.mean(centred * centred, axis=-1, keepdims=True))
    return centred * lax.rsqrt(variance + 1e-06) * norm_gain + norm_shift

def normalize(pooled):
    return pooled * lax.rsqrt(lax.optimization_barrier(jnp.sum(pooled * pooled, axis=-1, keepdims=True)) + 1e-06)

def attention(queries, key_rows, value_rows, causal):
    scores = jnp.einsum('gqhd,gkhd->ghqk', queries, key_rows, precision=lax.Precision.HIGHEST) * HD ** (-0.5)
    scores = low_back(scores)
    if causal:
        places = jnp.arange(scores.shape[-1], dtype=jnp.int32)
        scores = jnp.where(places[None, :] <= places[:, None], scores, -1e+30)
    highest = lax.optimization_barrier(jnp.max(scores, axis=-1, keepdims=True))
    weights = jnp.exp(scores - highest)
    attn_probs = low(weights / lax.optimization_barrier(jnp.sum(weights, axis=-1, keepdims=True)))
    return jnp.einsum('ghqk,gkhd->gqhd', attn_probs, value_rows, precision=lax.Precision.HIGHEST)

def block(tensor, params, causal):
    gain_one, shift_one, wq_mat, bq_vec, wk_mat, wv_mat, bv_vec, wo_mat, bo_vec, gain_two, shift_two, wh_mat, bh_vec, wp_mat, bp_vec = params
    groups, length = (tensor.shape[0], tensor.shape[1])
    tokens = tensor.reshape(groups * length, D)
    normed = low(layer_norm(tokens, gain_one, shift_one))
    queries = low(low_back(matmul(normed, wq_mat) + bq_vec))
    key_rows = low(low_back(matmul(normed, wk_mat)))
    value_rows = low(low_back(matmul(normed, wv_mat) + bv_vec))
    grid_shape = (groups, length, HEADS, HD)
    mixed_heads = attention(queries.reshape(grid_shape), key_rows.reshape(grid_shape), value_rows.reshape(grid_shape), causal)
    mixed_heads = low(low_back(mixed_heads.reshape(groups * length, D)))
    middle = tokens + low_back(matmul(mixed_heads, wo_mat)) + bo_vec
    normed_two = low(layer_norm(middle, gain_two, shift_two))
    hidden_pre = low_back(matmul(normed_two, wh_mat) + bh_vec)
    hidden_act = low(jax.nn.gelu(hidden_pre, approximate=True))
    output = middle + low_back(matmul(hidden_act, wp_mat)) + bp_vec
    return output.reshape(groups, length, D)

def masked_lse(logits, keep_mask):
    masked = jnp.where(keep_mask[None, :] > 0, logits, -1e+30)
    highest = lax.optimization_barrier(jnp.max(masked, axis=-1, keepdims=True))
    return highest[:, 0] + jnp.log(lax.optimization_barrier(jnp.sum(jnp.exp(masked - highest), axis=-1)))

def reference(sentence_entry_words, sentence_present_marks, picture_present_marks, matched_picture_positions, stored_picture_patches, log_logit_multiplier, leading_standardizer_stretch, leading_standardizer_shift, lookup_coefficients, lookup_offset, address_coefficients, content_coefficients, content_offset, mixer_exit_coefficients, mixer_exit_offset, trailing_standardizer_stretch, trailing_standardizer_shift, perceptron_entry_coefficients, perceptron_inner_offset, perceptron_exit_coefficients, perceptron_exit_offset, picture_lookup_coefficients, picture_address_coefficients, picture_content_coefficients, picture_mixer_exit, picture_perceptron_entry, picture_perceptron_exit):
    group_size = EXAMPLES // N_DP
    unit_gain = jnp.ones((D,), jnp.float32)
    zero_width = jnp.zeros((D,), jnp.float32)
    zero_hidden = jnp.zeros((FF,), jnp.float32)
    frozen = (unit_gain, zero_width, picture_lookup_coefficients.astype(jnp.float32), zero_width, picture_address_coefficients.astype(jnp.float32), picture_content_coefficients.astype(jnp.float32), zero_width, picture_mixer_exit.astype(jnp.float32), zero_width, unit_gain, zero_width, picture_perceptron_entry.astype(jnp.float32), zero_hidden, picture_perceptron_exit.astype(jnp.float32), zero_width)
    cache_groups = stored_picture_patches.astype(jnp.float32).reshape(N_DP, group_size, PATCHES, D)

    def image_group(piece):
        return low(normalize(lax.optimization_barrier(jnp.mean(block(piece, frozen, False), axis=1))))
    image_emb = lax.map(image_group, cache_groups).reshape(EXAMPLES, D)
    text_mask = sentence_present_marks.astype(jnp.float32)
    image_mask = picture_present_marks.astype(jnp.float32)
    order = jnp.arange(EXAMPLES, dtype=jnp.int32)
    inverse = jnp.zeros((EXAMPLES,), jnp.int32).at[matched_picture_positions].set(order)
    pair_valid = text_mask * image_mask[matched_picture_positions]
    image_weight = pair_valid[inverse]

    def forward(tokens, temp, *params):
        pieces = tokens.reshape(N_DP, group_size, LEN, D)
        runner = jax.checkpoint(partial(block, params=params, causal=True))
        outputs = lax.map(runner, pieces).reshape(EXAMPLES, LEN, D)
        text_emb = low(normalize(lax.optimization_barrier(jnp.mean(outputs, axis=1))))
        logit_multiplier = jnp.exp(temp[0])
        row_logits = logit_multiplier * low_back(matmul(text_emb, image_emb.T))
        column_logits = logit_multiplier * low_back(matmul(image_emb, text_emb.T))
        row_loss = masked_lse(row_logits, image_mask) - jnp.take_along_axis(row_logits, matched_picture_positions[:, None], axis=1)[:, 0]
        column_loss = masked_lse(column_logits, text_mask) - jnp.take_along_axis(column_logits, inverse[:, None], axis=1)[:, 0]
        total = 0.5 * (jnp.sum(pair_valid * row_loss) + jnp.sum(image_weight * column_loss))
        return (total, outputs.reshape(TEXT_TOKENS, D))
    forward_arguments = (sentence_entry_words.astype(jnp.float32), log_logit_multiplier, leading_standardizer_stretch, leading_standardizer_shift, lookup_coefficients.astype(jnp.float32), lookup_offset, address_coefficients.astype(jnp.float32), content_coefficients.astype(jnp.float32), content_offset, mixer_exit_coefficients.astype(jnp.float32), mixer_exit_offset, trailing_standardizer_stretch, trailing_standardizer_shift, perceptron_entry_coefficients.astype(jnp.float32), perceptron_inner_offset, perceptron_exit_coefficients.astype(jnp.float32), perceptron_exit_offset)
    total, pullback, outputs = jax.vjp(forward, *forward_arguments, has_aux=True)
    grads = pullback(jnp.ones_like(total))
    loss = jnp.reshape(total / jnp.sum(pair_valid), (1,))
    return (loss, outputs.astype(jnp.bfloat16), grads[0], grads[1], grads[2], grads[3], grads[4], grads[5], grads[6], grads[7], grads[8], grads[9], grads[10], grads[11], grads[12], grads[13], grads[14], grads[15], grads[16])
```

```python
from functools import partial

import jax
import jax.numpy as jnp
from jax import lax
from jax.sharding import PartitionSpec as P

D = 768
HEADS = 12
HD = 64
LEN = 16
PATCHES = 50


def layer_norm(tensor, norm_gain, norm_shift):
    centred = tensor - jnp.mean(tensor, axis=-1, keepdims=True)
    variance = jnp.mean(centred * centred, axis=-1, keepdims=True)
    return centred * lax.rsqrt(variance + 1e-06) * norm_gain + norm_shift


def normalize(pooled):
    return pooled * lax.rsqrt(jnp.sum(pooled * pooled, axis=-1, keepdims=True) + 1e-06)


def product(left, right):
    return jnp.dot(left, right, preferred_element_type=jnp.float32)


def masked_scores(queries, key_rows, causal):
    scores = jnp.einsum(
        "gqhd,gkhd->ghqk", queries, key_rows, preferred_element_type=jnp.float32
    ) * HD ** (-0.5)
    if causal:
        places = jnp.arange(scores.shape[-1], dtype=jnp.int32)
        scores = jnp.where(places[None, :] <= places[:, None], scores, -1e30)
    return scores


def softmax_rows(scores):
    highest = jnp.max(scores, axis=-1, keepdims=True)
    weights = jnp.exp(scores - highest)
    totals = jnp.sum(weights, axis=-1, keepdims=True)
    return (weights / totals, highest + jnp.log(totals))


def attention_back(queries, key_rows, value_rows, log_totals, mixed_grad):
    scores = masked_scores(queries, key_rows, True)
    attn_probs = jnp.exp(scores - log_totals)
    probs_grad = jnp.einsum(
        "gqhd,gkhd->ghqk", mixed_grad, value_rows, preferred_element_type=jnp.float32
    )
    value_grad = jnp.einsum(
        "ghqk,gqhd->gkhd",
        attn_probs.astype(jnp.bfloat16),
        mixed_grad,
        preferred_element_type=jnp.float32,
    )
    inner_sum = jnp.sum(attn_probs * probs_grad, axis=-1, keepdims=True)
    score_grad = (attn_probs * (probs_grad - inner_sum)).astype(jnp.bfloat16)
    query_grad = jnp.einsum(
        "ghqk,gkhd->gqhd", score_grad, key_rows, preferred_element_type=jnp.float32
    ) * HD ** (-0.5)
    key_grad = jnp.einsum(
        "ghqk,gqhd->gkhd", score_grad, queries, preferred_element_type=jnp.float32
    ) * HD ** (-0.5)
    return (query_grad, key_grad, value_grad)


def image_embed(stored_picture_patches, frozen):
    (
        picture_lookup_coefficients,
        picture_address_coefficients,
        picture_content_coefficients,
        picture_mixer_exit,
        picture_perceptron_entry,
        picture_perceptron_exit,
    ) = frozen
    tokens = stored_picture_patches.astype(jnp.float32)
    examples = tokens.shape[0] // PATCHES
    normed = layer_norm(tokens, 1.0, 0.0).astype(jnp.bfloat16)
    grid_shape = (examples, PATCHES, HEADS, HD)
    queries = product(normed, picture_lookup_coefficients).astype(jnp.bfloat16).reshape(grid_shape)
    key_rows = (
        product(normed, picture_address_coefficients).astype(jnp.bfloat16).reshape(grid_shape)
    )
    value_rows = (
        product(normed, picture_content_coefficients).astype(jnp.bfloat16).reshape(grid_shape)
    )
    attn_probs, unused_totals = softmax_rows(masked_scores(queries, key_rows, False))
    mixed_heads = jnp.einsum(
        "ghqk,gkhd->gqhd",
        attn_probs.astype(jnp.bfloat16),
        value_rows,
        preferred_element_type=jnp.float32,
    )
    mixed_heads = mixed_heads.reshape(examples * PATCHES, D).astype(jnp.bfloat16)
    middle = tokens + product(mixed_heads, picture_mixer_exit)
    normed_two = layer_norm(middle, 1.0, 0.0).astype(jnp.bfloat16)
    hidden_act = jax.nn.gelu(
        product(normed_two, picture_perceptron_entry), approximate=True
    ).astype(jnp.bfloat16)
    output = middle + product(hidden_act, picture_perceptron_exit)
    return normalize(jnp.mean(output.reshape(examples, PATCHES, D), axis=1)).astype(jnp.bfloat16)


def embed(block_out):
    return normalize(jnp.mean(block_out.reshape(-1, LEN, D), axis=1))


def body(
    sentence_entry_words,
    sentence_present_marks,
    picture_present_marks,
    matched_picture_positions,
    stored_picture_patches,
    log_logit_multiplier,
    leading_standardizer_stretch,
    leading_standardizer_shift,
    lookup_coefficients,
    lookup_offset,
    address_coefficients,
    content_coefficients,
    content_offset,
    mixer_exit_coefficients,
    mixer_exit_offset,
    trailing_standardizer_stretch,
    trailing_standardizer_shift,
    perceptron_entry_coefficients,
    perceptron_inner_offset,
    perceptron_exit_coefficients,
    perceptron_exit_offset,
    picture_lookup_coefficients,
    picture_address_coefficients,
    picture_content_coefficients,
    picture_mixer_exit,
    picture_perceptron_entry,
    picture_perceptron_exit,
):
    own_count = sentence_present_marks.shape[0]
    mp_count = lax.axis_size("mp")
    rank = lax.axis_index("mp")
    text_mask, image_mask = (
        lax.all_gather(sentence_present_marks.astype(jnp.float32), ("dp", "mp"), axis=0, tiled=True),
        lax.all_gather(picture_present_marks.astype(jnp.float32), ("dp", "mp"), axis=0, tiled=True),
    )
    wide = partial(lax.all_gather, axis_name="mp", axis=1, tiled=True)
    tall = partial(lax.all_gather, axis_name="mp", axis=0, tiled=True)
    w_q, w_k, w_v, w_o = (
        wide(lookup_coefficients),
        wide(address_coefficients),
        wide(content_coefficients),
        tall(mixer_exit_coefficients),
    )
    w_h, w_p = (wide(perceptron_entry_coefficients), tall(perceptron_exit_coefficients))
    b_q, b_v, b_h = (tall(lookup_offset), tall(content_offset), tall(perceptron_inner_offset))
    image_half = image_embed(
        stored_picture_patches,
        (
            picture_lookup_coefficients,
            picture_address_coefficients,
            picture_content_coefficients,
            picture_mixer_exit,
            picture_perceptron_entry,
            picture_perceptron_exit,
        ),
    )
    all_image = lax.all_gather(image_half, ("dp", "mp"), axis=0, tiled=True)
    tokens = sentence_entry_words.astype(jnp.float32)
    all_rows = tokens.shape[0]
    normed_one, norm_one_back = jax.vjp(
        layer_norm, tokens, leading_standardizer_stretch, leading_standardizer_shift
    )
    normed_one = normed_one.astype(jnp.bfloat16)
    grid_shape = (all_rows // LEN, LEN, HEADS, HD)
    queries = (product(normed_one, w_q) + b_q).astype(jnp.bfloat16).reshape(grid_shape)
    key_rows = product(normed_one, w_k).astype(jnp.bfloat16).reshape(grid_shape)
    value_rows = (product(normed_one, w_v) + b_v).astype(jnp.bfloat16).reshape(grid_shape)
    attn_probs, log_totals = softmax_rows(masked_scores(queries, key_rows, True))
    mixed_heads = jnp.einsum(
        "ghqk,gkhd->gqhd",
        attn_probs.astype(jnp.bfloat16),
        value_rows,
        preferred_element_type=jnp.float32,
    )
    mixed_heads = mixed_heads.reshape(all_rows, D).astype(jnp.bfloat16)
    middle = tokens + product(mixed_heads, w_o) + mixer_exit_offset
    normed_two, norm_two_back = jax.vjp(
        layer_norm, middle, trailing_standardizer_stretch, trailing_standardizer_shift
    )
    normed_two = normed_two.astype(jnp.bfloat16)
    hidden_pre = product(normed_two, w_h) + b_h
    hidden_act, gelu_back = jax.vjp(partial(jax.nn.gelu, approximate=True), hidden_pre)
    hidden_act = hidden_act.astype(jnp.bfloat16)
    output = middle + product(hidden_act, w_p) + perceptron_exit_offset
    text_emb, embed_back = jax.vjp(embed, output)
    text_half = text_emb.astype(jnp.bfloat16)

    everyone = text_mask.shape[0]
    order = jnp.arange(everyone, dtype=jnp.int32)
    offset = lax.axis_index(("dp", "mp")) * own_count
    own_pair = lax.dynamic_slice_in_dim(matched_picture_positions, offset, own_count, 0)
    own_text = sentence_present_marks.astype(jnp.float32)
    hits = (order[None, :] == own_pair[:, None]).astype(jnp.float32)
    text_weight = own_text * jnp.sum(hits * image_mask[None, :], axis=1)
    inverse = jnp.zeros((everyone,), jnp.int32).at[matched_picture_positions].set(order)
    image_weight = image_mask * text_mask[inverse]
    logit_multiplier = jnp.exp(log_logit_multiplier[0])
    logits = logit_multiplier * jnp.einsum(
        "id,jd->ij", text_half, all_image, preferred_element_type=jnp.float32
    )
    weights = jnp.exp(logits)
    row_weights = weights * image_mask[None, :]
    row_total = jnp.sum(row_weights, axis=1)
    column_weights = weights * own_text[:, None]
    column_total = lax.psum(jnp.sum(column_weights, axis=0), ("dp", "mp"))
    pair_total = jnp.sum(image_weight)
    safe_row = jnp.where(row_total > 0, row_total, 1.0)
    safe_column = jnp.where(column_total > 0, column_total, 1.0)
    hit_logit = jnp.sum(hits * logits, axis=1)
    column_part = 0.5 * jnp.sum(image_weight * jnp.log(safe_column))
    total_part = 0.5 * jnp.sum(text_weight * jnp.log(safe_row)) - jnp.sum(text_weight * hit_logit)
    row_grad = 0.5 * text_weight[:, None] * (row_weights / safe_row[:, None] - hits)
    column_grad = 0.5 * image_weight[None, :] * (column_weights / safe_column[None, :] - hits)
    temp_part = jnp.sum((row_grad + column_grad) * logits)
    text_grad = product((logit_multiplier * row_grad).astype(jnp.bfloat16), all_image) + product(
        (logit_multiplier * column_grad).astype(jnp.bfloat16), all_image
    )
    token_grad = embed_back(text_grad)[0]
    proj_bias_grad = jnp.sum(token_grad, axis=0)
    grad_rows = token_grad.astype(jnp.bfloat16)
    w_proj_grad = jnp.einsum("rf,rd->fd", hidden_act, grad_rows, preferred_element_type=jnp.float32)
    active_grad = jnp.einsum("rd,fd->rf", grad_rows, w_p, preferred_element_type=jnp.float32)
    hidden_grad = gelu_back(active_grad)[0].astype(jnp.bfloat16)
    w_hidden_grad = jnp.einsum(
        "rd,rf->df", normed_two, hidden_grad, preferred_element_type=jnp.float32
    )
    hidden_bias_grad = jnp.sum(hidden_grad.astype(jnp.float32), axis=0)
    normed_two_grad = jnp.einsum("rf,df->rd", hidden_grad, w_h, preferred_element_type=jnp.float32)
    norm_two_grads = norm_two_back(normed_two_grad)
    middle_grad = token_grad + norm_two_grads[0]
    attn_bias_grad = jnp.sum(middle_grad, axis=0)
    attn_grad_rows = middle_grad.astype(jnp.bfloat16)
    w_attn_out_grad = jnp.einsum(
        "rk,rd->kd", mixed_heads, attn_grad_rows, preferred_element_type=jnp.float32
    )
    mixed_grad = jnp.einsum("rd,kd->rk", attn_grad_rows, w_o, preferred_element_type=jnp.float32)
    mixed_grad = mixed_grad.astype(jnp.bfloat16).reshape(grid_shape)
    query_grad, key_grad, value_grad = attention_back(
        queries, key_rows, value_rows, log_totals, mixed_grad
    )
    query_grad = query_grad.reshape(all_rows, D).astype(jnp.bfloat16)
    key_grad = key_grad.reshape(all_rows, D).astype(jnp.bfloat16)
    value_grad = value_grad.reshape(all_rows, D).astype(jnp.bfloat16)
    back = partial(jnp.einsum, "rd,rk->dk", normed_one, preferred_element_type=jnp.float32)
    w_query_grad, w_key_grad, w_value_grad = (back(query_grad), back(key_grad), back(value_grad))
    query_bias_grad = jnp.sum(query_grad.astype(jnp.float32), axis=0)
    value_bias_grad = jnp.sum(value_grad.astype(jnp.float32), axis=0)
    down = partial(jnp.einsum, "rk,dk->rd", preferred_element_type=jnp.float32)
    normed_one_grad = down(query_grad, w_q) + down(key_grad, w_k) + down(value_grad, w_v)
    norm_one_grads = norm_one_back(normed_one_grad)
    text_in_grad = middle_grad + norm_one_grads[0]

    def share(grad, axis):
        part = lax.psum_scatter(
            grad.astype(jnp.bfloat16), "mp", scatter_dimension=axis, tiled=True
        )
        return lax.psum(part, "dp").astype(jnp.float32)

    shared = lax.psum(
        (
            total_part,
            temp_part,
            norm_one_grads[1],
            norm_one_grads[2],
            attn_bias_grad,
            norm_two_grads[1],
            norm_two_grads[2],
            proj_bias_grad,
            query_bias_grad,
            value_bias_grad,
            hidden_bias_grad,
        ),
        ("dp", "mp"),
    )
    loss = jnp.reshape((shared[0] + column_part) / pair_total, (1,))

    def own(vector):
        return lax.dynamic_slice_in_dim(
            vector, rank * (vector.shape[0] // mp_count), vector.shape[0] // mp_count, 0
        )

    return (
        loss,
        output.astype(jnp.bfloat16),
        text_in_grad,
        jnp.reshape(shared[1], (1,)),
        shared[2],
        shared[3],
        share(w_query_grad, 1),
        own(shared[8]),
        share(w_key_grad, 1),
        share(w_value_grad, 1),
        own(shared[9]),
        share(w_attn_out_grad, 0),
        shared[4],
        shared[5],
        shared[6],
        share(w_hidden_grad, 1),
        own(shared[10]),
        share(w_proj_grad, 0),
        shared[7],
    )


def solution(mesh):
    in_specs = (
        P(("dp", "mp"), None),
        P(("dp", "mp")),
        P(("dp", "mp")),
        P(),
        P(("dp", "mp"), None),
        P(),
        P(),
        P(),
        P(None, "mp"),
        P("mp"),
        P(None, "mp"),
        P(None, "mp"),
        P("mp"),
        P("mp", None),
        P(),
        P(),
        P(),
        P(None, "mp"),
        P("mp"),
        P("mp", None),
        P(),
        P(),
        P(),
        P(),
        P(),
        P(),
        P(),
    )
    out_specs = (
        P(),
        P(("dp", "mp"), None),
        P(("dp", "mp"), None),
        P(),
        P(),
        P(),
        P(None, "mp"),
        P("mp"),
        P(None, "mp"),
        P(None, "mp"),
        P("mp"),
        P("mp", None),
        P(),
        P(),
        P(),
        P(None, "mp"),
        P("mp"),
        P("mp", None),
        P(),
    )
    return jax.shard_map(body, mesh=mesh, in_specs=in_specs, out_specs=out_specs, check_vma=False)
```

```python
from functools import partial

import jax
import jax.numpy as jnp
from jax import lax
from jax.experimental import pallas as pl
from jax.experimental.pallas import tpu as pltpu
from jax.sharding import PartitionSpec as P

D = 768
HEADS = 12
HD = 64
LEN = 16
PATCHES = 50


def layer_norm(tensor, norm_gain, norm_shift):
    centred = tensor - jnp.mean(tensor, axis=-1, keepdims=True)
    variance = jnp.mean(centred * centred, axis=-1, keepdims=True)
    return centred * lax.rsqrt(variance + 1e-06) * norm_gain + norm_shift


def normalize(pooled):
    return pooled * lax.rsqrt(jnp.sum(pooled * pooled, axis=-1, keepdims=True) + 1e-06)


def product(left, right):
    return jnp.dot(left, right, preferred_element_type=jnp.float32)


def masked_scores(queries, key_rows, causal):
    scores = jnp.einsum(
        "gqhd,gkhd->ghqk", queries, key_rows, preferred_element_type=jnp.float32
    ) * HD ** (-0.5)
    if causal:
        places = jnp.arange(scores.shape[-1], dtype=jnp.int32)
        scores = jnp.where(places[None, :] <= places[:, None], scores, -1e30)
    return scores


def softmax_rows(scores):
    highest = jnp.max(scores, axis=-1, keepdims=True)
    weights = jnp.exp(scores - highest)
    totals = jnp.sum(weights, axis=-1, keepdims=True)
    return (weights / totals, highest + jnp.log(totals))


def attention_back(queries, key_rows, value_rows, log_totals, mixed_grad):
    scores = masked_scores(queries, key_rows, True)
    attn_probs = jnp.exp(scores - log_totals)
    probs_grad = jnp.einsum(
        "gqhd,gkhd->ghqk", mixed_grad, value_rows, preferred_element_type=jnp.float32
    )
    value_grad = jnp.einsum(
        "ghqk,gqhd->gkhd",
        attn_probs.astype(jnp.bfloat16),
        mixed_grad,
        preferred_element_type=jnp.float32,
    )
    inner_sum = jnp.sum(attn_probs * probs_grad, axis=-1, keepdims=True)
    score_grad = (attn_probs * (probs_grad - inner_sum)).astype(jnp.bfloat16)
    query_grad = jnp.einsum(
        "ghqk,gkhd->gqhd", score_grad, key_rows, preferred_element_type=jnp.float32
    ) * HD ** (-0.5)
    key_grad = jnp.einsum(
        "ghqk,gqhd->gkhd", score_grad, queries, preferred_element_type=jnp.float32
    ) * HD ** (-0.5)
    return (query_grad, key_grad, value_grad)


def image_embed(stored_picture_patches, frozen):
    (
        picture_lookup_coefficients,
        picture_address_coefficients,
        picture_content_coefficients,
        picture_mixer_exit,
        picture_perceptron_entry,
        picture_perceptron_exit,
    ) = frozen
    tokens = stored_picture_patches.astype(jnp.float32)
    examples = tokens.shape[0] // PATCHES
    normed = layer_norm(tokens, 1.0, 0.0).astype(jnp.bfloat16)
    grid_shape = (examples, PATCHES, HEADS, HD)
    queries = product(normed, picture_lookup_coefficients).astype(jnp.bfloat16).reshape(grid_shape)
    key_rows = (
        product(normed, picture_address_coefficients).astype(jnp.bfloat16).reshape(grid_shape)
    )
    value_rows = (
        product(normed, picture_content_coefficients).astype(jnp.bfloat16).reshape(grid_shape)
    )
    attn_probs, unused_totals = softmax_rows(masked_scores(queries, key_rows, False))
    mixed_heads = jnp.einsum(
        "ghqk,gkhd->gqhd",
        attn_probs.astype(jnp.bfloat16),
        value_rows,
        preferred_element_type=jnp.float32,
    )
    mixed_heads = mixed_heads.reshape(examples * PATCHES, D).astype(jnp.bfloat16)
    middle = tokens + product(mixed_heads, picture_mixer_exit)
    normed_two = layer_norm(middle, 1.0, 0.0).astype(jnp.bfloat16)
    hidden_act = jax.nn.gelu(
        product(normed_two, picture_perceptron_entry), approximate=True
    ).astype(jnp.bfloat16)
    output = middle + product(hidden_act, picture_perceptron_exit)
    return normalize(jnp.mean(output.reshape(examples, PATCHES, D), axis=1)).astype(jnp.bfloat16)


MESH = pl.DeviceIdType.MESH
ROWS = 128


def bit_of(value, bit):
    return lax.rem(lax.div(value, bit), 2)


def peer(axis, bit):
    dp, mp = lax.axis_index("dp"), lax.axis_index("mp")
    if axis == "dp":
        return (dp + bit - 2 * bit * bit_of(dp, bit), mp)
    return (dp, mp + bit - 2 * bit * bit_of(mp, bit))


def doubling_bits(dp_count):
    bits, bit = [], 1
    while bit < dp_count:
        bits.append(("dp", bit))
        bit *= 2
    return bits


def gradient_sum_kernel(dp_count, stack, small, out, small_out, keep, first, second, *rest):
    dp_bits = doubling_bits(dp_count)
    levels = len(dp_bits)
    parts, (whole, small_in, small_sum, send, receive, load, store, small_send, small_receive) = (
        rest[:levels],
        rest[levels:],
    )
    bits = [("mp", 1), ("mp", 2)] + dp_bits
    peers = [peer(*b) for b in bits]
    low, high = bit_of(lax.axis_index("mp"), 1), bit_of(lax.axis_index("mp"), 2)
    own = [bit_of(lax.axis_index("dp"), bit) for _, bit in dp_bits]
    chunks = stack.shape[2] // ROWS
    barrier = pltpu.get_barrier_semaphore()
    for p in peers:
        pl.semaphore_signal(barrier, inc=1, device_id=p, device_id_type=MESH)
    pl.semaphore_wait(barrier, len(peers))

    sizes = []
    size = ROWS
    for _ in dp_bits:
        halve = size >= 32
        size = size // 2 if halve else size
        sizes.append((size, halve))

    def add(target, other):
        target[...] = (target[...].astype(jnp.float32) + other[...].astype(jnp.float32)).astype(
            jnp.bfloat16
        )

    def rows(c):
        return pl.ds(pl.multiple_of(c * ROWS, ROWS), ROWS)

    def copy(stage, c):
        if stage == 0:
            source, target, who = stack.at[:, 1 - low, rows(c)], first.at[c], 0
        elif stage == 1:
            source, target, who = first.at[c, 1 - high], second.at[c], 1
        elif stage < 2 + levels:
            i = stage - 2
            n, halve = sizes[i]
            before = second if i == 0 else parts[i - 1]
            source = before.at[c, pl.ds((1 - own[i]) * n, n)] if halve else before.at[c]
            target, who = parts[i].at[c], stage
        else:
            i = gathers[stage - 2 - levels]
            n = sizes[i][0]
            where = sum(
                own[j] * sizes[j][0] for j in range(i + 1) if sizes[j][1]
            )
            source = target = whole.at[c, pl.ds(where, n)]
            who = 2 + i
        return pltpu.make_async_remote_copy(
            src_ref=source,
            dst_ref=target,
            send_sem=send.at[stage, c],
            recv_sem=receive.at[stage, c],
            device_id=peers[who],
            device_id_type=MESH,
        )

    gathers = [i for i in reversed(range(levels)) if sizes[i][1]]
    stages = 2 + levels + len(gathers)

    def load_copy(c):
        return pltpu.make_async_copy(stack.at[:, low, rows(c)], keep.at[c], load.at[c])

    def store_copy(c):
        return pltpu.make_async_copy(whole.at[c], out.at[rows(c)], store.at[c])

    def finish(stage, c):
        copy(stage, c).wait_recv()
        if stage == 0:
            load_copy(c).wait()
            add(first.at[c], keep.at[c])
        elif stage == 1:
            add(second.at[c], first.at[c, high])
        elif stage < 2 + levels:
            i = stage - 2
            n, halve = sizes[i]
            before = second if i == 0 else parts[i - 1]
            source = before.at[c, pl.ds(pl.multiple_of(own[i] * n, n), n)] if halve else before.at[c]
            if i < levels - 1:
                add(parts[i].at[c], source)
            else:
                where = sum(own[j] * sizes[j][0] for j in range(levels) if sizes[j][1])
                whole.at[c, pl.ds(pl.multiple_of(where, n), n)][...] = (
                    parts[i].at[c][...].astype(jnp.float32) + source[...].astype(jnp.float32)
                ).astype(jnp.bfloat16)

    def small_copy(i):
        return pltpu.make_async_remote_copy(
            src_ref=small if i == 0 else small_sum.at[i - 1],
            dst_ref=small_in.at[i],
            send_sem=small_send.at[i],
            recv_sem=small_receive.at[i],
            device_id=peers[i],
            device_id_type=MESH,
        )

    small_copy(0).start()

    @pl.loop(0, chunks + stages)
    def _(t):
        for slot in range(stages + 1):
            c = t - slot

            @pl.when((c >= 0) & (c < chunks))
            def _():
                if slot == 0:
                    load_copy(c).start()
                else:
                    finish(slot - 1, c)
                if slot < stages:
                    copy(slot, c).start()
                else:
                    store_copy(c).start()

        for i in range(len(bits)):

            @pl.when(t == 2 * i + 1)
            def _():
                small_copy(i).wait_recv()
                total = (small if i == 0 else small_sum.at[i - 1])[...] + small_in[i]
                if i < len(bits) - 1:
                    small_sum[i] = total
                    small_copy(i + 1).start()
                else:
                    small_out[...] = total

    for i in range(len(bits)):
        small_copy(i).wait_send()

    @pl.loop(0, chunks)
    def _(c):
        for stage in range(stages):
            copy(stage, c).wait_send()
        store_copy(c).wait()


def gradient_sum(dp_count, stack, small):
    levels = len(doubling_bits(dp_count))
    chunks = stack.shape[2] // ROWS
    sizes, size, halvings = [], ROWS, 0
    for _ in range(levels):
        halvings += size >= 32
        size = size // 2 if size >= 32 else size
        sizes.append(size)
    stages = 2 + levels + halvings
    half = jnp.bfloat16
    return pl.pallas_call(
        partial(gradient_sum_kernel, dp_count),
        out_shape=(
            jax.ShapeDtypeStruct(stack.shape[2:], half),
            jax.ShapeDtypeStruct(small.shape, jnp.float32),
        ),
        in_specs=[pl.BlockSpec(memory_space=pl.ANY), pl.BlockSpec(memory_space=pltpu.VMEM)],
        out_specs=(pl.BlockSpec(memory_space=pl.ANY), pl.BlockSpec(memory_space=pltpu.VMEM)),
        scratch_shapes=[
            pltpu.VMEM((chunks, 2, ROWS, D), half),
            pltpu.VMEM((chunks, 2, ROWS, D), half),
            pltpu.VMEM((chunks, ROWS, D), half),
        ]
        + [pltpu.VMEM((chunks, n, D), half) for n in sizes]
        + [
            pltpu.VMEM((chunks, ROWS, D), half),
            pltpu.VMEM((levels + 2,) + small.shape, jnp.float32),
            pltpu.VMEM((levels + 1,) + small.shape, jnp.float32),
            pltpu.SemaphoreType.DMA((stages, chunks)),
            pltpu.SemaphoreType.DMA((stages, chunks)),
            pltpu.SemaphoreType.DMA((chunks,)),
            pltpu.SemaphoreType.DMA((chunks,)),
            pltpu.SemaphoreType.DMA((levels + 2,)),
            pltpu.SemaphoreType.DMA((levels + 2,)),
        ],
        compiler_params=pltpu.CompilerParams(
            collective_id=1, has_side_effects=True, vmem_limit_bytes=56 * 2**20
        ),
        name="gradient_sum",
    )(stack, small)


def column_sum_kernel(value, out, near, far, send, receive):
    dp, mp = lax.axis_index("dp"), lax.axis_index("mp")
    dp_count, mp_count = far.shape[0], near.shape[0]
    barrier = pltpu.get_barrier_semaphore()
    for step in range(1, mp_count):
        pl.semaphore_signal(
            barrier, inc=1, device_id=(dp, lax.rem(mp + step, mp_count)), device_id_type=MESH
        )

    @pl.loop(1, dp_count)
    def _(step):
        pl.semaphore_signal(
            barrier, inc=1, device_id=(lax.rem(dp + step, dp_count), mp), device_id_type=MESH
        )

    pl.semaphore_wait(barrier, mp_count + dp_count - 2)

    def near_copy(step, sender):
        return pltpu.make_async_remote_copy(
            src_ref=value,
            dst_ref=near.at[sender],
            send_sem=send.at[step],
            recv_sem=receive.at[step],
            device_id=(dp, lax.rem(mp + step, mp_count)),
            device_id_type=MESH,
        )

    def far_copy(step, sender):
        return pltpu.make_async_remote_copy(
            src_ref=far.at[dp],
            dst_ref=far.at[sender],
            send_sem=send.at[mp_count + step],
            recv_sem=receive.at[mp_count + step],
            device_id=(lax.rem(dp + step, dp_count), mp),
            device_id_type=MESH,
        )

    for step in range(1, mp_count):
        near_copy(step, mp).start()
    near[mp] = value[...]
    for step in range(1, mp_count):
        near_copy(step, lax.rem(mp + mp_count - step, mp_count)).wait_recv()
    total = near[0]
    for i in range(1, mp_count):
        total = total + near[i]
    far[dp] = total

    @pl.loop(1, dp_count)
    def _(step):
        far_copy(step, dp).start()

    @pl.loop(1, dp_count)
    def _(step):
        far_copy(step, lax.rem(dp + dp_count - step, dp_count)).wait_recv()

    out[...] = far[0]

    @pl.loop(1, dp_count)
    def _(i):
        out[...] += far[i]

    for step in range(1, mp_count):
        near_copy(step, mp).wait_send()

    @pl.loop(1, dp_count)
    def _(step):
        far_copy(step, dp).wait_send()


def column_sum(dp_count, mp_count, value):
    return pl.pallas_call(
        column_sum_kernel,
        out_shape=jax.ShapeDtypeStruct(value.shape, jnp.float32),
        in_specs=[pl.BlockSpec(memory_space=pltpu.VMEM)],
        out_specs=pl.BlockSpec(memory_space=pltpu.VMEM),
        scratch_shapes=[
            pltpu.VMEM((mp_count,) + value.shape, jnp.float32),
            pltpu.VMEM((dp_count,) + value.shape, jnp.float32),
            pltpu.SemaphoreType.DMA((mp_count + dp_count,)),
            pltpu.SemaphoreType.DMA((mp_count + dp_count,)),
        ],
        compiler_params=pltpu.CompilerParams(collective_id=2, has_side_effects=True),
        name="column_sum",
    )(value)


def embed(block_out):
    return normalize(jnp.mean(block_out.reshape(-1, LEN, D), axis=1))


def body(
    sentence_entry_words,
    sentence_present_marks,
    picture_present_marks,
    matched_picture_positions,
    stored_picture_patches,
    log_logit_multiplier,
    leading_standardizer_stretch,
    leading_standardizer_shift,
    lookup_coefficients,
    lookup_offset,
    address_coefficients,
    content_coefficients,
    content_offset,
    mixer_exit_coefficients,
    mixer_exit_offset,
    trailing_standardizer_stretch,
    trailing_standardizer_shift,
    perceptron_entry_coefficients,
    perceptron_inner_offset,
    perceptron_exit_coefficients,
    perceptron_exit_offset,
    picture_lookup_coefficients,
    picture_address_coefficients,
    picture_content_coefficients,
    picture_mixer_exit,
    picture_perceptron_entry,
    picture_perceptron_exit,
):
    own_count = sentence_present_marks.shape[0]
    mp_count = lax.axis_size("mp")
    rank = lax.axis_index("mp")
    text_mask, image_mask = (
        lax.all_gather(sentence_present_marks.astype(jnp.float32), ("dp", "mp"), axis=0, tiled=True),
        lax.all_gather(picture_present_marks.astype(jnp.float32), ("dp", "mp"), axis=0, tiled=True),
    )
    wide = partial(lax.all_gather, axis_name="mp", axis=1, tiled=True)
    tall = partial(lax.all_gather, axis_name="mp", axis=0, tiled=True)
    w_q, w_k, w_v, w_o = (
        wide(lookup_coefficients),
        wide(address_coefficients),
        wide(content_coefficients),
        tall(mixer_exit_coefficients),
    )
    w_h, w_p = (wide(perceptron_entry_coefficients), tall(perceptron_exit_coefficients))
    b_q, b_v, b_h = (tall(lookup_offset), tall(content_offset), tall(perceptron_inner_offset))
    image_half = image_embed(
        stored_picture_patches,
        (
            picture_lookup_coefficients,
            picture_address_coefficients,
            picture_content_coefficients,
            picture_mixer_exit,
            picture_perceptron_entry,
            picture_perceptron_exit,
        ),
    )
    all_image = lax.all_gather(image_half, ("dp", "mp"), axis=0, tiled=True)
    tokens = sentence_entry_words.astype(jnp.float32)
    all_rows = tokens.shape[0]
    normed_one, norm_one_back = jax.vjp(
        layer_norm, tokens, leading_standardizer_stretch, leading_standardizer_shift
    )
    normed_one = normed_one.astype(jnp.bfloat16)
    grid_shape = (all_rows // LEN, LEN, HEADS, HD)
    queries = (product(normed_one, w_q) + b_q).astype(jnp.bfloat16).reshape(grid_shape)
    key_rows = product(normed_one, w_k).astype(jnp.bfloat16).reshape(grid_shape)
    value_rows = (product(normed_one, w_v) + b_v).astype(jnp.bfloat16).reshape(grid_shape)
    attn_probs, log_totals = softmax_rows(masked_scores(queries, key_rows, True))
    mixed_heads = jnp.einsum(
        "ghqk,gkhd->gqhd",
        attn_probs.astype(jnp.bfloat16),
        value_rows,
        preferred_element_type=jnp.float32,
    )
    mixed_heads = mixed_heads.reshape(all_rows, D).astype(jnp.bfloat16)
    middle = tokens + product(mixed_heads, w_o) + mixer_exit_offset
    normed_two, norm_two_back = jax.vjp(
        layer_norm, middle, trailing_standardizer_stretch, trailing_standardizer_shift
    )
    normed_two = normed_two.astype(jnp.bfloat16)
    hidden_pre = product(normed_two, w_h) + b_h
    hidden_act, gelu_back = jax.vjp(partial(jax.nn.gelu, approximate=True), hidden_pre)
    hidden_act = hidden_act.astype(jnp.bfloat16)
    output = middle + product(hidden_act, w_p) + perceptron_exit_offset
    text_emb, embed_back = jax.vjp(embed, output)
    text_half = text_emb.astype(jnp.bfloat16)

    everyone = text_mask.shape[0]
    order = jnp.arange(everyone, dtype=jnp.int32)
    offset = lax.axis_index(("dp", "mp")) * own_count
    own_pair = lax.dynamic_slice_in_dim(matched_picture_positions, offset, own_count, 0)
    own_text = sentence_present_marks.astype(jnp.float32)
    hits = (order[None, :] == own_pair[:, None]).astype(jnp.float32)
    text_weight = own_text * jnp.sum(hits * image_mask[None, :], axis=1)
    inverse = jnp.zeros((everyone,), jnp.int32).at[matched_picture_positions].set(order)
    image_weight = image_mask * text_mask[inverse]
    logit_multiplier = jnp.exp(log_logit_multiplier[0])
    logits = logit_multiplier * jnp.einsum(
        "id,jd->ij", text_half, all_image, preferred_element_type=jnp.float32
    )
    weights = jnp.exp(logits)
    row_weights = weights * image_mask[None, :]
    row_total = jnp.sum(row_weights, axis=1)
    column_weights = weights * own_text[:, None]
    column_total = column_sum(
        lax.axis_size("dp"), mp_count, jnp.sum(column_weights, axis=0).reshape(-1, 128)
    ).reshape(-1)
    pair_total = jnp.sum(image_weight)
    safe_row = jnp.where(row_total > 0, row_total, 1.0)
    safe_column = jnp.where(column_total > 0, column_total, 1.0)
    hit_logit = jnp.sum(hits * logits, axis=1)
    column_part = 0.5 * jnp.sum(image_weight * jnp.log(safe_column))
    total_part = 0.5 * jnp.sum(text_weight * jnp.log(safe_row)) - jnp.sum(text_weight * hit_logit)
    row_grad = 0.5 * text_weight[:, None] * (row_weights / safe_row[:, None] - hits)
    column_grad = 0.5 * image_weight[None, :] * (column_weights / safe_column[None, :] - hits)
    temp_part = jnp.sum((row_grad + column_grad) * logits)
    text_grad = product((logit_multiplier * row_grad).astype(jnp.bfloat16), all_image) + product(
        (logit_multiplier * column_grad).astype(jnp.bfloat16), all_image
    )
    token_grad = embed_back(text_grad)[0]
    proj_bias_grad = jnp.sum(token_grad, axis=0)
    grad_rows = token_grad.astype(jnp.bfloat16)
    w_proj_grad = jnp.einsum("rf,rd->fd", hidden_act, grad_rows, preferred_element_type=jnp.float32)
    active_grad = jnp.einsum("rd,fd->rf", grad_rows, w_p, preferred_element_type=jnp.float32)
    hidden_grad = gelu_back(active_grad)[0].astype(jnp.bfloat16)
    w_hidden_grad = jnp.einsum(
        "rd,rf->df", normed_two, hidden_grad, preferred_element_type=jnp.float32
    )
    hidden_bias_grad = jnp.sum(hidden_grad.astype(jnp.float32), axis=0)
    normed_two_grad = jnp.einsum("rf,df->rd", hidden_grad, w_h, preferred_element_type=jnp.float32)
    norm_two_grads = norm_two_back(normed_two_grad)
    middle_grad = token_grad + norm_two_grads[0]
    attn_bias_grad = jnp.sum(middle_grad, axis=0)
    attn_grad_rows = middle_grad.astype(jnp.bfloat16)
    w_attn_out_grad = jnp.einsum(
        "rk,rd->kd", mixed_heads, attn_grad_rows, preferred_element_type=jnp.float32
    )
    mixed_grad = jnp.einsum("rd,kd->rk", attn_grad_rows, w_o, preferred_element_type=jnp.float32)
    mixed_grad = mixed_grad.astype(jnp.bfloat16).reshape(grid_shape)
    query_grad, key_grad, value_grad = attention_back(
        queries, key_rows, value_rows, log_totals, mixed_grad
    )
    query_grad = query_grad.reshape(all_rows, D).astype(jnp.bfloat16)
    key_grad = key_grad.reshape(all_rows, D).astype(jnp.bfloat16)
    value_grad = value_grad.reshape(all_rows, D).astype(jnp.bfloat16)
    back = partial(jnp.einsum, "rd,rk->dk", normed_one, preferred_element_type=jnp.float32)
    w_query_grad, w_key_grad, w_value_grad = (back(query_grad), back(key_grad), back(value_grad))
    query_bias_grad = jnp.sum(query_grad.astype(jnp.float32), axis=0)
    value_bias_grad = jnp.sum(value_grad.astype(jnp.float32), axis=0)
    down = partial(jnp.einsum, "rk,dk->rd", preferred_element_type=jnp.float32)
    normed_one_grad = down(query_grad, w_q) + down(key_grad, w_k) + down(value_grad, w_v)
    norm_one_grads = norm_one_back(normed_one_grad)
    text_in_grad = middle_grad + norm_one_grads[0]

    def quarters(grad):
        return grad.astype(jnp.bfloat16).reshape(mp_count, -1, D)

    scalars = jnp.stack([total_part, temp_part])
    vectors = [
        norm_one_grads[1],
        norm_one_grads[2],
        attn_bias_grad,
        norm_two_grads[1],
        norm_two_grads[2],
        proj_bias_grad,
        query_bias_grad,
        value_bias_grad,
        hidden_bias_grad,
    ]
    small = jnp.concatenate(vectors + [scalars])
    filled = small.shape[0]
    small = jnp.pad(small, (0, -filled % 1024)).reshape(-1, 128)
    stack = jnp.concatenate(
        [
            quarters(w_proj_grad),
            jnp.stack(jnp.split(w_hidden_grad.astype(jnp.bfloat16), mp_count, axis=1)),
            quarters(w_query_grad.T),
            quarters(w_key_grad.T),
            quarters(w_value_grad.T),
            quarters(w_attn_out_grad),
        ],
        axis=1,
    )
    own_grads, small = gradient_sum(
        lax.axis_size("dp"), stack.reshape((2, 2) + stack.shape[1:]), small
    )
    small = small.reshape(-1)
    shared, start = [], 0
    for vector in vectors:
        shared.append(small[start : start + vector.shape[0]])
        start += vector.shape[0]
    shared = [small[start], small[start + 1]] + shared
    loss = jnp.reshape((shared[0] + column_part) / pair_total, (1,))
    quarter = D // mp_count

    def rows_of(start, count):
        return own_grads[start : start + count].astype(jnp.float32)

    def own(vector):
        return lax.dynamic_slice_in_dim(
            vector, rank * (vector.shape[0] // mp_count), vector.shape[0] // mp_count, 0
        )

    return (
        loss,
        output.astype(jnp.bfloat16),
        text_in_grad,
        jnp.reshape(shared[1], (1,)),
        shared[2],
        shared[3],
        rows_of(2 * D, quarter).T,
        own(shared[8]),
        rows_of(2 * D + 1 * quarter, quarter).T,
        rows_of(2 * D + 2 * quarter, quarter).T,
        own(shared[9]),
        rows_of(2 * D + 3 * quarter, quarter),
        shared[4],
        shared[5],
        shared[6],
        rows_of(D, D),
        own(shared[10]),
        rows_of(0, D),
        shared[7],
    )


def solution(mesh):
    in_specs = (
        P(("dp", "mp"), None),
        P(("dp", "mp")),
        P(("dp", "mp")),
        P(),
        P(("dp", "mp"), None),
        P(),
        P(),
        P(),
        P(None, "mp"),
        P("mp"),
        P(None, "mp"),
        P(None, "mp"),
        P("mp"),
        P("mp", None),
        P(),
        P(),
        P(),
        P(None, "mp"),
        P("mp"),
        P("mp", None),
        P(),
        P(),
        P(),
        P(),
        P(),
        P(),
        P(),
    )
    out_specs = (
        P(),
        P(("dp", "mp"), None),
        P(("dp", "mp"), None),
        P(),
        P(),
        P(),
        P(None, "mp"),
        P("mp"),
        P(None, "mp"),
        P(None, "mp"),
        P("mp"),
        P("mp", None),
        P(),
        P(),
        P(),
        P(None, "mp"),
        P("mp"),
        P("mp", None),
        P(),
    )
    return jax.shard_map(body, mesh=mesh, in_specs=in_specs, out_specs=out_specs, check_vma=False)
```

```python
from functools import partial

import jax
import jax.numpy as jnp
from jax import lax
from jax.experimental import pallas as pl
from jax.experimental.pallas import tpu as pltpu
from jax.sharding import PartitionSpec as P

D = 768
HEADS = 12
HD = 64
LEN = 16
PATCHES = 50
SCALE = HD ** (-0.5)
BLOCK = 8 * PATCHES
WINDOW = 112
STEP = 96
QUARTERS = 4
TEXT_WINDOW = 128
LOSS_WIDTH = 1024


def normalize(pooled):
    return pooled * lax.rsqrt(jnp.sum(pooled * pooled, axis=-1, keepdims=True) + 1e-06)


def dot(left, right):
    return lax.dot_general(
        left, right, (((1,), (0,)), ((), ())), preferred_element_type=jnp.float32
    )


def dot_nt(left, right):
    return lax.dot_general(
        left, right, (((1,), (1,)), ((), ())), preferred_element_type=jnp.float32
    )


def dot_tn(left, right):
    return lax.dot_general(
        left, right, (((0,), (0,)), ((), ())), preferred_element_type=jnp.float32
    )


def centre(tensor):
    centred = tensor - jnp.mean(tensor, axis=-1, keepdims=True)
    return centred * lax.rsqrt(jnp.mean(centred * centred, axis=-1, keepdims=True) + 1e-06)


def gelu(v):
    return 0.5 * v * (1.0 + jnp.tanh(0.7978845608028654 * (v + 0.044715 * v * v * v)))


MESH = pl.DeviceIdType.MESH
ROWS = 128


def bit_of(value, bit):
    return lax.rem(lax.div(value, bit), 2)


def peer(axis, bit):
    dp, mp = lax.axis_index("dp"), lax.axis_index("mp")
    if axis == "dp":
        return (dp + bit - 2 * bit * bit_of(dp, bit), mp)
    return (dp, mp + bit - 2 * bit * bit_of(mp, bit))


def doubling_bits(dp_count):
    bits, bit = [], 1
    while bit < dp_count:
        bits.append(("dp", bit))
        bit *= 2
    return bits


def gradient_sum_kernel(dp_count, stack, small, out, small_out, keep, first, second, *rest):
    dp_bits = doubling_bits(dp_count)
    levels = len(dp_bits)
    parts, (whole, small_in, small_sum, send, receive, load, store, small_send, small_receive) = (
        rest[:levels],
        rest[levels:],
    )
    bits = [("mp", 1), ("mp", 2)] + dp_bits
    peers = [peer(*b) for b in bits]
    low, high = bit_of(lax.axis_index("mp"), 1), bit_of(lax.axis_index("mp"), 2)
    own = [bit_of(lax.axis_index("dp"), bit) for _, bit in dp_bits]
    chunks = stack.shape[2] // ROWS
    barrier = pltpu.get_barrier_semaphore()
    for p in peers:
        pl.semaphore_signal(barrier, inc=1, device_id=p, device_id_type=MESH)
    pl.semaphore_wait(barrier, len(peers))

    sizes = []
    size = ROWS
    for _ in dp_bits:
        halve = size >= 32
        size = size // 2 if halve else size
        sizes.append((size, halve))

    def add(target, other):
        target[...] = (target[...].astype(jnp.float32) + other[...].astype(jnp.float32)).astype(
            jnp.bfloat16
        )

    def rows(c):
        return pl.ds(pl.multiple_of(c * ROWS, ROWS), ROWS)

    def copy(stage, c):
        if stage == 0:
            source, target, who = stack.at[:, 1 - low, rows(c)], first.at[c], 0
        elif stage == 1:
            source, target, who = first.at[c, 1 - high], second.at[c], 1
        elif stage < 2 + levels:
            i = stage - 2
            n, halve = sizes[i]
            before = second if i == 0 else parts[i - 1]
            source = before.at[c, pl.ds((1 - own[i]) * n, n)] if halve else before.at[c]
            target, who = parts[i].at[c], stage
        else:
            i = gathers[stage - 2 - levels]
            n = sizes[i][0]
            where = sum(
                own[j] * sizes[j][0] for j in range(i + 1) if sizes[j][1]
            )
            source = target = whole.at[c, pl.ds(where, n)]
            who = 2 + i
        return pltpu.make_async_remote_copy(
            src_ref=source,
            dst_ref=target,
            send_sem=send.at[stage, c],
            recv_sem=receive.at[stage, c],
            device_id=peers[who],
            device_id_type=MESH,
        )

    gathers = [i for i in reversed(range(levels)) if sizes[i][1]]
    stages = 2 + levels + len(gathers)

    def load_copy(c):
        return pltpu.make_async_copy(stack.at[:, low, rows(c)], keep.at[c], load.at[c])

    def store_copy(c):
        return pltpu.make_async_copy(whole.at[c], out.at[rows(c)], store.at[c])

    def finish(stage, c):
        copy(stage, c).wait_recv()
        if stage == 0:
            load_copy(c).wait()
            add(first.at[c], keep.at[c])
        elif stage == 1:
            add(second.at[c], first.at[c, high])
        elif stage < 2 + levels:
            i = stage - 2
            n, halve = sizes[i]
            before = second if i == 0 else parts[i - 1]
            source = before.at[c, pl.ds(pl.multiple_of(own[i] * n, n), n)] if halve else before.at[c]
            if i < levels - 1:
                add(parts[i].at[c], source)
            else:
                where = sum(own[j] * sizes[j][0] for j in range(levels) if sizes[j][1])
                whole.at[c, pl.ds(pl.multiple_of(where, n), n)][...] = (
                    parts[i].at[c][...].astype(jnp.float32) + source[...].astype(jnp.float32)
                ).astype(jnp.bfloat16)

    def small_copy(i):
        return pltpu.make_async_remote_copy(
            src_ref=small if i == 0 else small_sum.at[i - 1],
            dst_ref=small_in.at[i],
            send_sem=small_send.at[i],
            recv_sem=small_receive.at[i],
            device_id=peers[i],
            device_id_type=MESH,
        )

    small_copy(0).start()

    @pl.loop(0, chunks + stages)
    def _(t):
        for slot in range(stages + 1):
            c = t - slot

            @pl.when((c >= 0) & (c < chunks))
            def _():
                if slot == 0:
                    load_copy(c).start()
                else:
                    finish(slot - 1, c)
                if slot < stages:
                    copy(slot, c).start()
                else:
                    store_copy(c).start()

        for i in range(len(bits)):

            @pl.when(t == 2 * i + 1)
            def _():
                small_copy(i).wait_recv()
                total = (small if i == 0 else small_sum.at[i - 1])[...] + small_in[i]
                if i < len(bits) - 1:
                    small_sum[i] = total
                    small_copy(i + 1).start()
                else:
                    small_out[...] = total

    for i in range(len(bits)):
        small_copy(i).wait_send()

    @pl.loop(0, chunks)
    def _(c):
        for stage in range(stages):
            copy(stage, c).wait_send()
        store_copy(c).wait()


def gradient_sum(dp_count, stack, small):
    levels = len(doubling_bits(dp_count))
    chunks = stack.shape[2] // ROWS
    sizes, size, halvings = [], ROWS, 0
    for _ in range(levels):
        halvings += size >= 32
        size = size // 2 if size >= 32 else size
        sizes.append(size)
    stages = 2 + levels + halvings
    half = jnp.bfloat16
    return pl.pallas_call(
        partial(gradient_sum_kernel, dp_count),
        out_shape=(
            jax.ShapeDtypeStruct(stack.shape[2:], half),
            jax.ShapeDtypeStruct(small.shape, jnp.float32),
        ),
        in_specs=[pl.BlockSpec(memory_space=pl.ANY), pl.BlockSpec(memory_space=pltpu.VMEM)],
        out_specs=(pl.BlockSpec(memory_space=pl.ANY), pl.BlockSpec(memory_space=pltpu.VMEM)),
        scratch_shapes=[
            pltpu.VMEM((chunks, 2, ROWS, D), half),
            pltpu.VMEM((chunks, 2, ROWS, D), half),
            pltpu.VMEM((chunks, ROWS, D), half),
        ]
        + [pltpu.VMEM((chunks, n, D), half) for n in sizes]
        + [
            pltpu.VMEM((chunks, ROWS, D), half),
            pltpu.VMEM((levels + 2,) + small.shape, jnp.float32),
            pltpu.VMEM((levels + 1,) + small.shape, jnp.float32),
            pltpu.SemaphoreType.DMA((stages, chunks)),
            pltpu.SemaphoreType.DMA((stages, chunks)),
            pltpu.SemaphoreType.DMA((chunks,)),
            pltpu.SemaphoreType.DMA((chunks,)),
            pltpu.SemaphoreType.DMA((levels + 2,)),
            pltpu.SemaphoreType.DMA((levels + 2,)),
        ],
        compiler_params=pltpu.CompilerParams(
            collective_id=1, has_side_effects=True, vmem_limit_bytes=56 * 2**20
        ),
        name="gradient_sum",
    )(stack, small)


def other(mp, bit):
    return mp + bit - 2 * bit * bit_of(mp, bit)


def greet(dp, mp, dp_count, mp_count):
    barrier = pltpu.get_barrier_semaphore()
    for step in range(1, mp_count):
        pl.semaphore_signal(
            barrier, inc=1, device_id=(dp, lax.rem(mp + step, mp_count)), device_id_type=MESH
        )

    @pl.loop(1, dp_count)
    def _(step):
        pl.semaphore_signal(
            barrier, inc=1, device_id=(lax.rem(dp + step, dp_count), mp), device_id_type=MESH
        )

    pl.semaphore_wait(barrier, mp_count + dp_count - 2)


class Spread:
    def __init__(self, value, near, far, send, receive):
        self.dp, self.mp = lax.axis_index("dp"), lax.axis_index("mp")
        self.dp_count, self.mp_count = far.shape[0], near.shape[0]
        self.value, self.near, self.far = value, near, far
        self.send, self.receive = send, receive

    def near_copy(self, step, sender):
        return pltpu.make_async_remote_copy(
            src_ref=self.value,
            dst_ref=self.near.at[sender],
            send_sem=self.send.at[step],
            recv_sem=self.receive.at[step],
            device_id=(self.dp, lax.rem(self.mp + step, self.mp_count)),
            device_id_type=MESH,
        )

    def far_copy(self, step, sender):
        return pltpu.make_async_remote_copy(
            src_ref=self.far.at[self.dp],
            dst_ref=self.far.at[sender],
            send_sem=self.send.at[self.mp_count + step],
            recv_sem=self.receive.at[self.mp_count + step],
            device_id=(lax.rem(self.dp + step, self.dp_count), self.mp),
            device_id_type=MESH,
        )

    def start_near(self):
        for step in range(1, self.mp_count):
            self.near_copy(step, self.mp).start()
        self.near[self.mp] = self.value[...]

    def wait_near(self):
        for step in range(1, self.mp_count):
            self.near_copy(step, lax.rem(self.mp + self.mp_count - step, self.mp_count)).wait_recv()

    def start_far(self):
        @pl.loop(1, self.dp_count)
        def _(step):
            self.far_copy(step, self.dp).start()

    def wait_far(self):
        @pl.loop(1, self.dp_count)
        def _(step):
            self.far_copy(
                step, lax.rem(self.dp + self.dp_count - step, self.dp_count)
            ).wait_recv()

    def wait_near_sends(self):
        for step in range(1, self.mp_count):
            self.near_copy(step, self.mp).wait_send()

    def wait_far_sends(self):
        @pl.loop(1, self.dp_count)
        def _(step):
            self.far_copy(step, self.dp).wait_send()


PIECE = 96
PIECES = 12


def image_kernel(
    x, wq, wk, wv, wo, we, wx, squares, entry, leave, small,
    out, gathered, small_all,
    bq, bk, bv, bo, be, bx, load, normed, q, k, v, mixed, middle, bias,
    own, own_load, own_store, send, receive, near, far, small_send, small_receive,
):
    step = pl.program_id(0)
    last = pl.num_programs(0) - 1
    dp, mp = lax.axis_index("dp"), lax.axis_index("mp")
    y = bit_of(dp, 1)
    across, beside, along = (dp, other(mp, 2)), (dp, other(mp, 1)), (other(dp, 1), mp)
    pairs = [(wq, bq), (wk, bk), (wv, bv), (wo, bo), (we, be), (wx, bx)]
    spread = Spread(small, near, far, small_send, small_receive)

    def load_copy(i):
        return pltpu.make_async_copy(pairs[i][0], pairs[i][1], load.at[i])

    def own_copy(i):
        return pltpu.make_async_copy((leave, entry, squares)[i], own.at[i], own_load.at[i])

    def keep_copy():
        return pltpu.make_async_copy(own, gathered.at[mp], own_store)

    def travel(kind, c):
        matrix = lax.div(c, PIECES // 3)
        start = lax.rem(c, PIECES // 3) * PIECE
        mine = pl.ds(pl.multiple_of(start + y * (D // 2), PIECE), PIECE)
        theirs = pl.ds(pl.multiple_of(start + (1 - y) * (D // 2), PIECE), PIECE)
        source_mp = other(mp, 2)
        if kind == 0:
            source, target, who = own.at[matrix, mine], gathered.at[mp, matrix, mine], across
        elif kind == 4:
            source, target, who = own.at[c], gathered.at[mp, c], beside
        else:
            rows = theirs if kind == 3 else mine
            source = target = gathered.at[source_mp, matrix, rows]
            who = along if kind == 1 else beside
        return pltpu.make_async_remote_copy(
            src_ref=source,
            dst_ref=target,
            send_sem=send.at[kind, c],
            recv_sem=receive.at[kind, c],
            device_id=who,
            device_id_type=MESH,
        )

    def forward_across(c):
        travel(0, c).wait_recv()
        travel(1, c).start()
        travel(2, c).start()

    def forward_along(c):
        travel(1, c).wait_recv()
        travel(3, c).start()

    def pump(j):
        n = step * 4 + j

        @pl.when((n >= 2) & (n < 2 + PIECES))
        def _():
            forward_across(n - 2)

        @pl.when((n >= 4) & (n < 4 + PIECES))
        def _():
            forward_along(n - 4)

    @pl.when(step == 0)
    def _():
        for i in range(3):
            own_copy(i).start()
        for i in range(6):
            load_copy(i).start()
        greet(dp, mp, far.shape[0], near.shape[0])
        spread.start_near()
        for i in range(3):
            own_copy(i).wait()

        @pl.loop(0, PIECES)
        def _(c):
            travel(0, c).start()

        for i in range(3):
            travel(4, i).start()
        keep_copy().start()
        for p in range(4):
            row = lax.broadcasted_iota(jnp.int32, (WINDOW, WINDOW), 0) + STEP * p
            column = lax.broadcasted_iota(jnp.int32, (WINDOW, WINDOW), 1) + STEP * p
            bias[p] = jnp.where(row // PATCHES == column // PATCHES, 0.0, -1e30)

    def ready(i):
        @pl.when(step == 0)
        def _():
            load_copy(i).wait()

    z = x[...].astype(jnp.float32)
    normed[...] = centre(z).astype(jnp.bfloat16)
    ready(0)
    q[...] = (dot(normed[...], bq[...]) * SCALE).astype(jnp.bfloat16)
    ready(1)
    k[...] = dot(normed[...], bk[...]).astype(jnp.bfloat16)
    ready(2)
    v[...] = dot(normed[...], bv[...]).astype(jnp.bfloat16)
    pump(0)

    @pl.when(step == 0)
    def _():
        spread.wait_near()
        far[dp] = near[...]
        spread.start_far()

    first = lax.broadcasted_iota(jnp.int32, (WINDOW, 128), 1) < HD
    for p in range(4):
        if p == 2:
            pump(1)
        rows = pl.ds(STEP * p, WINDOW)
        for h in range(HEADS // 2):
            lanes = pl.ds(128 * h, 128)
            part = q[rows, lanes]
            none = jnp.zeros_like(part)
            both = jnp.concatenate([jnp.where(first, part, none), jnp.where(first, none, part)])
            scores = dot_nt(both, k[rows, lanes])
            mask = bias[p]
            scores = scores + jnp.concatenate([mask, mask])
            weights = jnp.exp(scores - jnp.max(scores, axis=-1, keepdims=True))
            probs = (weights * (1.0 / jnp.sum(weights, axis=-1, keepdims=True))).astype(jnp.bfloat16)
            heads = dot(probs, v[rows, lanes])
            merged = jnp.where(first, heads[:WINDOW], heads[WINDOW:]).astype(jnp.bfloat16)
            if p:
                edge = pl.ds(STEP * p, 16)
                late = lax.broadcasted_iota(jnp.int32, (16, 128), 0) >= 2 * PATCHES * p - STEP * p
                mixed[edge, lanes] = jnp.where(late, merged[:16], mixed[edge, lanes])
                mixed[pl.ds(STEP * p + 16, WINDOW - 16), lanes] = merged[16:]
            else:
                mixed[rows, lanes] = merged
    pump(2)
    ready(3)
    middle[...] = x[...].astype(jnp.float32) + dot(mixed[...], bo[...])
    normed[...] = centre(middle[...]).astype(jnp.bfloat16)
    ready(4)
    ready(5)
    for c in range(4):
        if c == 2:
            pump(3)
        part = pl.ds(c * D, D)
        active = gelu(dot(normed[...], be[:, part])).astype(jnp.bfloat16)
        middle[...] += dot(active, bx[part, :])
    total = middle[...]
    high = total.astype(jnp.bfloat16)
    low = (total - high.astype(jnp.float32)).astype(jnp.bfloat16)
    owner = lax.broadcasted_iota(jnp.int32, (8, BLOCK), 1) // PATCHES
    pool = jnp.where(owner == lax.broadcasted_iota(jnp.int32, (8, BLOCK), 0), 1.0, 0.0)
    pool = pool.astype(jnp.bfloat16)
    pooled = (dot(pool, high) + dot(pool, low)) * (1.0 / PATCHES)
    out[...] = normalize(pooled)

    @pl.when(step == last)
    def _():
        spread.wait_far()
        small_all[...] = far[...]
        spread.wait_near_sends()
        spread.wait_far_sends()
        keep_copy().wait()
        for i in range(3):
            travel(4, i).wait()

        @pl.loop(0, PIECES)
        def _(c):
            travel(2, c).wait_recv()
            travel(3, c).wait_recv()
            for kind in range(4):
                travel(kind, c).wait_send()


def image_layer(dp_count, mp_count, tokens, frozen, squares, entry, leave, small):
    half = jnp.bfloat16
    any_space = pl.BlockSpec(memory_space=pl.ANY)
    blocks = tokens.shape[0] // BLOCK
    square = pltpu.VMEM((D, D), half)
    rows = pltpu.VMEM((BLOCK, D), half)
    kinds = pltpu.SemaphoreType.DMA((5, PIECES))
    return pl.pallas_call(
        image_kernel,
        grid=(blocks,),
        out_shape=(
            jax.ShapeDtypeStruct((blocks * 8, D), jnp.float32),
            jax.ShapeDtypeStruct((mp_count, 3, D, D), half),
            jax.ShapeDtypeStruct((dp_count, mp_count) + small.shape, jnp.float32),
        ),
        in_specs=[pl.BlockSpec((BLOCK, D), lambda i: (i, 0))]
        + [any_space] * 9
        + [pl.BlockSpec(memory_space=pltpu.VMEM)],
        out_specs=(
            pl.BlockSpec((8, D), lambda i: (i, 0)),
            any_space,
            pl.BlockSpec(memory_space=pltpu.VMEM),
        ),
        scratch_shapes=[square] * 4
        + [
            pltpu.VMEM((D, 4 * D), half),
            pltpu.VMEM((4 * D, D), half),
            pltpu.SemaphoreType.DMA((6,)),
        ]
        + [rows] * 5
        + [
            pltpu.VMEM((BLOCK, D), jnp.float32),
            pltpu.VMEM((4, WINDOW, WINDOW), jnp.float32),
            pltpu.VMEM((3, D, D), half),
            pltpu.SemaphoreType.DMA((3,)),
            pltpu.SemaphoreType.DMA,
            kinds,
            kinds,
            pltpu.VMEM((mp_count,) + small.shape, jnp.float32),
            pltpu.VMEM((dp_count, mp_count) + small.shape, jnp.float32),
            pltpu.SemaphoreType.DMA((mp_count + dp_count,)),
            pltpu.SemaphoreType.DMA((mp_count + dp_count,)),
        ],
        compiler_params=pltpu.CompilerParams(
            collective_id=3, has_side_effects=True, vmem_limit_bytes=56 * 2**20
        ),
        name="image_layer",
    )(tokens, *frozen, squares, entry, leave, small)


def gelu_slope(v):
    bend = jnp.tanh(0.7978845608028654 * (v + 0.044715 * v * v * v))
    inner = 0.7978845608028654 * (1.0 + 0.134145 * v * v)
    return 0.5 * (1.0 + bend) + 0.5 * v * (1.0 - bend * bend) * inner


def hat(tensor):
    centred = tensor - jnp.mean(tensor, axis=-1, keepdims=True)
    inverse = lax.rsqrt(jnp.mean(centred * centred, axis=-1, keepdims=True) + 1e-06)
    return centred * inverse, inverse


def hat_back(unit, inverse, grad):
    mean = jnp.mean(grad, axis=-1, keepdims=True)
    return inverse * (grad - mean - unit * jnp.mean(grad * unit, axis=-1, keepdims=True))


def split(v):
    high = v.astype(jnp.bfloat16)
    return jnp.concatenate([high, (v - high.astype(jnp.float32)).astype(jnp.bfloat16)])


def total_of(v):
    return jnp.sum(jnp.sum(v, axis=1, keepdims=True), axis=0, keepdims=True)


def text_kernel(
    x, image, own_text, own_pair, image_mask, scale,
    g1, s1, b_q, b_v, b_o, g2, s2, b_h, b_p, gathered,
    text_out, in_grad, stack, vectors, plain,
    squares, entry, leave, load, images, far_send, far_receive, x_send, x_receive, core_send,
    core_receive, normed, q, k, v, mixed, middle, normed_two, pre, sums, bias, stage, stage_sem,
    logits, value, near, far, column_send, column_receive,
):
    work, mixed_grad = in_grad, normed_two
    dp, mp = lax.axis_index("dp"), lax.axis_index("mp")
    dp_count, mp_count = far.shape[0], near.shape[0]
    rows_count, own_count = x.shape[0], own_text.shape[0]
    part_rows = D // QUARTERS
    half = jnp.bfloat16

    def square_copy(i, m):
        return pltpu.make_async_copy(
            gathered.at[m, 2, pl.ds(i * part_rows, part_rows)],
            squares.at[i, pl.ds(m * part_rows, part_rows)],
            load.at[i, m],
        )

    def entry_copy(m):
        return pltpu.make_async_copy(gathered.at[m, 1], entry.at[m], load.at[4, m])

    def leave_copy(m):
        return pltpu.make_async_copy(gathered.at[m, 0], leave.at[m], load.at[5, m])

    for i in range(4):
        for m in range(QUARTERS):
            square_copy(i, m).start()
    for m in range(QUARTERS):
        entry_copy(m).start()
        leave_copy(m).start()
    images[dp, mp] = image[...].astype(half)
    greet(dp, mp, dp_count, mp_count)

    def sender(step):
        return lax.rem(dp + dp_count - step, dp_count)

    def far_image(step):
        return pltpu.make_async_remote_copy(
            src_ref=images.at[dp, mp],
            dst_ref=images.at[dp, mp],
            send_sem=far_send.at[step],
            recv_sem=far_receive.at[step],
            device_id=(lax.rem(dp + step, dp_count), mp),
            device_id_type=MESH,
        )

    def x_image(step):
        return pltpu.make_async_remote_copy(
            src_ref=images.at[sender(step), mp],
            dst_ref=images.at[sender(step), mp],
            send_sem=x_send.at[step],
            recv_sem=x_receive.at[step],
            device_id=(dp, other(mp, 2)),
            device_id_type=MESH,
        )

    def core_image(kind, step):
        source = other(mp, 2) if kind else mp
        return pltpu.make_async_remote_copy(
            src_ref=images.at[sender(step), source],
            dst_ref=images.at[sender(step), source],
            send_sem=core_send.at[kind, step],
            recv_sem=core_receive.at[kind, step],
            device_id=(dp, other(mp, 1)),
            device_id_type=MESH,
        )

    @pl.loop(1, dp_count)
    def _(step):
        far_image(step).start()

    x_image(0).start()
    core_image(0, 0).start()

    row = lax.broadcasted_iota(jnp.int32, (TEXT_WINDOW, TEXT_WINDOW), 0)
    column = lax.broadcasted_iota(jnp.int32, (TEXT_WINDOW, TEXT_WINDOW), 1)
    bias[...] = jnp.where((row // LEN == column // LEN) & (column <= row), 0.0, -1e30)
    first = lax.broadcasted_iota(jnp.int32, (TEXT_WINDOW, 128), 1) < HD

    unit, unused = hat(x[...].astype(jnp.float32))
    normed[...] = (unit * g1[...] + s1[...]).astype(half)
    for m in range(QUARTERS):
        square_copy(0, m).wait()
    q[...] = ((dot_nt(normed[...], squares[0]) + b_q[...]) * SCALE).astype(half)
    for m in range(QUARTERS):
        square_copy(1, m).wait()
    k[...] = dot_nt(normed[...], squares[1]).astype(half)
    for m in range(QUARTERS):
        square_copy(2, m).wait()
    v[...] = (dot_nt(normed[...], squares[2]) + b_v[...]).astype(half)

    def doubled(part):
        none = jnp.zeros_like(part)
        return jnp.concatenate([jnp.where(first, part, none), jnp.where(first, none, part)])

    def probabilities(both, keys):
        scores = dot_nt(both, keys) + jnp.concatenate([bias[...], bias[...]])
        weights = jnp.exp(scores - jnp.max(scores, axis=-1, keepdims=True))
        return weights * (1.0 / jnp.sum(weights, axis=-1, keepdims=True))

    def merge(heads):
        return jnp.where(first, heads[:TEXT_WINDOW], heads[TEXT_WINDOW:])

    @pl.loop(0, rows_count // TEXT_WINDOW)
    def _(w):
        rows = pl.ds(pl.multiple_of(w * TEXT_WINDOW, TEXT_WINDOW), TEXT_WINDOW)
        for h in range(HEADS // 2):
            lanes = pl.ds(128 * h, 128)
            probs = probabilities(doubled(q[rows, lanes]), k[rows, lanes]).astype(half)
            mixed[rows, lanes] = merge(dot(probs, v[rows, lanes])).astype(half)

    @pl.loop(1, dp_count)
    def _(step):
        far_image(step).wait_recv()
        x_image(step).start()
        core_image(0, step).start()

    for m in range(QUARTERS):
        square_copy(3, m).wait()
    middle[...] = x[...].astype(jnp.float32) + dot(mixed[...], squares[3]) + b_o[...]
    unit, unused = hat(middle[...])
    normed_two[...] = (unit * g2[...] + s2[...]).astype(half)
    owner = lax.broadcasted_iota(jnp.int32, (own_count, rows_count), 1) // LEN
    pool = jnp.where(owner == lax.broadcasted_iota(jnp.int32, (own_count, rows_count), 0), 1.0, 0.0)
    pool = pool.astype(half)
    work[...] = middle[...] + b_p[...]
    for m in range(QUARTERS):
        if m == 2:

            @pl.loop(0, dp_count)
            def _(step):
                x_image(step).wait_recv()
                core_image(1, step).start()

        entry_copy(m).wait()
        leave_copy(m).wait()
        hidden = dot(normed_two[...], entry[m]) + b_h[pl.ds(m, 1), :]
        pre[m] = hidden
        active = gelu(hidden).astype(half)
        sums[m] = split(dot(pool, active))
        work[...] += dot(active, leave[m])
    text_out[...] = work[...].astype(half)
    output = split(work[...])
    pooled = (dot(pool, output[:rows_count]) + dot(pool, output[rows_count:])) * (1.0 / LEN)

    @pl.loop(0, dp_count)
    def _(step):
        core_image(0, step).wait_recv()
        core_image(1, step).wait_recv()

    text_unit = normalize(pooled)
    everyone = image_mask.shape[1]
    width = LOSS_WIDTH
    multiplier = scale[...]
    text_half = text_unit.astype(half)
    tiles = everyone // 128
    group_count = width // (mp_count * own_count)
    sections = [pl.ds(c * width, width) for c in range(everyone // width)]

    def images_of(c):
        return images[pl.ds(c * group_count, group_count)].reshape(width, D)

    def hits_of(c):
        place = lax.broadcasted_iota(jnp.int32, (own_count, width), 1) + c * width
        return jnp.where(place == own_pair[...], 1.0, 0.0)

    row_total = text_hits = hit_logit = jnp.zeros((own_count, 1), jnp.float32)
    for c, lanes in enumerate(sections):
        logits[:, lanes] = dot_nt(text_half, images_of(c)) * multiplier
        hits = hits_of(c)
        weights = jnp.exp(logits[:, lanes])
        row_total += jnp.sum(weights * image_mask[:, lanes], axis=1, keepdims=True)
        text_hits += jnp.sum(hits * image_mask[:, lanes], axis=1, keepdims=True)
        hit_logit += jnp.sum(hits * logits[:, lanes], axis=1, keepdims=True)
        column_part = jnp.sum(weights * own_text[...], axis=0, keepdims=True)
        owner_part = jnp.sum(hits * own_text[...], axis=0, keepdims=True)
        for i in range(width // 128):
            piece = slice(128 * i, 128 * i + 128)
            value[pl.ds(c * width // 128 + i, 1), :] = column_part[:, piece]
            value[pl.ds(tiles + c * width // 128 + i, 1), :] = owner_part[:, piece]
    spread = Spread(value, near, far, column_send, column_receive)
    spread.start_near()
    safe_row = jnp.where(row_total > 0, row_total, 1.0)
    text_weight = own_text[...] * text_hits
    total_part = total_of(0.5 * text_weight * jnp.log(safe_row) - text_weight * hit_logit)
    spread.wait_near()
    group = near[0]
    for i in range(1, mp_count):
        group = group + near[i]
    far[dp] = group
    spread.start_far()
    text_grad = jnp.zeros((own_count, D), jnp.float32)
    temp_part = column_loss = pairs = jnp.zeros((1, 1), jnp.float32)
    for c, lanes in enumerate(sections):
        row_weights = jnp.exp(logits[:, lanes]) * image_mask[:, lanes]
        row_grad = 0.5 * text_weight * (row_weights / safe_row - hits_of(c))
        temp_part += total_of(row_grad * logits[:, lanes])
        text_grad += dot((multiplier * row_grad).astype(half), images_of(c))
    spread.wait_far()
    spread.wait_near_sends()
    value[...] = far[0]

    @pl.loop(1, dp_count)
    def _(i):
        value[...] += far[i]

    def line_of(start):
        return jnp.concatenate([value[pl.ds(start + i, 1), :] for i in range(width // 128)], axis=1)

    for c, lanes in enumerate(sections):
        column_total = line_of(c * width // 128)
        image_weight = image_mask[:, lanes] * line_of(tiles + c * width // 128)
        safe_column = jnp.where(column_total > 0, column_total, 1.0)
        column_weights = jnp.exp(logits[:, lanes]) * own_text[...]
        column_grad = 0.5 * image_weight * (column_weights / safe_column - hits_of(c))
        temp_part += total_of(column_grad * logits[:, lanes])
        column_loss += total_of(0.5 * image_weight * jnp.log(safe_column))
        pairs += total_of(image_weight)
        text_grad += dot((multiplier * column_grad).astype(half), images_of(c))
    lane = lax.broadcasted_iota(jnp.int32, (8, D), 1)
    plain[...] = jnp.where(lane == 0, column_loss, jnp.where(lane == 1, pairs, 0.0))
    vectors[pl.ds(8, 8), :] = jnp.where(lane == 0, total_part, jnp.where(lane == 1, temp_part, 0.0))

    inverse = lax.rsqrt(jnp.sum(pooled * pooled, axis=-1, keepdims=True) + 1e-06)
    caption_grad = (1.0 / LEN) * inverse * (
        text_grad - text_unit * jnp.sum(text_unit * text_grad, axis=-1, keepdims=True)
    )
    vectors[pl.ds(5, 1), :] = LEN * jnp.sum(caption_grad, axis=0, keepdims=True)
    spot = lax.broadcasted_iota(jnp.int32, (rows_count, own_count), 0) // LEN
    repeat = jnp.where(
        spot == lax.broadcasted_iota(jnp.int32, (rows_count, own_count), 1), 1.0, 0.0
    ).astype(half)
    caption_half = caption_grad.astype(half)
    grad_rows = dot(repeat, caption_half).astype(half)
    caption_pair = jnp.concatenate([caption_half, caption_half])

    def stage_copies(piece):
        slot = piece % 3
        if piece < 8:
            m, kind = piece // 2, piece % 2
            return [
                pltpu.make_async_copy(
                    stage.at[slot],
                    stack.at[m // 2, m % 2, pl.ds(kind * D, D)],
                    stage_sem.at[slot, 0],
                )
            ]
        place = 2 * D + (3, 0, 1, 2)[piece - 8] * part_rows
        return [
            pltpu.make_async_copy(
                stage.at[slot, pl.ds(m * part_rows, part_rows)],
                stack.at[m // 2, m % 2, pl.ds(place, part_rows)],
                stage_sem.at[slot, m],
            )
            for m in range(QUARTERS)
        ]

    def emit(piece, gradient):
        if piece >= 3:
            for copy in stage_copies(piece - 3):
                copy.wait()
        stage[piece % 3] = gradient.astype(half)
        for copy in stage_copies(piece):
            copy.start()

    work[...] = jnp.zeros_like(work)
    for m in range(QUARTERS):
        emit(2 * m, dot_tn(sums[m], caption_pair))
        active_grad = dot_nt(grad_rows, leave[m])
        hidden_grad = active_grad * gelu_slope(pre[m])
        hidden_half = hidden_grad.astype(half)
        vectors[pl.ds(8 + 1 + m, 1), :] = jnp.sum(
            hidden_half.astype(jnp.float32), axis=0, keepdims=True
        )
        emit(2 * m + 1, dot_tn(normed_two[...], hidden_half))
        work[...] += dot_nt(hidden_half, entry[m])
    unit, inverse = hat(middle[...])
    grad = work[...]
    vectors[pl.ds(3, 1), :] = jnp.sum(grad * unit, axis=0, keepdims=True)
    vectors[pl.ds(4, 1), :] = jnp.sum(grad, axis=0, keepdims=True)
    caption_parts = split(caption_grad)
    token_grad = dot(repeat, caption_parts[:own_count]) + dot(repeat, caption_parts[own_count:])
    middle_grad = token_grad + hat_back(unit, inverse, grad * g2[...])
    middle[...] = middle_grad
    vectors[pl.ds(2, 1), :] = jnp.sum(middle_grad, axis=0, keepdims=True)
    attn_grad = middle_grad.astype(half)
    emit(8, dot_tn(mixed[...], attn_grad))
    mixed_grad[...] = dot_nt(attn_grad, squares[3]).astype(half)

    @pl.loop(0, rows_count // TEXT_WINDOW)
    def _(w):
        rows = pl.ds(pl.multiple_of(w * TEXT_WINDOW, TEXT_WINDOW), TEXT_WINDOW)
        for h in range(HEADS // 2):
            lanes = pl.ds(128 * h, 128)
            queries, keys, values = doubled(q[rows, lanes]), k[rows, lanes], v[rows, lanes]
            probs = probabilities(queries, keys)
            outer = doubled(mixed_grad[rows, lanes])
            probs_grad = dot_nt(outer, values)
            v[rows, lanes] = dot_tn(probs.astype(half), outer).astype(half)
            inner = jnp.sum(probs * probs_grad, axis=-1, keepdims=True)
            score_grad = (probs * (probs_grad - inner)).astype(half)
            q[rows, lanes] = (merge(dot(score_grad, keys)) * SCALE).astype(half)
            k[rows, lanes] = dot_tn(score_grad, queries).astype(half)

    vectors[pl.ds(6, 1), :] = jnp.sum(q[...].astype(jnp.float32), axis=0, keepdims=True)
    vectors[pl.ds(7, 1), :] = jnp.sum(v[...].astype(jnp.float32), axis=0, keepdims=True)
    for i, part in enumerate([q, k, v]):
        emit(9 + i, dot_tn(part[...], normed[...]))
    work[...] = (
        dot(q[...], squares[0]) + dot(k[...], squares[1]) + dot(v[...], squares[2])
    )
    unit, inverse = hat(x[...].astype(jnp.float32))
    grad = work[...]
    vectors[pl.ds(0, 1), :] = jnp.sum(grad * unit, axis=0, keepdims=True)
    vectors[pl.ds(1, 1), :] = jnp.sum(grad, axis=0, keepdims=True)
    in_grad[...] = middle[...] + hat_back(unit, inverse, grad * g1[...])

    for piece in range(9, 12):
        for copy in stage_copies(piece):
            copy.wait()
    spread.wait_far_sends()

    @pl.loop(1, dp_count)
    def _(step):
        far_image(step).wait_send()

    @pl.loop(0, dp_count)
    def _(step):
        x_image(step).wait_send()
        core_image(0, step).wait_send()
        core_image(1, step).wait_send()


def text_layer(dp_count, mp_count, operands, gathered):
    half = jnp.bfloat16
    vmem, any_space = pl.BlockSpec(memory_space=pltpu.VMEM), pl.BlockSpec(memory_space=pl.ANY)
    rows_count, own_count = operands[0].shape[0], operands[1].shape[0]
    lines = 2 * dp_count * mp_count * own_count // 128
    rows = pltpu.VMEM((rows_count, D), half)
    wide = pltpu.VMEM((rows_count, D), jnp.float32)
    matrices = pltpu.VMEM((QUARTERS, D, D), half)
    single, double = pltpu.SemaphoreType.DMA((dp_count,)), pltpu.SemaphoreType.DMA((2, dp_count))
    column = pltpu.SemaphoreType.DMA((mp_count + dp_count,))
    return pl.pallas_call(
        text_kernel,
        out_shape=(
            jax.ShapeDtypeStruct((rows_count, D), half),
            jax.ShapeDtypeStruct((rows_count, D), jnp.float32),
            jax.ShapeDtypeStruct((2, 2, 3 * D, D), half),
            jax.ShapeDtypeStruct((16, D), jnp.float32),
            jax.ShapeDtypeStruct((8, D), jnp.float32),
        ),
        in_specs=[vmem] * len(operands) + [any_space],
        out_specs=(vmem, vmem, any_space, vmem, vmem),
        scratch_shapes=[
            matrices,
            matrices,
            matrices,
            pltpu.SemaphoreType.DMA((6, QUARTERS)),
            pltpu.VMEM((dp_count, mp_count, own_count, D), half),
            single,
            single,
            single,
            single,
            double,
            double,
        ]
        + [rows] * 5
        + [
            wide,
            rows,
            pltpu.VMEM((QUARTERS, rows_count, D), jnp.float32),
            pltpu.VMEM((QUARTERS, 2 * own_count, D), half),
        ]
        + [
            pltpu.VMEM((TEXT_WINDOW, TEXT_WINDOW), jnp.float32),
            pltpu.VMEM((3, D, D), half),
            pltpu.SemaphoreType.DMA((3, QUARTERS)),
            pltpu.VMEM((own_count, lines * 64), jnp.float32),
            pltpu.VMEM((lines, 128), jnp.float32),
            pltpu.VMEM((mp_count, lines, 128), jnp.float32),
            pltpu.VMEM((dp_count, lines, 128), jnp.float32),
            column,
            column,
        ],
        compiler_params=pltpu.CompilerParams(
            collective_id=2, has_side_effects=True, vmem_limit_bytes=67043328
        ),
        name="text_layer",
    )(*operands, gathered)


def body(
    sentence_entry_words,
    sentence_present_marks,
    picture_present_marks,
    matched_picture_positions,
    stored_picture_patches,
    log_logit_multiplier,
    leading_standardizer_stretch,
    leading_standardizer_shift,
    lookup_coefficients,
    lookup_offset,
    address_coefficients,
    content_coefficients,
    content_offset,
    mixer_exit_coefficients,
    mixer_exit_offset,
    trailing_standardizer_stretch,
    trailing_standardizer_shift,
    perceptron_entry_coefficients,
    perceptron_inner_offset,
    perceptron_exit_coefficients,
    perceptron_exit_offset,
    picture_lookup_coefficients,
    picture_address_coefficients,
    picture_content_coefficients,
    picture_mixer_exit,
    picture_perceptron_entry,
    picture_perceptron_exit,
):
    own_count = sentence_present_marks.shape[0]
    dp_count, mp_count = lax.axis_size("dp"), lax.axis_size("mp")
    rank = lax.axis_index("mp")
    squares = jnp.concatenate(
        [
            lookup_coefficients.T,
            address_coefficients.T,
            content_coefficients.T,
            mixer_exit_coefficients,
        ]
    )
    small = jnp.concatenate(
        [
            lookup_offset,
            content_offset,
            perceptron_inner_offset,
            picture_present_marks.astype(jnp.float32),
        ]
    )
    quarter = D // mp_count
    marks_at = 2 * quarter + D
    small = jnp.pad(small, (0, 2048 - small.shape[0])).reshape(16, 128)
    image, gathered, small_all = image_layer(
        dp_count,
        mp_count,
        stored_picture_patches,
        (
            picture_lookup_coefficients,
            picture_address_coefficients,
            picture_content_coefficients,
            picture_mixer_exit,
            picture_perceptron_entry,
            picture_perceptron_exit,
        ),
        squares,
        perceptron_entry_coefficients,
        perceptron_exit_coefficients,
        small,
    )
    small_all = small_all.reshape(dp_count, mp_count, 2048)
    image_mask = small_all[:, :, marks_at : marks_at + own_count].reshape(1, -1)
    b_q = small_all[0, :, :quarter].reshape(1, D)
    b_v = small_all[0, :, quarter : 2 * quarter].reshape(1, D)
    b_h = small_all[0, :, 2 * quarter : marks_at]
    offset = lax.axis_index(("dp", "mp")) * own_count
    own_pair = lax.dynamic_slice_in_dim(matched_picture_positions, offset, own_count, 0)
    line = partial(jnp.reshape, shape=(1, D))
    output, text_in_grad, stack, vectors, plain = text_layer(
        dp_count,
        mp_count,
        (
            sentence_entry_words,
            image,
            sentence_present_marks.astype(jnp.float32)[:, None],
            own_pair[:, None],
            image_mask,
            jnp.exp(log_logit_multiplier).reshape(1, 1),
            line(leading_standardizer_stretch),
            line(leading_standardizer_shift),
            b_q,
            b_v,
            line(mixer_exit_offset),
            line(trailing_standardizer_stretch),
            line(trailing_standardizer_shift),
            b_h,
            line(perceptron_exit_offset),
        ),
        gathered,
    )
    own_grads, shared = gradient_sum(dp_count, stack, vectors)
    loss = jnp.reshape((shared[8, 0] + plain[0, 0]) / plain[0, 1], (1,))

    def rows_of(start, count):
        return own_grads[start : start + count].astype(jnp.float32)

    def own(vector):
        return lax.dynamic_slice_in_dim(vector, rank * quarter, quarter, 0)

    return (
        loss,
        output,
        text_in_grad,
        shared[8, 1:2],
        shared[0],
        shared[1],
        rows_of(2 * D, quarter).T,
        own(shared[6]),
        rows_of(2 * D + 1 * quarter, quarter).T,
        rows_of(2 * D + 2 * quarter, quarter).T,
        own(shared[7]),
        rows_of(2 * D + 3 * quarter, quarter),
        shared[2],
        shared[3],
        shared[4],
        rows_of(D, D),
        lax.dynamic_slice_in_dim(shared, 9 + rank, 1, 0)[0],
        rows_of(0, D),
        shared[5],
    )


def solution(mesh):
    in_specs = (
        P(("dp", "mp"), None),
        P(("dp", "mp")),
        P(("dp", "mp")),
        P(),
        P(("dp", "mp"), None),
        P(),
        P(),
        P(),
        P(None, "mp"),
        P("mp"),
        P(None, "mp"),
        P(None, "mp"),
        P("mp"),
        P("mp", None),
        P(),
        P(),
        P(),
        P(None, "mp"),
        P("mp"),
        P("mp", None),
        P(),
        P(),
        P(),
        P(),
        P(),
        P(),
        P(),
    )
    out_specs = (
        P(),
        P(("dp", "mp"), None),
        P(("dp", "mp"), None),
        P(),
        P(),
        P(),
        P(None, "mp"),
        P("mp"),
        P(None, "mp"),
        P(None, "mp"),
        P("mp"),
        P("mp", None),
        P(),
        P(),
        P(),
        P(None, "mp"),
        P("mp"),
        P("mp", None),
        P(),
    )
    return jax.shard_map(body, mesh=mesh, in_specs=in_specs, out_specs=out_specs, check_vma=False)
```

```python
from functools import partial

import jax
import jax.numpy as jnp
from jax import lax
from jax.experimental import pallas as pl
from jax.experimental.pallas import tpu as pltpu
from jax.sharding import PartitionSpec as P

D = 768
HEADS = 12
HD = 64
LEN = 16
PATCHES = 50
SCALE = HD ** (-0.5)
BLOCK = 8 * PATCHES
WINDOW = 112
STEP = 96
QUARTERS = 4
TEXT_WINDOW = 128
LOSS_WIDTH = 1024


def normalize(pooled):
    return pooled * lax.rsqrt(jnp.sum(pooled * pooled, axis=-1, keepdims=True) + 1e-06)


def dot(left, right):
    return lax.dot_general(
        left, right, (((1,), (0,)), ((), ())), preferred_element_type=jnp.float32
    )


def dot_nt(left, right):
    return lax.dot_general(
        left, right, (((1,), (1,)), ((), ())), preferred_element_type=jnp.float32
    )


def dot_tn(left, right):
    return lax.dot_general(
        left, right, (((0,), (0,)), ((), ())), preferred_element_type=jnp.float32
    )


def centre(tensor):
    centred = tensor - jnp.mean(tensor, axis=-1, keepdims=True)
    return centred * lax.rsqrt(jnp.mean(centred * centred, axis=-1, keepdims=True) + 1e-06)


def gelu(v):
    return 0.5 * v * (1.0 + jnp.tanh(0.7978845608028654 * (v + 0.044715 * v * v * v)))


MESH = pl.DeviceIdType.MESH
ROWS = 64
LAG = 2


def bit_of(value, bit):
    return lax.rem(lax.div(value, bit), 2)


def peer(axis, bit):
    dp, mp = lax.axis_index("dp"), lax.axis_index("mp")
    if axis == "dp":
        return (dp + bit - 2 * bit * bit_of(dp, bit), mp)
    return (dp, mp + bit - 2 * bit * bit_of(mp, bit))


def doubling_bits(dp_count):
    bits, bit = [], 1
    while bit < dp_count:
        bits.append(("dp", bit))
        bit *= 2
    return bits


def gradient_sum_kernel(dp_count, stack, small, out, small_out, keep, first, second, *rest):
    dp_bits = doubling_bits(dp_count)
    levels = len(dp_bits)
    parts, (whole, small_in, small_sum, send, receive, load, store, small_send, small_receive) = (
        rest[:levels],
        rest[levels:],
    )
    bits = [("mp", 1), ("mp", 2)] + dp_bits
    peers = [peer(*b) for b in bits]
    low, high = bit_of(lax.axis_index("mp"), 1), bit_of(lax.axis_index("mp"), 2)
    own = [bit_of(lax.axis_index("dp"), bit) for _, bit in dp_bits]
    chunks = stack.shape[2] // ROWS
    barrier = pltpu.get_barrier_semaphore()
    for p in peers:
        pl.semaphore_signal(barrier, inc=1, device_id=p, device_id_type=MESH)
    pl.semaphore_wait(barrier, len(peers))

    sizes = []
    size = ROWS
    for _ in dp_bits:
        halve = size >= 32
        size = size // 2 if halve else size
        sizes.append((size, halve))

    def add(target, other):
        target[...] = (target[...].astype(jnp.float32) + other[...].astype(jnp.float32)).astype(
            jnp.bfloat16
        )

    def rows(c):
        return pl.ds(pl.multiple_of(c * ROWS, ROWS), ROWS)

    def copy(stage, c):
        if stage == 0:
            source, target, who = stack.at[:, 1 - low, rows(c)], first.at[c], 0
        elif stage == 1:
            source, target, who = first.at[c, 1 - high], second.at[c], 1
        elif stage < 2 + levels:
            i = stage - 2
            n, halve = sizes[i]
            before = second if i == 0 else parts[i - 1]
            source = before.at[c, pl.ds((1 - own[i]) * n, n)] if halve else before.at[c]
            target, who = parts[i].at[c], stage
        else:
            i = gathers[stage - 2 - levels]
            n = sizes[i][0]
            where = sum(
                own[j] * sizes[j][0] for j in range(i + 1) if sizes[j][1]
            )
            source = target = whole.at[c, pl.ds(where, n)]
            who = 2 + i
        return pltpu.make_async_remote_copy(
            src_ref=source,
            dst_ref=target,
            send_sem=send.at[stage, c],
            recv_sem=receive.at[stage, c],
            device_id=peers[who],
            device_id_type=MESH,
        )

    gathers = [i for i in reversed(range(levels)) if sizes[i][1]]
    stages = 2 + levels + len(gathers)

    def load_copy(c):
        return pltpu.make_async_copy(stack.at[:, low, rows(c)], keep.at[c], load.at[c])

    def store_copy(c):
        return pltpu.make_async_copy(whole.at[c], out.at[rows(c)], store.at[c])

    def finish(stage, c):
        copy(stage, c).wait_recv()
        if stage == 0:
            load_copy(c).wait()
            add(first.at[c], keep.at[c])
        elif stage == 1:
            add(second.at[c], first.at[c, high])
        elif stage < 2 + levels:
            i = stage - 2
            n, halve = sizes[i]
            before = second if i == 0 else parts[i - 1]
            source = before.at[c, pl.ds(pl.multiple_of(own[i] * n, n), n)] if halve else before.at[c]
            if i < levels - 1:
                add(parts[i].at[c], source)
            else:
                where = sum(own[j] * sizes[j][0] for j in range(levels) if sizes[j][1])
                whole.at[c, pl.ds(pl.multiple_of(where, n), n)][...] = (
                    parts[i].at[c][...].astype(jnp.float32) + source[...].astype(jnp.float32)
                ).astype(jnp.bfloat16)

    def small_copy(i):
        return pltpu.make_async_remote_copy(
            src_ref=small if i == 0 else small_sum.at[i - 1],
            dst_ref=small_in.at[i],
            send_sem=small_send.at[i],
            recv_sem=small_receive.at[i],
            device_id=peers[i],
            device_id_type=MESH,
        )

    small_copy(0).start()

    @pl.loop(0, chunks + LAG * stages)
    def _(t):
        for slot in range(stages + 1):
            c = t - LAG * slot

            @pl.when((c >= 0) & (c < chunks))
            def _():
                if slot == 0:
                    load_copy(c).start()
                else:
                    finish(slot - 1, c)
                if slot < stages:
                    copy(slot, c).start()
                else:
                    store_copy(c).start()

        for i in range(len(bits)):

            @pl.when(t == 2 * i + 1)
            def _():
                small_copy(i).wait_recv()
                total = (small if i == 0 else small_sum.at[i - 1])[...] + small_in[i]
                if i < len(bits) - 1:
                    small_sum[i] = total
                    small_copy(i + 1).start()
                else:
                    small_out[...] = total

    for i in range(len(bits)):
        small_copy(i).wait_send()

    @pl.loop(0, chunks)
    def _(c):
        for stage in range(stages):
            copy(stage, c).wait_send()
        store_copy(c).wait()


def gradient_sum(dp_count, stack, small):
    levels = len(doubling_bits(dp_count))
    chunks = stack.shape[2] // ROWS
    sizes, size, halvings = [], ROWS, 0
    for _ in range(levels):
        halvings += size >= 32
        size = size // 2 if size >= 32 else size
        sizes.append(size)
    stages = 2 + levels + halvings
    half = jnp.bfloat16
    return pl.pallas_call(
        partial(gradient_sum_kernel, dp_count),
        out_shape=(
            jax.ShapeDtypeStruct(stack.shape[2:], half),
            jax.ShapeDtypeStruct(small.shape, jnp.float32),
        ),
        in_specs=[pl.BlockSpec(memory_space=pl.ANY), pl.BlockSpec(memory_space=pltpu.VMEM)],
        out_specs=(pl.BlockSpec(memory_space=pl.ANY), pl.BlockSpec(memory_space=pltpu.VMEM)),
        scratch_shapes=[
            pltpu.VMEM((chunks, 2, ROWS, D), half),
            pltpu.VMEM((chunks, 2, ROWS, D), half),
            pltpu.VMEM((chunks, ROWS, D), half),
        ]
        + [pltpu.VMEM((chunks, n, D), half) for n in sizes]
        + [
            pltpu.VMEM((chunks, ROWS, D), half),
            pltpu.VMEM((levels + 2,) + small.shape, jnp.float32),
            pltpu.VMEM((levels + 1,) + small.shape, jnp.float32),
            pltpu.SemaphoreType.DMA((stages, chunks)),
            pltpu.SemaphoreType.DMA((stages, chunks)),
            pltpu.SemaphoreType.DMA((chunks,)),
            pltpu.SemaphoreType.DMA((chunks,)),
            pltpu.SemaphoreType.DMA((levels + 2,)),
            pltpu.SemaphoreType.DMA((levels + 2,)),
        ],
        compiler_params=pltpu.CompilerParams(
            collective_id=1, has_side_effects=True, vmem_limit_bytes=56 * 2**20
        ),
        name="gradient_sum",
    )(stack, small)


def other(mp, bit):
    return mp + bit - 2 * bit * bit_of(mp, bit)


def greet(dp, mp, dp_count, mp_count):
    barrier = pltpu.get_barrier_semaphore()
    for step in range(1, mp_count):
        pl.semaphore_signal(
            barrier, inc=1, device_id=(dp, lax.rem(mp + step, mp_count)), device_id_type=MESH
        )

    @pl.loop(1, dp_count)
    def _(step):
        pl.semaphore_signal(
            barrier, inc=1, device_id=(lax.rem(dp + step, dp_count), mp), device_id_type=MESH
        )

    pl.semaphore_wait(barrier, mp_count + dp_count - 2)


class Spread:
    def __init__(self, value, near, far, send, receive):
        self.dp, self.mp = lax.axis_index("dp"), lax.axis_index("mp")
        self.dp_count, self.mp_count = far.shape[0], near.shape[0]
        self.value, self.near, self.far = value, near, far
        self.send, self.receive = send, receive

    def near_copy(self, step, sender):
        return pltpu.make_async_remote_copy(
            src_ref=self.value,
            dst_ref=self.near.at[sender],
            send_sem=self.send.at[step],
            recv_sem=self.receive.at[step],
            device_id=(self.dp, lax.rem(self.mp + step, self.mp_count)),
            device_id_type=MESH,
        )

    def far_copy(self, step, sender):
        return pltpu.make_async_remote_copy(
            src_ref=self.far.at[self.dp],
            dst_ref=self.far.at[sender],
            send_sem=self.send.at[self.mp_count + step],
            recv_sem=self.receive.at[self.mp_count + step],
            device_id=(lax.rem(self.dp + step, self.dp_count), self.mp),
            device_id_type=MESH,
        )

    def start_near(self):
        for step in range(1, self.mp_count):
            self.near_copy(step, self.mp).start()
        self.near[self.mp] = self.value[...]

    def wait_near(self):
        for step in range(1, self.mp_count):
            self.near_copy(step, lax.rem(self.mp + self.mp_count - step, self.mp_count)).wait_recv()

    def start_far(self):
        @pl.loop(1, self.dp_count)
        def _(step):
            self.far_copy(step, self.dp).start()

    def wait_far(self):
        @pl.loop(1, self.dp_count)
        def _(step):
            self.far_copy(
                step, lax.rem(self.dp + self.dp_count - step, self.dp_count)
            ).wait_recv()

    def wait_near_sends(self):
        for step in range(1, self.mp_count):
            self.near_copy(step, self.mp).wait_send()

    def wait_far_sends(self):
        @pl.loop(1, self.dp_count)
        def _(step):
            self.far_copy(step, self.dp).wait_send()


PIECE = 96
PIECES = 12


def image_kernel(
    x, wq, wk, wv, wo, we, wx, squares, entry, leave, small,
    out, gathered, packed, mask,
    bq, bk, bv, bo, be, bx, load, normed, q, k, v, mixed, middle, bias,
    own, own_load, own_store, send, receive, near, far, small_send, small_receive,
):
    step = pl.program_id(0)
    last = pl.num_programs(0) - 1
    dp, mp = lax.axis_index("dp"), lax.axis_index("mp")
    y = bit_of(dp, 1)
    across, beside, along = (dp, other(mp, 2)), (dp, other(mp, 1)), (other(dp, 1), mp)
    pairs = [(wq, bq), (wk, bk), (wv, bv), (wo, bo), (we, be), (wx, bx)]
    spread = Spread(small, near, far, small_send, small_receive)

    def load_copy(i):
        return pltpu.make_async_copy(pairs[i][0], pairs[i][1], load.at[i])

    def own_copy(i):
        return pltpu.make_async_copy((leave, entry, squares)[i], own.at[i], own_load.at[i])

    def keep_copy():
        return pltpu.make_async_copy(own, gathered.at[mp], own_store)

    def travel(kind, c):
        matrix = lax.div(c, PIECES // 3)
        start = lax.rem(c, PIECES // 3) * PIECE
        mine = pl.ds(pl.multiple_of(start + y * (D // 2), PIECE), PIECE)
        theirs = pl.ds(pl.multiple_of(start + (1 - y) * (D // 2), PIECE), PIECE)
        source_mp = other(mp, 2)
        if kind == 0:
            source, target, who = own.at[matrix, mine], gathered.at[mp, matrix, mine], across
        elif kind == 4:
            source, target, who = own.at[c], gathered.at[mp, c], beside
        else:
            rows = theirs if kind == 3 else mine
            source = target = gathered.at[source_mp, matrix, rows]
            who = along if kind == 1 else beside
        return pltpu.make_async_remote_copy(
            src_ref=source,
            dst_ref=target,
            send_sem=send.at[kind, c],
            recv_sem=receive.at[kind, c],
            device_id=who,
            device_id_type=MESH,
        )

    def forward_across(c):
        travel(0, c).wait_recv()
        travel(1, c).start()
        travel(2, c).start()

    def forward_along(c):
        travel(1, c).wait_recv()
        travel(3, c).start()

    def pump(j):
        n = step * 4 + j

        @pl.when((n >= 2) & (n < 2 + PIECES))
        def _():
            forward_across(n - 2)

        @pl.when((n >= 4) & (n < 4 + PIECES))
        def _():
            forward_along(n - 4)

    @pl.when(step == 0)
    def _():
        for i in range(3):
            own_copy(i).start()
        for i in range(6):
            load_copy(i).start()
        greet(dp, mp, far.shape[0], near.shape[0])
        spread.start_near()
        for i in range(3):
            own_copy(i).wait()

        @pl.loop(0, PIECES)
        def _(c):
            travel(0, c).start()

        for i in range(3):
            travel(4, i).start()
        keep_copy().start()
        for p in range(4):
            row = lax.broadcasted_iota(jnp.int32, (WINDOW, WINDOW), 0) + STEP * p
            column = lax.broadcasted_iota(jnp.int32, (WINDOW, WINDOW), 1) + STEP * p
            bias[p] = jnp.where(row // PATCHES == column // PATCHES, 0.0, -1e30)

    def ready(i):
        @pl.when(step == 0)
        def _():
            load_copy(i).wait()

    z = x[...].astype(jnp.float32)
    normed[...] = centre(z).astype(jnp.bfloat16)
    ready(0)
    q[...] = (dot(normed[...], bq[...]) * SCALE).astype(jnp.bfloat16)
    ready(1)
    k[...] = dot(normed[...], bk[...]).astype(jnp.bfloat16)
    ready(2)
    v[...] = dot(normed[...], bv[...]).astype(jnp.bfloat16)
    pump(0)

    @pl.when(step == 0)
    def _():
        spread.wait_near()
        group = near[0] + near[1]
        for m in range(2, near.shape[0]):
            group = group + near[m]
        packed[pl.ds(0, 4), :] = group[:4]
        for m in range(QUARTERS):
            packed[pl.ds(4 + m, 1), :] = near[m, pl.ds(3, 1), :]
        far[dp] = jnp.broadcast_to(group[2:3, :128], (8, 128))
        spread.start_far()

    first = lax.broadcasted_iota(jnp.int32, (WINDOW, 128), 1) < HD
    for p in range(4):
        if p == 2:
            pump(1)
        rows = pl.ds(STEP * p, WINDOW)
        for h in range(HEADS // 2):
            lanes = pl.ds(128 * h, 128)
            part = q[rows, lanes]
            none = jnp.zeros_like(part)
            both = jnp.concatenate([jnp.where(first, part, none), jnp.where(first, none, part)])
            scores = dot_nt(both, k[rows, lanes])
            scores = scores + jnp.concatenate([bias[p], bias[p]])
            weights = jnp.exp(scores - jnp.max(scores, axis=-1, keepdims=True))
            probs = (weights * (1.0 / jnp.sum(weights, axis=-1, keepdims=True))).astype(jnp.bfloat16)
            heads = dot(probs, v[rows, lanes])
            merged = jnp.where(first, heads[:WINDOW], heads[WINDOW:]).astype(jnp.bfloat16)
            if p:
                edge = pl.ds(STEP * p, 16)
                late = lax.broadcasted_iota(jnp.int32, (16, 128), 0) >= 2 * PATCHES * p - STEP * p
                mixed[edge, lanes] = jnp.where(late, merged[:16], mixed[edge, lanes])
                mixed[pl.ds(STEP * p + 16, WINDOW - 16), lanes] = merged[16:]
            else:
                mixed[rows, lanes] = merged
    pump(2)
    ready(3)
    middle[...] = x[...].astype(jnp.float32) + dot(mixed[...], bo[...])
    normed[...] = centre(middle[...]).astype(jnp.bfloat16)
    ready(4)
    ready(5)
    for c in range(4):
        if c == 2:
            pump(3)
        part = pl.ds(c * D, D)
        active = gelu(dot(normed[...], be[:, part])).astype(jnp.bfloat16)
        middle[...] += dot(active, bx[part, :])
    total = middle[...]
    high = total.astype(jnp.bfloat16)
    low = (total - high.astype(jnp.float32)).astype(jnp.bfloat16)
    owner = lax.broadcasted_iota(jnp.int32, (8, BLOCK), 1) // PATCHES
    pool = jnp.where(owner == lax.broadcasted_iota(jnp.int32, (8, BLOCK), 0), 1.0, 0.0)
    pool = pool.astype(jnp.bfloat16)
    pooled = (dot(pool, high) + dot(pool, low)) * (1.0 / PATCHES)
    out[...] = normalize(pooled)

    @pl.when(step == last)
    def _():
        spread.wait_far()
        for d in range(far.shape[0]):
            mask[:, pl.ds(128 * d, 128)] = far[d, pl.ds(0, 1), :]
        spread.wait_near_sends()
        spread.wait_far_sends()
        keep_copy().wait()
        for i in range(3):
            travel(4, i).wait()

        @pl.loop(0, PIECES)
        def _(c):
            travel(2, c).wait_recv()
            travel(3, c).wait_recv()
            for kind in range(4):
                travel(kind, c).wait_send()


def image_layer(dp_count, mp_count, tokens, frozen, squares, entry, leave, small):
    half = jnp.bfloat16
    any_space = pl.BlockSpec(memory_space=pl.ANY)
    blocks = tokens.shape[0] // BLOCK
    square = pltpu.VMEM((D, D), half)
    rows = pltpu.VMEM((BLOCK, D), half)
    kinds = pltpu.SemaphoreType.DMA((5, PIECES))
    return pl.pallas_call(
        image_kernel,
        grid=(blocks,),
        out_shape=(
            jax.ShapeDtypeStruct((blocks * 8, D), jnp.float32),
            jax.ShapeDtypeStruct((mp_count, 3, D, D), half),
            jax.ShapeDtypeStruct((8, D), jnp.float32),
            jax.ShapeDtypeStruct((1, dp_count * 128), jnp.float32),
        ),
        in_specs=[pl.BlockSpec((BLOCK, D), lambda i: (i, 0))]
        + [any_space] * 9
        + [pl.BlockSpec(memory_space=pltpu.VMEM)],
        out_specs=(
            pl.BlockSpec((8, D), lambda i: (i, 0)),
            any_space,
            pl.BlockSpec(memory_space=pltpu.VMEM),
            pl.BlockSpec(memory_space=pltpu.VMEM),
        ),
        scratch_shapes=[square] * 4
        + [
            pltpu.VMEM((D, 4 * D), half),
            pltpu.VMEM((4 * D, D), half),
            pltpu.SemaphoreType.DMA((6,)),
        ]
        + [rows] * 5
        + [
            pltpu.VMEM((BLOCK, D), jnp.float32),
            pltpu.VMEM((4, WINDOW, WINDOW), jnp.float32),
            pltpu.VMEM((3, D, D), half),
            pltpu.SemaphoreType.DMA((3,)),
            pltpu.SemaphoreType.DMA,
            kinds,
            kinds,
            pltpu.VMEM((mp_count,) + small.shape, jnp.float32),
            pltpu.VMEM((dp_count, 8, 128), jnp.float32),
            pltpu.SemaphoreType.DMA((mp_count + dp_count,)),
            pltpu.SemaphoreType.DMA((mp_count + dp_count,)),
        ],
        compiler_params=pltpu.CompilerParams(
            collective_id=3, has_side_effects=True, vmem_limit_bytes=56 * 2**20
        ),
        name="image_layer",
    )(tokens, *frozen, squares, entry, leave, small)


def gelu_slope(v):
    bend = jnp.tanh(0.7978845608028654 * (v + 0.044715 * v * v * v))
    inner = 0.7978845608028654 * (1.0 + 0.134145 * v * v)
    return 0.5 * (1.0 + bend) + 0.5 * v * (1.0 - bend * bend) * inner


def hat(tensor):
    centred = tensor - jnp.mean(tensor, axis=-1, keepdims=True)
    inverse = lax.rsqrt(jnp.mean(centred * centred, axis=-1, keepdims=True) + 1e-06)
    return centred * inverse, inverse


def hat_back(unit, inverse, grad):
    mean = jnp.mean(grad, axis=-1, keepdims=True)
    return inverse * (grad - mean - unit * jnp.mean(grad * unit, axis=-1, keepdims=True))


def split(v):
    high = v.astype(jnp.bfloat16)
    return jnp.concatenate([high, (v - high.astype(jnp.float32)).astype(jnp.bfloat16)])


def total_of(v):
    return jnp.sum(jnp.sum(v, axis=1, keepdims=True), axis=0, keepdims=True)


class Gather:
    def __init__(self, own, blocks, sems):
        self.dp, self.mp = lax.axis_index("dp"), lax.axis_index("mp")
        self.own, self.blocks, self.count = own, blocks, blocks.shape[0]
        self.sems = sems

    def copy(self, kind, step):
        who = lax.rem(self.dp + self.count - step, self.count)
        lane = other(self.mp, 2) if kind == 3 else self.mp
        target = (self.dp, other(self.mp, 2 if kind == 1 else 1))
        if kind == 0:
            who, target = self.dp, (lax.rem(self.dp + step, self.count), self.mp)
        home = kind == 0 or (kind < 3 and isinstance(step, int) and step == 0)
        block = self.blocks.at[who, lane]
        return pltpu.make_async_remote_copy(
            src_ref=self.own if home else block,
            dst_ref=block,
            send_sem=self.sems[0].at[kind, step],
            recv_sem=self.sems[1].at[kind, step],
            device_id=target,
            device_id_type=MESH,
        )

    def start(self):
        @pl.loop(1, self.count)
        def _(step):
            self.copy(0, step).start()

        self.copy(1, 0).start()
        self.copy(2, 0).start()

    def forward(self, low, high):
        @pl.loop(low, high)
        def _(step):
            self.copy(0, step).wait_recv()
            self.copy(1, step).start()
            self.copy(2, step).start()

    def forward_last(self):
        @pl.loop(0, self.count)
        def _(step):
            self.copy(1, step).wait_recv()
            self.copy(3, step).start()

    def arrive(self):
        @pl.loop(0, self.count)
        def _(step):
            self.copy(2, step).wait_recv()
            self.copy(3, step).wait_recv()

    def wait_sends(self):
        @pl.loop(1, self.count)
        def _(step):
            self.copy(0, step).wait_send()

        @pl.loop(0, self.count)
        def _(step):
            for kind in (1, 2, 3):
                self.copy(kind, step).wait_send()


class FactorGather:
    def __init__(self, sums, blocks, near, line, mate, keep):
        self.dp, self.mp = lax.axis_index("dp"), lax.axis_index("mp")
        self.sums, self.blocks = sums, blocks
        self.near, self.line, self.mate, self.keep = near, line, mate, keep
        self.count, self.half = blocks.shape[0], blocks.shape[0] // 2

    def near_copy(self, step):
        to = lax.rem(self.mp + step, QUARTERS)
        return pltpu.make_async_remote_copy(
            src_ref=self.sums.at[to],
            dst_ref=self.blocks.at[self.dp, self.mp],
            send_sem=self.near[0].at[step],
            recv_sem=self.near[1].at[step],
            device_id=(self.dp, to),
            device_id_type=MESH,
        )

    def keep_copy(self):
        return pltpu.make_async_copy(
            self.sums.at[self.mp], self.blocks.at[self.dp, self.mp], self.keep
        )

    def line_copy(self, step):
        return pltpu.make_async_remote_copy(
            src_ref=self.blocks.at[self.dp],
            dst_ref=self.blocks.at[self.dp],
            send_sem=self.line[0].at[step],
            recv_sem=self.line[1].at[step],
            device_id=(lax.rem(self.dp + 2 * step, self.count), self.mp),
            device_id_type=MESH,
        )

    def mate_copy(self, step):
        block = self.blocks.at[lax.rem(self.dp + self.count - 2 * step, self.count)]
        return pltpu.make_async_remote_copy(
            src_ref=block,
            dst_ref=block,
            send_sem=self.mate[0].at[step],
            recv_sem=self.mate[1].at[step],
            device_id=(other(self.dp, 1), self.mp),
            device_id_type=MESH,
        )

    def start(self):
        self.keep_copy().start()
        for step in range(1, QUARTERS):
            self.near_copy(step).start()

    def spread(self):
        self.keep_copy().wait()
        for step in range(1, QUARTERS):
            self.near_copy(step).wait_recv()

        @pl.loop(1, self.half)
        def _(step):
            self.line_copy(step).start()

        self.mate_copy(0).start()

    def forward(self, low, high):
        @pl.loop(low, high)
        def _(step):
            self.line_copy(step).wait_recv()
            self.mate_copy(step).start()

    def finish(self):
        @pl.loop(0, self.half)
        def _(step):
            self.mate_copy(step).wait()

        @pl.loop(1, self.half)
        def _(step):
            self.line_copy(step).wait_send()

        for step in range(1, QUARTERS):
            self.near_copy(step).wait_send()


def text_kernel(
    x, image, columns, image_mask, params, packed, gathered,
    text_out, in_grad, stack, vectors, plain, factors, rows_all,
    squares, entry, leave, load, images, image_sems, image_arrivals, row_sems, row_arrivals,
    own_rows, own_keep, factor_near, factor_near_in, factor_line, factor_line_in, factor_mate,
    factor_mate_in, factor_keep, normed, q, k, v, mixed, middle, normed_two, pre, sums, bias,
    stage, stage_sem, logits, value, near, far, column_send, column_receive,
):
    work, mixed_grad = in_grad, normed_two
    g1, s1, b_o, g2, s2, b_p = [params.at[pl.ds(i, 1)] for i in range(6)]
    b_q, b_v = packed.at[pl.ds(0, 1)], packed.at[pl.ds(1, 1)]
    own_text, own_pair = columns[:, 0:1].astype(jnp.float32), columns[:, 1:2]
    dp, mp = lax.axis_index("dp"), lax.axis_index("mp")
    dp_count, mp_count = far.shape[0], near.shape[0]
    rows_count, own_count = x.shape[0], columns.shape[0]
    part_rows = D // QUARTERS
    half = jnp.bfloat16

    def square_copy(i, m):
        return pltpu.make_async_copy(
            gathered.at[m, 2, pl.ds(i * part_rows, part_rows)],
            squares.at[i, pl.ds(m * part_rows, part_rows)],
            load.at[i, m],
        )

    def entry_copy(m):
        return pltpu.make_async_copy(gathered.at[m, 1], entry.at[m], load.at[4, m])

    def leave_copy(m):
        return pltpu.make_async_copy(gathered.at[m, 0], leave.at[m], load.at[5, m])

    for i in range(4):
        for m in range(QUARTERS):
            square_copy(i, m).start()
    for m in range(QUARTERS):
        entry_copy(m).start()
        leave_copy(m).start()
    images[dp, mp] = image[...].astype(half)
    greet(dp, mp, dp_count, mp_count)

    image_gather = Gather(images.at[dp, mp], images, (image_sems, image_arrivals))
    image_gather.start()
    row_gather = Gather(own_rows, rows_all, (row_sems, row_arrivals))
    factor_gather = FactorGather(
        sums,
        factors,
        (factor_near, factor_near_in),
        (factor_line, factor_line_in),
        (factor_mate, factor_mate_in),
        factor_keep,
    )

    def own_rows_copy():
        return pltpu.make_async_copy(own_rows, rows_all.at[dp, mp], own_keep)

    row = lax.broadcasted_iota(jnp.int32, (TEXT_WINDOW, TEXT_WINDOW), 0)
    column = lax.broadcasted_iota(jnp.int32, (TEXT_WINDOW, TEXT_WINDOW), 1)
    bias[...] = jnp.where((row // LEN == column // LEN) & (column <= row), 0.0, -1e30)
    first = lax.broadcasted_iota(jnp.int32, (TEXT_WINDOW, 128), 1) < HD

    unit, unused = hat(x[...].astype(jnp.float32))
    normed[...] = (unit * g1[...] + s1[...]).astype(half)
    for m in range(QUARTERS):
        square_copy(0, m).wait()
    q[...] = ((dot_nt(normed[...], squares[0]) + b_q[...]) * SCALE).astype(half)
    for m in range(QUARTERS):
        square_copy(1, m).wait()
    k[...] = dot_nt(normed[...], squares[1]).astype(half)
    for m in range(QUARTERS):
        square_copy(2, m).wait()
    v[...] = (dot_nt(normed[...], squares[2]) + b_v[...]).astype(half)

    def doubled(part):
        none = jnp.zeros_like(part)
        return jnp.concatenate([jnp.where(first, part, none), jnp.where(first, none, part)])

    def probabilities(both, keys):
        scores = dot_nt(both, keys) + jnp.concatenate([bias[...], bias[...]])
        weights = jnp.exp(scores - jnp.max(scores, axis=-1, keepdims=True))
        return weights * (1.0 / jnp.sum(weights, axis=-1, keepdims=True))

    def merge(heads):
        return jnp.where(first, heads[:TEXT_WINDOW], heads[TEXT_WINDOW:])

    @pl.loop(0, rows_count // TEXT_WINDOW)
    def _(w):
        rows = pl.ds(pl.multiple_of(w * TEXT_WINDOW, TEXT_WINDOW), TEXT_WINDOW)
        for h in range(HEADS // 2):
            lanes = pl.ds(128 * h, 128)
            probs = probabilities(doubled(q[rows, lanes]), k[rows, lanes]).astype(half)
            mixed[rows, lanes] = merge(dot(probs, v[rows, lanes])).astype(half)

    image_gather.forward(1, dp_count)
    for m in range(QUARTERS):
        square_copy(3, m).wait()
    middle[...] = x[...].astype(jnp.float32) + dot(mixed[...], squares[3]) + b_o[...]
    unit, unused = hat(middle[...])
    normed_two[...] = (unit * g2[...] + s2[...]).astype(half)
    owner = lax.broadcasted_iota(jnp.int32, (own_count, rows_count), 1) // LEN
    pool = jnp.where(owner == lax.broadcasted_iota(jnp.int32, (own_count, rows_count), 0), 1.0, 0.0)
    pool = pool.astype(half)
    work[...] = middle[...] + b_p[...]
    for m in range(QUARTERS):
        if m == 2:
            image_gather.forward_last()
        entry_copy(m).wait()
        leave_copy(m).wait()
        hidden = dot(normed_two[...], entry[m]) + packed[pl.ds(4 + m, 1), :]
        pre[m] = hidden
        active = gelu(hidden).astype(half)
        sums[m] = dot(pool, active).astype(half)
        work[...] += dot(active, leave[m])
    factor_gather.start()
    text_out[...] = work[...].astype(half)
    output = split(work[...])
    pooled = (dot(pool, output[:rows_count]) + dot(pool, output[rows_count:])) * (1.0 / LEN)

    image_gather.arrive()
    text_unit = normalize(pooled)
    everyone = image_mask.shape[1]
    width = LOSS_WIDTH
    multiplier = jnp.exp(params[pl.ds(6, 1), pl.ds(0, 1)])
    text_half = text_unit.astype(half)
    tiles = everyone // 128
    group_count = width // (mp_count * own_count)
    sections = [pl.ds(c * width, width) for c in range(everyone // width)]

    def images_of(c):
        return images[pl.ds(c * group_count, group_count)].reshape(width, D)

    def hits_of(c):
        place = lax.broadcasted_iota(jnp.int32, (own_count, width), 1) + c * width
        return jnp.where(place == own_pair, 1.0, 0.0)

    row_total = text_hits = hit_logit = jnp.zeros((own_count, 1), jnp.float32)
    for c, lanes in enumerate(sections):
        logits[:, lanes] = dot_nt(text_half, images_of(c)) * multiplier
        hits = hits_of(c)
        weights = jnp.exp(logits[:, lanes])
        row_total += jnp.sum(weights * image_mask[:, lanes], axis=1, keepdims=True)
        text_hits += jnp.sum(hits * image_mask[:, lanes], axis=1, keepdims=True)
        hit_logit += jnp.sum(hits * logits[:, lanes], axis=1, keepdims=True)
        column_part = jnp.sum(weights * own_text, axis=0, keepdims=True)
        owner_part = jnp.sum(hits * own_text, axis=0, keepdims=True)
        for i in range(width // 128):
            piece = slice(128 * i, 128 * i + 128)
            value[pl.ds(c * width // 128 + i, 1), :] = column_part[:, piece]
            value[pl.ds(tiles + c * width // 128 + i, 1), :] = owner_part[:, piece]
    spread = Spread(value, near, far, column_send, column_receive)
    spread.start_near()
    safe_row = jnp.where(row_total > 0, row_total, 1.0)
    text_weight = own_text * text_hits
    total_part = total_of(0.5 * text_weight * jnp.log(safe_row) - text_weight * hit_logit)
    spread.wait_near()
    group = near[0]
    for i in range(1, mp_count):
        group = group + near[i]
    far[dp] = group
    spread.start_far()
    text_grad = jnp.zeros((own_count, D), jnp.float32)
    temp_part = column_loss = pairs = jnp.zeros((1, 1), jnp.float32)
    for c, lanes in enumerate(sections):
        row_weights = jnp.exp(logits[:, lanes]) * image_mask[:, lanes]
        row_grad = 0.5 * text_weight * (row_weights / safe_row - hits_of(c))
        temp_part += total_of(row_grad * logits[:, lanes])
        text_grad += dot((multiplier * row_grad).astype(half), images_of(c))
    spread.wait_far()
    spread.wait_near_sends()
    value[...] = far[0]

    @pl.loop(1, dp_count)
    def _(i):
        value[...] += far[i]

    def line_of(start):
        return jnp.concatenate([value[pl.ds(start + i, 1), :] for i in range(width // 128)], axis=1)

    for c, lanes in enumerate(sections):
        column_total = line_of(c * width // 128)
        image_weight = image_mask[:, lanes] * line_of(tiles + c * width // 128)
        safe_column = jnp.where(column_total > 0, column_total, 1.0)
        column_weights = jnp.exp(logits[:, lanes]) * own_text
        column_grad = 0.5 * image_weight * (column_weights / safe_column - hits_of(c))
        temp_part += total_of(column_grad * logits[:, lanes])
        column_loss += total_of(0.5 * image_weight * jnp.log(safe_column))
        pairs += total_of(image_weight)
        text_grad += dot((multiplier * column_grad).astype(half), images_of(c))
    lane = lax.broadcasted_iota(jnp.int32, (8, D), 1)
    plain[...] = jnp.where(lane == 0, column_loss, jnp.where(lane == 1, pairs, 0.0))
    vectors[pl.ds(8, 8), :] = jnp.where(lane == 0, total_part, jnp.where(lane == 1, temp_part, 0.0))

    inverse = lax.rsqrt(jnp.sum(pooled * pooled, axis=-1, keepdims=True) + 1e-06)
    caption_grad = (1.0 / LEN) * inverse * (
        text_grad - text_unit * jnp.sum(text_unit * text_grad, axis=-1, keepdims=True)
    )
    vectors[pl.ds(5, 1), :] = LEN * jnp.sum(caption_grad, axis=0, keepdims=True)
    spot = lax.broadcasted_iota(jnp.int32, (rows_count, own_count), 0) // LEN
    repeat = jnp.where(
        spot == lax.broadcasted_iota(jnp.int32, (rows_count, own_count), 1), 1.0, 0.0
    ).astype(half)
    caption_half = caption_grad.astype(half)
    own_rows[...] = caption_half
    factor_gather.spread()
    own_rows_copy().start()
    row_gather.start()
    grad_rows = dot(repeat, caption_half).astype(half)

    def stage_copies(piece):
        slot = piece % 3
        if piece < 4:
            return [
                pltpu.make_async_copy(
                    stage.at[slot],
                    stack.at[piece // 2, piece % 2, pl.ds(0, D)],
                    stage_sem.at[slot, 0],
                )
            ]
        place = D + (3, 0, 1, 2)[piece - 4] * part_rows
        return [
            pltpu.make_async_copy(
                stage.at[slot, pl.ds(m * part_rows, part_rows)],
                stack.at[m // 2, m % 2, pl.ds(place, part_rows)],
                stage_sem.at[slot, m],
            )
            for m in range(QUARTERS)
        ]

    def emit(piece, gradient):
        if piece >= 3:
            for copy in stage_copies(piece - 3):
                copy.wait()
        stage[piece % 3] = gradient.astype(half)
        for copy in stage_copies(piece):
            copy.start()

    work[...] = jnp.zeros_like(work)
    for m in range(QUARTERS):
        active_grad = dot_nt(grad_rows, leave[m])
        hidden_grad = active_grad * gelu_slope(pre[m])
        hidden_half = hidden_grad.astype(half)
        vectors[pl.ds(9 + m, 1), :] = jnp.sum(
            hidden_half.astype(jnp.float32), axis=0, keepdims=True
        )
        emit(m, dot_tn(normed_two[...], hidden_half))
        work[...] += dot_nt(hidden_half, entry[m])
    unit, inverse = hat(middle[...])
    grad = work[...]
    vectors[pl.ds(3, 1), :] = jnp.sum(grad * unit, axis=0, keepdims=True)
    vectors[pl.ds(4, 1), :] = jnp.sum(grad, axis=0, keepdims=True)
    caption_parts = split(caption_grad)
    token_grad = dot(repeat, caption_parts[:own_count]) + dot(repeat, caption_parts[own_count:])
    middle_grad = token_grad + hat_back(unit, inverse, grad * g2[...])
    middle[...] = middle_grad
    vectors[pl.ds(2, 1), :] = jnp.sum(middle_grad, axis=0, keepdims=True)
    attn_grad = middle_grad.astype(half)
    factor_gather.forward(1, (dp_count // 2 + 1) // 2)
    emit(4, dot_tn(mixed[...], attn_grad))
    mixed_grad[...] = dot_nt(attn_grad, squares[3]).astype(half)

    @pl.loop(0, rows_count // TEXT_WINDOW)
    def _(w):
        rows = pl.ds(pl.multiple_of(w * TEXT_WINDOW, TEXT_WINDOW), TEXT_WINDOW)
        for h in range(HEADS // 2):
            lanes = pl.ds(128 * h, 128)
            queries, keys, values = doubled(q[rows, lanes]), k[rows, lanes], v[rows, lanes]
            probs = probabilities(queries, keys)
            outer = doubled(mixed_grad[rows, lanes])
            probs_grad = dot_nt(outer, values)
            v[rows, lanes] = dot_tn(probs.astype(half), outer).astype(half)
            inner = jnp.sum(probs * probs_grad, axis=-1, keepdims=True)
            score_grad = (probs * (probs_grad - inner)).astype(half)
            q[rows, lanes] = (merge(dot(score_grad, keys)) * SCALE).astype(half)
            k[rows, lanes] = dot_tn(score_grad, queries).astype(half)

    factor_gather.forward((dp_count // 2 + 1) // 2, dp_count // 2)
    vectors[pl.ds(6, 1), :] = jnp.sum(q[...].astype(jnp.float32), axis=0, keepdims=True)
    vectors[pl.ds(7, 1), :] = jnp.sum(v[...].astype(jnp.float32), axis=0, keepdims=True)
    for i, part in enumerate([q, k, v]):
        emit(5 + i, dot_tn(part[...], normed[...]))
    row_gather.forward(1, dp_count)
    work[...] = (
        dot(q[...], squares[0]) + dot(k[...], squares[1]) + dot(v[...], squares[2])
    )
    unit, inverse = hat(x[...].astype(jnp.float32))
    grad = work[...]
    vectors[pl.ds(0, 1), :] = jnp.sum(grad * unit, axis=0, keepdims=True)
    vectors[pl.ds(1, 1), :] = jnp.sum(grad, axis=0, keepdims=True)
    in_grad[...] = middle[...] + hat_back(unit, inverse, grad * g1[...])

    row_gather.forward_last()
    for piece in range(5, 8):
        for copy in stage_copies(piece):
            copy.wait()
    spread.wait_far_sends()
    own_rows_copy().wait()
    factor_gather.finish()
    row_gather.arrive()
    row_gather.wait_sends()
    image_gather.wait_sends()


def text_layer(dp_count, mp_count, operands, gathered):
    half = jnp.bfloat16
    vmem, any_space = pl.BlockSpec(memory_space=pltpu.VMEM), pl.BlockSpec(memory_space=pl.ANY)
    rows_count, own_count = operands[0].shape[0], operands[1].shape[0]
    lines = 2 * dp_count * mp_count * own_count // 128
    rows = pltpu.VMEM((rows_count, D), half)
    wide = pltpu.VMEM((rows_count, D), jnp.float32)
    matrices = pltpu.VMEM((QUARTERS, D, D), half)
    kinds, few = pltpu.SemaphoreType.DMA((4, dp_count)), pltpu.SemaphoreType.DMA((QUARTERS,))
    line = pltpu.SemaphoreType.DMA((dp_count // 2,))
    everyone = jax.ShapeDtypeStruct((dp_count, mp_count, own_count, D), half)
    column = pltpu.SemaphoreType.DMA((mp_count + dp_count,))
    return pl.pallas_call(
        text_kernel,
        out_shape=(
            jax.ShapeDtypeStruct((rows_count, D), half),
            jax.ShapeDtypeStruct((rows_count, D), jnp.float32),
            jax.ShapeDtypeStruct((2, 2, 2 * D, D), half),
            jax.ShapeDtypeStruct((16, D), jnp.float32),
            jax.ShapeDtypeStruct((8, D), jnp.float32),
            everyone,
            everyone,
        ),
        in_specs=[vmem] * len(operands) + [any_space],
        out_specs=(vmem, vmem, any_space, vmem, vmem, any_space, any_space),
        scratch_shapes=[
            matrices,
            matrices,
            matrices,
            pltpu.SemaphoreType.DMA((6, QUARTERS)),
            pltpu.VMEM((dp_count, mp_count, own_count, D), half),
            kinds,
            kinds,
            kinds,
            kinds,
            pltpu.VMEM((own_count, D), half),
            pltpu.SemaphoreType.DMA,
            few,
            few,
            line,
            line,
            line,
            line,
            pltpu.SemaphoreType.DMA,
        ]
        + [rows] * 5
        + [
            wide,
            rows,
            pltpu.VMEM((QUARTERS, rows_count, D), jnp.float32),
            pltpu.VMEM((QUARTERS, own_count, D), half),
        ]
        + [
            pltpu.VMEM((TEXT_WINDOW, TEXT_WINDOW), jnp.float32),
            pltpu.VMEM((3, D, D), half),
            pltpu.SemaphoreType.DMA((3, QUARTERS)),
            pltpu.VMEM((own_count, lines * 64), jnp.float32),
            pltpu.VMEM((lines, 128), jnp.float32),
            pltpu.VMEM((mp_count, lines, 128), jnp.float32),
            pltpu.VMEM((dp_count, lines, 128), jnp.float32),
            column,
            column,
        ],
        compiler_params=pltpu.CompilerParams(
            collective_id=2, has_side_effects=True, vmem_limit_bytes=67043328
        ),
        name="text_layer",
    )(*operands, gathered)


def body(
    sentence_entry_words,
    sentence_present_marks,
    picture_present_marks,
    matched_picture_positions,
    stored_picture_patches,
    log_logit_multiplier,
    leading_standardizer_stretch,
    leading_standardizer_shift,
    lookup_coefficients,
    lookup_offset,
    address_coefficients,
    content_coefficients,
    content_offset,
    mixer_exit_coefficients,
    mixer_exit_offset,
    trailing_standardizer_stretch,
    trailing_standardizer_shift,
    perceptron_entry_coefficients,
    perceptron_inner_offset,
    perceptron_exit_coefficients,
    perceptron_exit_offset,
    picture_lookup_coefficients,
    picture_address_coefficients,
    picture_content_coefficients,
    picture_mixer_exit,
    picture_perceptron_entry,
    picture_perceptron_exit,
):
    own_count = sentence_present_marks.shape[0]
    dp_count, mp_count = lax.axis_size("dp"), lax.axis_size("mp")
    rank = lax.axis_index("mp")
    squares = jnp.concatenate(
        [
            lookup_coefficients.T,
            address_coefficients.T,
            content_coefficients.T,
            mixer_exit_coefficients,
        ]
    )
    quarter = D // mp_count

    def placed(vector, size):
        empty = jnp.zeros((D,), jnp.float32)
        return lax.dynamic_update_slice_in_dim(empty, vector, rank * size, 0)

    small = jnp.stack(
        [
            placed(lookup_offset, quarter),
            placed(content_offset, quarter),
            placed(picture_present_marks.astype(jnp.float32), own_count),
            perceptron_inner_offset,
        ]
        + [jnp.zeros((D,), jnp.float32)] * 4
    )
    params = jnp.stack(
        [
            leading_standardizer_stretch,
            leading_standardizer_shift,
            mixer_exit_offset,
            trailing_standardizer_stretch,
            trailing_standardizer_shift,
            perceptron_exit_offset,
            jnp.broadcast_to(log_logit_multiplier, (D,)),
            jnp.zeros((D,), jnp.float32),
        ]
    )
    image, gathered, packed, image_mask = image_layer(
        dp_count,
        mp_count,
        stored_picture_patches,
        (
            picture_lookup_coefficients,
            picture_address_coefficients,
            picture_content_coefficients,
            picture_mixer_exit,
            picture_perceptron_entry,
            picture_perceptron_exit,
        ),
        squares,
        perceptron_entry_coefficients,
        perceptron_exit_coefficients,
        small,
    )
    offset = lax.axis_index(("dp", "mp")) * own_count
    own_pair = lax.dynamic_slice_in_dim(matched_picture_positions, offset, own_count, 0)
    columns = jnp.stack([sentence_present_marks, own_pair], axis=1)
    output, text_in_grad, stack, vectors, plain, factors, rows_all = text_layer(
        dp_count,
        mp_count,
        (sentence_entry_words, image, columns, image_mask, params, packed),
        gathered,
    )
    w_proj_grad = dot_tn(factors.reshape(-1, D), rows_all.reshape(-1, D))
    own_grads, shared = gradient_sum(dp_count, stack, vectors)
    loss = jnp.reshape((shared[8, 0] + plain[0, 0]) / plain[0, 1], (1,))

    def rows_of(start, count):
        return own_grads[start : start + count].astype(jnp.float32)

    def own(vector):
        return lax.dynamic_slice_in_dim(vector, rank * quarter, quarter, 0)

    return (
        loss,
        output,
        text_in_grad,
        shared[8, 1:2],
        shared[0],
        shared[1],
        rows_of(D, quarter).T,
        own(shared[6]),
        rows_of(D + 1 * quarter, quarter).T,
        rows_of(D + 2 * quarter, quarter).T,
        own(shared[7]),
        rows_of(D + 3 * quarter, quarter),
        shared[2],
        shared[3],
        shared[4],
        rows_of(0, D),
        lax.dynamic_slice_in_dim(shared, 9 + rank, 1, 0)[0],
        w_proj_grad,
        shared[5],
    )


def solution(mesh):
    in_specs = (
        P(("dp", "mp"), None),
        P(("dp", "mp")),
        P(("dp", "mp")),
        P(),
        P(("dp", "mp"), None),
        P(),
        P(),
        P(),
        P(None, "mp"),
        P("mp"),
        P(None, "mp"),
        P(None, "mp"),
        P("mp"),
        P("mp", None),
        P(),
        P(),
        P(),
        P(None, "mp"),
        P("mp"),
        P("mp", None),
        P(),
        P(),
        P(),
        P(),
        P(),
        P(),
        P(),
    )
    out_specs = (
        P(),
        P(("dp", "mp"), None),
        P(("dp", "mp"), None),
        P(),
        P(),
        P(),
        P(None, "mp"),
        P("mp"),
        P(None, "mp"),
        P(None, "mp"),
        P("mp"),
        P("mp", None),
        P(),
        P(),
        P(),
        P(None, "mp"),
        P("mp"),
        P("mp", None),
        P(),
    )
    return jax.shard_map(body, mesh=mesh, in_specs=in_specs, out_specs=out_specs, check_vma=False)
```

```python
from functools import partial

import jax
import jax.numpy as jnp
from jax import lax
from jax.experimental import pallas as pl
from jax.experimental.pallas import tpu as pltpu
from jax.sharding import PartitionSpec as P

D = 768
HEADS = 12
HD = 64
LEN = 16
PATCHES = 50
SCALE = HD ** (-0.5)
BLOCK = 8 * PATCHES
WINDOW = 112
STEP = 96
QUARTERS = 4
TEXT_WINDOW = 128
LOSS_WIDTH = 1024


def normalize(pooled):
    return pooled * lax.rsqrt(jnp.sum(pooled * pooled, axis=-1, keepdims=True) + 1e-06)


def dot(left, right):
    return lax.dot_general(
        left, right, (((1,), (0,)), ((), ())), preferred_element_type=jnp.float32
    )


def dot_nt(left, right):
    return lax.dot_general(
        left, right, (((1,), (1,)), ((), ())), preferred_element_type=jnp.float32
    )


def dot_tn(left, right):
    return lax.dot_general(
        left, right, (((0,), (0,)), ((), ())), preferred_element_type=jnp.float32
    )


def centre(tensor):
    centred = tensor - jnp.mean(tensor, axis=-1, keepdims=True)
    return centred * lax.rsqrt(jnp.mean(centred * centred, axis=-1, keepdims=True) + 1e-06)


def gelu(v):
    return 0.5 * v * (1.0 + jnp.tanh(0.7978845608028654 * (v + 0.044715 * v * v * v)))


MESH = pl.DeviceIdType.MESH
ROWS = 64
LAG = 2


def bit_of(value, bit):
    return lax.rem(lax.div(value, bit), 2)


def peer(axis, bit):
    dp, mp = lax.axis_index("dp"), lax.axis_index("mp")
    if axis == "dp":
        return (dp + bit - 2 * bit * bit_of(dp, bit), mp)
    return (dp, mp + bit - 2 * bit * bit_of(mp, bit))


def doubling_bits(dp_count):
    bits, bit = [], 1
    while bit < dp_count:
        bits.append(("dp", bit))
        bit *= 2
    return bits


def gradient_sum_kernel(dp_count, stack, small, out, small_out, keep, first, second, *rest):
    dp_bits = doubling_bits(dp_count)
    levels = len(dp_bits)
    parts, (whole, small_in, small_sum, send, receive, load, store, small_send, small_receive) = (
        rest[:levels],
        rest[levels:],
    )
    bits = [("mp", 1), ("mp", 2)] + dp_bits
    peers = [peer(*b) for b in bits]
    low, high = bit_of(lax.axis_index("mp"), 1), bit_of(lax.axis_index("mp"), 2)
    own = [bit_of(lax.axis_index("dp"), bit) for _, bit in dp_bits]
    chunks = stack.shape[2] // ROWS
    barrier = pltpu.get_barrier_semaphore()
    for p in peers:
        pl.semaphore_signal(barrier, inc=1, device_id=p, device_id_type=MESH)
    pl.semaphore_wait(barrier, len(peers))

    sizes = []
    size = ROWS
    for _ in dp_bits:
        halve = size >= 32
        size = size // 2 if halve else size
        sizes.append((size, halve))

    def add(target, other):
        target[...] = (target[...].astype(jnp.float32) + other[...].astype(jnp.float32)).astype(
            jnp.bfloat16
        )

    def rows(c):
        return pl.ds(pl.multiple_of(c * ROWS, ROWS), ROWS)

    def copy(stage, c):
        if stage == 0:
            source, target, who = stack.at[:, 1 - low, rows(c)], first.at[c], 0
        elif stage == 1:
            source, target, who = first.at[c, 1 - high], second.at[c], 1
        elif stage < 2 + levels:
            i = stage - 2
            n, halve = sizes[i]
            before = second if i == 0 else parts[i - 1]
            source = before.at[c, pl.ds((1 - own[i]) * n, n)] if halve else before.at[c]
            target, who = parts[i].at[c], stage
        else:
            i = gathers[stage - 2 - levels]
            n = sizes[i][0]
            where = sum(
                own[j] * sizes[j][0] for j in range(i + 1) if sizes[j][1]
            )
            source = target = whole.at[c, pl.ds(where, n)]
            who = 2 + i
        return pltpu.make_async_remote_copy(
            src_ref=source,
            dst_ref=target,
            send_sem=send.at[stage, c],
            recv_sem=receive.at[stage, c],
            device_id=peers[who],
            device_id_type=MESH,
        )

    gathers = [i for i in reversed(range(levels)) if sizes[i][1]]
    stages = 2 + levels + len(gathers)

    def load_copy(c):
        return pltpu.make_async_copy(stack.at[:, low, rows(c)], keep.at[c], load.at[c])

    def store_copy(c):
        return pltpu.make_async_copy(whole.at[c], out.at[rows(c)], store.at[c])

    def finish(stage, c):
        copy(stage, c).wait_recv()
        if stage == 0:
            load_copy(c).wait()
            add(first.at[c], keep.at[c])
        elif stage == 1:
            add(second.at[c], first.at[c, high])
        elif stage < 2 + levels:
            i = stage - 2
            n, halve = sizes[i]
            before = second if i == 0 else parts[i - 1]
            source = before.at[c, pl.ds(pl.multiple_of(own[i] * n, n), n)] if halve else before.at[c]
            if i < levels - 1:
                add(parts[i].at[c], source)
            else:
                where = sum(own[j] * sizes[j][0] for j in range(levels) if sizes[j][1])
                whole.at[c, pl.ds(pl.multiple_of(where, n), n)][...] = (
                    parts[i].at[c][...].astype(jnp.float32) + source[...].astype(jnp.float32)
                ).astype(jnp.bfloat16)

    def small_copy(i):
        return pltpu.make_async_remote_copy(
            src_ref=small if i == 0 else small_sum.at[i - 1],
            dst_ref=small_in.at[i],
            send_sem=small_send.at[i],
            recv_sem=small_receive.at[i],
            device_id=peers[i],
            device_id_type=MESH,
        )

    small_copy(0).start()

    @pl.loop(0, chunks + LAG * stages)
    def _(t):
        for slot in range(stages + 1):
            c = t - LAG * slot

            @pl.when((c >= 0) & (c < chunks))
            def _():
                if slot == 0:
                    load_copy(c).start()
                else:
                    finish(slot - 1, c)
                if slot < stages:
                    copy(slot, c).start()
                else:
                    store_copy(c).start()

        for i in range(len(bits)):

            @pl.when(t == 2 * i + 1)
            def _():
                small_copy(i).wait_recv()
                total = (small if i == 0 else small_sum.at[i - 1])[...] + small_in[i]
                if i < len(bits) - 1:
                    small_sum[i] = total
                    small_copy(i + 1).start()
                else:
                    small_out[...] = total

    for i in range(len(bits)):
        small_copy(i).wait_send()

    @pl.loop(0, chunks)
    def _(c):
        for stage in range(stages):
            copy(stage, c).wait_send()
        store_copy(c).wait()


def gradient_sum(dp_count, stack, small):
    levels = len(doubling_bits(dp_count))
    chunks = stack.shape[2] // ROWS
    sizes, size, halvings = [], ROWS, 0
    for _ in range(levels):
        halvings += size >= 32
        size = size // 2 if size >= 32 else size
        sizes.append(size)
    stages = 2 + levels + halvings
    half = jnp.bfloat16
    return pl.pallas_call(
        partial(gradient_sum_kernel, dp_count),
        out_shape=(
            jax.ShapeDtypeStruct(stack.shape[2:], half),
            jax.ShapeDtypeStruct(small.shape, jnp.float32),
        ),
        in_specs=[pl.BlockSpec(memory_space=pl.ANY), pl.BlockSpec(memory_space=pltpu.VMEM)],
        out_specs=(pl.BlockSpec(memory_space=pl.ANY), pl.BlockSpec(memory_space=pltpu.VMEM)),
        scratch_shapes=[
            pltpu.VMEM((chunks, 2, ROWS, D), half),
            pltpu.VMEM((chunks, 2, ROWS, D), half),
            pltpu.VMEM((chunks, ROWS, D), half),
        ]
        + [pltpu.VMEM((chunks, n, D), half) for n in sizes]
        + [
            pltpu.VMEM((chunks, ROWS, D), half),
            pltpu.VMEM((levels + 2,) + small.shape, jnp.float32),
            pltpu.VMEM((levels + 1,) + small.shape, jnp.float32),
            pltpu.SemaphoreType.DMA((stages, chunks)),
            pltpu.SemaphoreType.DMA((stages, chunks)),
            pltpu.SemaphoreType.DMA((chunks,)),
            pltpu.SemaphoreType.DMA((chunks,)),
            pltpu.SemaphoreType.DMA((levels + 2,)),
            pltpu.SemaphoreType.DMA((levels + 2,)),
        ],
        compiler_params=pltpu.CompilerParams(
            collective_id=1, has_side_effects=True, vmem_limit_bytes=56 * 2**20
        ),
        name="gradient_sum",
    )(stack, small)


def other(mp, bit):
    return mp + bit - 2 * bit * bit_of(mp, bit)


def greet(dp, mp, dp_count, mp_count):
    barrier = pltpu.get_barrier_semaphore()
    for step in range(1, mp_count):
        pl.semaphore_signal(
            barrier, inc=1, device_id=(dp, lax.rem(mp + step, mp_count)), device_id_type=MESH
        )

    @pl.loop(1, dp_count)
    def _(step):
        pl.semaphore_signal(
            barrier, inc=1, device_id=(lax.rem(dp + step, dp_count), mp), device_id_type=MESH
        )


def greeted(dp_count, mp_count):
    pl.semaphore_wait(pltpu.get_barrier_semaphore(), mp_count + dp_count - 2)


class Spread:
    def __init__(self, value, near, far, send, receive):
        self.dp, self.mp = lax.axis_index("dp"), lax.axis_index("mp")
        self.dp_count, self.mp_count = far.shape[0], near.shape[0]
        self.value, self.near, self.far = value, near, far
        self.send, self.receive = send, receive

    def near_copy(self, step, sender):
        return pltpu.make_async_remote_copy(
            src_ref=self.value,
            dst_ref=self.near.at[sender],
            send_sem=self.send.at[step],
            recv_sem=self.receive.at[step],
            device_id=(self.dp, lax.rem(self.mp + step, self.mp_count)),
            device_id_type=MESH,
        )

    def far_copy(self, step, sender):
        return pltpu.make_async_remote_copy(
            src_ref=self.far.at[self.dp],
            dst_ref=self.far.at[sender],
            send_sem=self.send.at[self.mp_count + step],
            recv_sem=self.receive.at[self.mp_count + step],
            device_id=(lax.rem(self.dp + step, self.dp_count), self.mp),
            device_id_type=MESH,
        )

    def start_near(self):
        for step in range(1, self.mp_count):
            self.near_copy(step, self.mp).start()
        self.near[self.mp] = self.value[...]

    def wait_near(self):
        for step in range(1, self.mp_count):
            self.near_copy(step, lax.rem(self.mp + self.mp_count - step, self.mp_count)).wait_recv()

    def start_far(self):
        @pl.loop(1, self.dp_count)
        def _(step):
            self.far_copy(step, self.dp).start()

    def wait_far(self):
        @pl.loop(1, self.dp_count)
        def _(step):
            self.far_copy(
                step, lax.rem(self.dp + self.dp_count - step, self.dp_count)
            ).wait_recv()

    def wait_near_sends(self):
        for step in range(1, self.mp_count):
            self.near_copy(step, self.mp).wait_send()

    def wait_far_sends(self):
        @pl.loop(1, self.dp_count)
        def _(step):
            self.far_copy(step, self.dp).wait_send()


PIECE = 96
PIECES = 6


def image_kernel(
    x, wq, wk, wv, wo, we, wx, squares, entry, leave, small,
    out, gathered, packed, mask,
    bq, bk, bv, bo, be, bx, load, normed, q, k, v, mixed, middle, bias,
    own, own_load, own_store, send, receive, near, far, small_send, small_receive,
):
    step = pl.program_id(0)
    last = pl.num_programs(0) - 1
    dp, mp = lax.axis_index("dp"), lax.axis_index("mp")
    y_bit, z_bit = bit_of(dp, 1), bit_of(dp, 2)
    across, beside = (dp, other(mp, 2)), (dp, other(mp, 1))
    along, behind = (other(dp, 1), mp), (other(dp, 2), mp)
    pairs = [(wq, bq), (wk, bk), (wv, bv), (wo, bo), (we, be), (wx, bx)]
    spread = Spread(small.at[pl.ds(8, 8)], near, far, small_send, small_receive)

    def load_copy(i):
        return pltpu.make_async_copy(pairs[i][0], pairs[i][1], load.at[i])

    def own_copy(i):
        return pltpu.make_async_copy((leave, entry, squares)[i], own.at[i], own_load.at[i])

    def keep_copy():
        return pltpu.make_async_copy(own, gathered.at[mp], own_store)

    def travel(kind, c):
        if kind == 9:
            source, target, who = own.at[c], gathered.at[mp, c], beside
        else:
            quarter = (y_bit if kind in (0, 1, 2, 3, 6, 7) else 1 - y_bit) + 2 * (
                z_bit if kind in (0, 1, 2, 3, 4, 5) else 1 - z_bit
            )
            matrix = lax.div(c, PIECES // 3)
            start = lax.rem(c, PIECES // 3) * PIECE + quarter * (D // 4)
            rows = pl.ds(pl.multiple_of(start, PIECE), PIECE)
            if kind == 0:
                source, target = own.at[matrix, rows], gathered.at[mp, matrix, rows]
            else:
                source = target = gathered.at[other(mp, 2), matrix, rows]
            who = (across, along, behind, beside, beside, behind, beside, along, beside)[kind]
        return pltpu.make_async_remote_copy(
            src_ref=source,
            dst_ref=target,
            send_sem=send.at[kind, c],
            recv_sem=receive.at[kind, c],
            device_id=who,
            device_id_type=MESH,
        )

    def early_or_late(c, early, late):
        @pl.when(c < PIECES // 2)
        def _():
            early()

        @pl.when(c >= PIECES // 2)
        def _():
            late()

    def forward_first(c):
        travel(0, c).wait_recv()
        for kind in (1, 2, 3):
            travel(kind, c).start()

    def forward_second(c):
        travel(1, c).wait_recv()
        travel(4, c).start()
        travel(2, c).wait_recv()
        travel(6, c).start()
        early_or_late(c, travel(5, c).start, travel(7, c).start)

    def forward_third(c):
        early_or_late(c, travel(5, c).wait_recv, travel(7, c).wait_recv)
        travel(8, c).start()

    def pump(j):
        n = step * 4 + j

        for lag, forward in ((3, forward_first), (6, forward_second), (10, forward_third)):

            @pl.when((n >= lag) & (n < lag + PIECES))
            def _():
                forward(n - lag)

    @pl.when(step == 0)
    def _():
        for i in range(3):
            own_copy(i).start()
        for i in range(6):
            load_copy(i).start()
        greet(dp, mp, far.shape[0], near.shape[0])
        for p in range(4):
            row = lax.broadcasted_iota(jnp.int32, (WINDOW, WINDOW), 0) + STEP * p
            column = lax.broadcasted_iota(jnp.int32, (WINDOW, WINDOW), 1) + STEP * p
            bias[p] = jnp.where(row // PATCHES == column // PATCHES, 0.0, -1e30)

    def ready(i):
        @pl.when(step == 0)
        def _():
            load_copy(i).wait()

    z = x[...].astype(jnp.float32)
    normed[...] = centre(z).astype(jnp.bfloat16)
    ready(0)
    q[...] = (dot(normed[...], bq[...]) * SCALE).astype(jnp.bfloat16)

    @pl.when(step == 0)
    def _():
        greeted(far.shape[0], near.shape[0])
        spread.start_near()
        for i in range(3):
            own_copy(i).wait()

        @pl.loop(0, PIECES)
        def _(c):
            travel(0, c).start()

        for i in range(3):
            travel(9, i).start()
        keep_copy().start()

    ready(1)
    k[...] = dot(normed[...], bk[...]).astype(jnp.bfloat16)
    ready(2)
    v[...] = dot(normed[...], bv[...]).astype(jnp.bfloat16)
    pump(0)
    first = lax.broadcasted_iota(jnp.int32, (WINDOW, 128), 1) < HD

    @pl.when(step == 1)
    def _():
        spread.wait_near()
        group = near[0] + near[1]
        for m in range(2, near.shape[0]):
            group = group + near[m]
        packed[pl.ds(0, 4), :] = group[:4]
        for m in range(QUARTERS):
            packed[pl.ds(4 + m, 1), :] = near[m, pl.ds(3, 1), :]
        far[dp] = jnp.broadcast_to(group[2:3, :128], (8, 128))
        spread.start_far()

    for p in range(4):
        if p == 2:
            pump(1)
        rows = pl.ds(STEP * p, WINDOW)
        for h in range(HEADS // 2):
            lanes = pl.ds(128 * h, 128)
            part = q[rows, lanes]
            none = jnp.zeros_like(part)
            both = jnp.concatenate([jnp.where(first, part, none), jnp.where(first, none, part)])
            scores = dot_nt(both, k[rows, lanes])
            scores = scores + jnp.concatenate([bias[p], bias[p]])
            weights = jnp.exp(scores - jnp.max(scores, axis=-1, keepdims=True))
            probs = (weights * (1.0 / jnp.sum(weights, axis=-1, keepdims=True))).astype(jnp.bfloat16)
            heads = dot(probs, v[rows, lanes])
            merged = jnp.where(first, heads[:WINDOW], heads[WINDOW:]).astype(jnp.bfloat16)
            if p:
                edge = pl.ds(STEP * p, 16)
                late = lax.broadcasted_iota(jnp.int32, (16, 128), 0) >= 2 * PATCHES * p - STEP * p
                mixed[edge, lanes] = jnp.where(late, merged[:16], mixed[edge, lanes])
                mixed[pl.ds(STEP * p + 16, WINDOW - 16), lanes] = merged[16:]
            else:
                mixed[rows, lanes] = merged
    pump(2)
    ready(3)
    middle[...] = x[...].astype(jnp.float32) + dot(mixed[...], bo[...])
    normed[...] = centre(middle[...]).astype(jnp.bfloat16)
    ready(4)
    ready(5)
    for c in range(4):
        if c == 2:
            pump(3)
        part = pl.ds(c * D, D)
        active = gelu(dot(normed[...], be[:, part])).astype(jnp.bfloat16)
        middle[...] += dot(active, bx[part, :])
    total = middle[...]
    high = total.astype(jnp.bfloat16)
    low = (total - high.astype(jnp.float32)).astype(jnp.bfloat16)
    owner = lax.broadcasted_iota(jnp.int32, (8, BLOCK), 1) // PATCHES
    pool = jnp.where(owner == lax.broadcasted_iota(jnp.int32, (8, BLOCK), 0), 1.0, 0.0)
    pool = pool.astype(jnp.bfloat16)
    pooled = (dot(pool, high) + dot(pool, low)) * (1.0 / PATCHES)
    out[...] = normalize(pooled)

    @pl.when(step == last)
    def _():
        spread.wait_far()
        for d in range(far.shape[0]):
            mask[:, pl.ds(128 * d, 128)] = far[d, pl.ds(0, 1), :]
        spread.wait_near_sends()
        spread.wait_far_sends()
        keep_copy().wait()
        for i in range(3):
            travel(9, i).wait()

        @pl.loop(0, PIECES)
        def _(c):
            for kind in (3, 4, 6, 8):
                travel(kind, c).wait_recv()
            for kind in (0, 1, 2, 3, 4, 6, 8):
                travel(kind, c).wait_send()
            early_or_late(c, travel(5, c).wait_send, travel(7, c).wait_send)


def image_layer(dp_count, mp_count, tokens, frozen, squares, entry, leave, small):
    half = jnp.bfloat16
    any_space = pl.BlockSpec(memory_space=pl.ANY)
    blocks = tokens.shape[0] // BLOCK
    square = pltpu.VMEM((D, D), half)
    rows = pltpu.VMEM((BLOCK, D), half)
    kinds = pltpu.SemaphoreType.DMA((10, PIECES))
    return pl.pallas_call(
        image_kernel,
        grid=(blocks,),
        out_shape=(
            jax.ShapeDtypeStruct((blocks * 8, D), jnp.float32),
            jax.ShapeDtypeStruct((mp_count, 3, D, D), half),
            jax.ShapeDtypeStruct((8, D), jnp.float32),
            jax.ShapeDtypeStruct((1, dp_count * 128), jnp.float32),
        ),
        in_specs=[pl.BlockSpec((BLOCK, D), lambda i: (i, 0))]
        + [any_space] * 9
        + [pl.BlockSpec(memory_space=pltpu.VMEM)],
        out_specs=(
            pl.BlockSpec((8, D), lambda i: (i, 0)),
            any_space,
            pl.BlockSpec(memory_space=pltpu.VMEM),
            pl.BlockSpec(memory_space=pltpu.VMEM),
        ),
        scratch_shapes=[square] * 4
        + [
            pltpu.VMEM((D, 4 * D), half),
            pltpu.VMEM((4 * D, D), half),
            pltpu.SemaphoreType.DMA((6,)),
        ]
        + [rows] * 5
        + [
            pltpu.VMEM((BLOCK, D), jnp.float32),
            pltpu.VMEM((4, WINDOW, WINDOW), jnp.float32),
            pltpu.VMEM((3, D, D), half),
            pltpu.SemaphoreType.DMA((3,)),
            pltpu.SemaphoreType.DMA,
            kinds,
            kinds,
            pltpu.VMEM((mp_count, 8, D), jnp.float32),
            pltpu.VMEM((dp_count, 8, 128), jnp.float32),
            pltpu.SemaphoreType.DMA((mp_count + dp_count,)),
            pltpu.SemaphoreType.DMA((mp_count + dp_count,)),
        ],
        compiler_params=pltpu.CompilerParams(
            collective_id=3, has_side_effects=True, vmem_limit_bytes=56 * 2**20
        ),
        name="image_layer",
    )(tokens, *frozen, squares, entry, leave, small)


def gelu_slope(v):
    bend = jnp.tanh(0.7978845608028654 * (v + 0.044715 * v * v * v))
    inner = 0.7978845608028654 * (1.0 + 0.134145 * v * v)
    return 0.5 * (1.0 + bend) + 0.5 * v * (1.0 - bend * bend) * inner


def hat(tensor):
    centred = tensor - jnp.mean(tensor, axis=-1, keepdims=True)
    inverse = lax.rsqrt(jnp.mean(centred * centred, axis=-1, keepdims=True) + 1e-06)
    return centred * inverse, inverse


def hat_back(unit, inverse, grad):
    mean = jnp.mean(grad, axis=-1, keepdims=True)
    return inverse * (grad - mean - unit * jnp.mean(grad * unit, axis=-1, keepdims=True))


def split(v):
    high = v.astype(jnp.bfloat16)
    return jnp.concatenate([high, (v - high.astype(jnp.float32)).astype(jnp.bfloat16)])


def total_of(v):
    return jnp.sum(jnp.sum(v, axis=1, keepdims=True), axis=0, keepdims=True)


class Gather:
    def __init__(self, own, blocks, sems):
        self.dp, self.mp = lax.axis_index("dp"), lax.axis_index("mp")
        self.own, self.blocks, self.count = own, blocks, blocks.shape[0]
        self.sems = sems

    def copy(self, kind, step):
        who = lax.rem(self.dp + self.count - step, self.count)
        lane = other(self.mp, 2) if kind == 3 else self.mp
        target = (self.dp, other(self.mp, 2 if kind == 1 else 1))
        if kind == 0:
            who, target = self.dp, (lax.rem(self.dp + step, self.count), self.mp)
        home = kind == 0 or (kind < 3 and isinstance(step, int) and step == 0)
        block = self.blocks.at[who, lane]
        return pltpu.make_async_remote_copy(
            src_ref=self.own if home else block,
            dst_ref=block,
            send_sem=self.sems[0].at[kind, step],
            recv_sem=self.sems[1].at[kind, step],
            device_id=target,
            device_id_type=MESH,
        )

    def start(self):
        @pl.loop(1, self.count)
        def _(step):
            self.copy(0, step).start()

        self.copy(1, 0).start()
        self.copy(2, 0).start()

    def forward(self, low, high):
        @pl.loop(low, high)
        def _(step):
            self.copy(0, step).wait_recv()
            self.copy(1, step).start()
            self.copy(2, step).start()

    def forward_last(self):
        @pl.loop(0, self.count)
        def _(step):
            self.copy(1, step).wait_recv()
            self.copy(3, step).start()

    def arrive(self):
        @pl.loop(0, self.count)
        def _(step):
            self.copy(2, step).wait_recv()
            self.copy(3, step).wait_recv()

    def wait_sends(self):
        @pl.loop(1, self.count)
        def _(step):
            self.copy(0, step).wait_send()

        @pl.loop(0, self.count)
        def _(step):
            for kind in (1, 2, 3):
                self.copy(kind, step).wait_send()


class FactorGather:
    def __init__(self, sums, blocks, near, line, mate, keep):
        self.dp, self.mp = lax.axis_index("dp"), lax.axis_index("mp")
        self.sums, self.blocks = sums, blocks
        self.near, self.line, self.mate, self.keep = near, line, mate, keep
        self.count, self.half = blocks.shape[0], blocks.shape[0] // 2

    def near_copy(self, step):
        to = lax.rem(self.mp + step, QUARTERS)
        return pltpu.make_async_remote_copy(
            src_ref=self.sums.at[to],
            dst_ref=self.blocks.at[self.dp, self.mp],
            send_sem=self.near[0].at[step],
            recv_sem=self.near[1].at[step],
            device_id=(self.dp, to),
            device_id_type=MESH,
        )

    def keep_copy(self):
        return pltpu.make_async_copy(
            self.sums.at[self.mp], self.blocks.at[self.dp, self.mp], self.keep
        )

    def line_copy(self, step):
        return pltpu.make_async_remote_copy(
            src_ref=self.blocks.at[self.dp],
            dst_ref=self.blocks.at[self.dp],
            send_sem=self.line[0].at[step],
            recv_sem=self.line[1].at[step],
            device_id=(lax.rem(self.dp + 2 * step, self.count), self.mp),
            device_id_type=MESH,
        )

    def mate_copy(self, step):
        block = self.blocks.at[lax.rem(self.dp + self.count - 2 * step, self.count)]
        return pltpu.make_async_remote_copy(
            src_ref=block,
            dst_ref=block,
            send_sem=self.mate[0].at[step],
            recv_sem=self.mate[1].at[step],
            device_id=(other(self.dp, 1), self.mp),
            device_id_type=MESH,
        )

    def start(self):
        self.keep_copy().start()
        for step in range(1, QUARTERS):
            self.near_copy(step).start()

    def spread(self):
        self.keep_copy().wait()
        for step in range(1, QUARTERS):
            self.near_copy(step).wait_recv()

        @pl.loop(1, self.half)
        def _(step):
            self.line_copy(step).start()

        self.mate_copy(0).start()

    def forward(self, low, high):
        @pl.loop(low, high)
        def _(step):
            self.line_copy(step).wait_recv()
            self.mate_copy(step).start()

    def finish(self):
        @pl.loop(0, self.half)
        def _(step):
            self.mate_copy(step).wait()

        @pl.loop(1, self.half)
        def _(step):
            self.line_copy(step).wait_send()

        for step in range(1, QUARTERS):
            self.near_copy(step).wait_send()


def text_kernel(
    x, image, image_mask, params, packed, gathered,
    text_out, in_grad, stack, vectors, plain, factors, rows_all,
    squares, entry, leave, load, images, image_sems, image_arrivals, row_sems, row_arrivals,
    own_rows, own_keep, factor_near, factor_near_in, factor_line, factor_line_in, factor_mate,
    factor_mate_in, factor_keep, normed, q, k, v, mixed, middle, normed_two, pre, sums, bias,
    stage, stage_sem, logits, value, near, far, column_send, column_receive,
):
    work, mixed_grad = in_grad, normed_two
    g1, s1, b_o, g2, s2, b_p = [params.at[pl.ds(i, 1)] for i in range(6)]
    b_q, b_v = packed.at[pl.ds(0, 1)], packed.at[pl.ds(1, 1)]
    own_count = image.shape[0]
    own_line = jnp.broadcast_to(params[pl.ds(6, 1), pl.ds(0, 128)], (own_count, 128))
    line_lane = lax.broadcasted_iota(jnp.int32, (own_count, 128), 1)
    line_row = lax.broadcasted_iota(jnp.int32, (own_count, 128), 0)

    def standing(shift):
        return jnp.sum(jnp.where(line_lane == line_row + shift, own_line, 0.0), axis=1, keepdims=True)

    own_text, own_pair = standing(0), standing(own_count)
    dp, mp = lax.axis_index("dp"), lax.axis_index("mp")
    dp_count, mp_count = far.shape[0], near.shape[0]
    rows_count = x.shape[0]
    part_rows = D // QUARTERS
    half = jnp.bfloat16

    def square_copy(i, m):
        return pltpu.make_async_copy(
            gathered.at[m, 2, pl.ds(i * part_rows, part_rows)],
            squares.at[i, pl.ds(m * part_rows, part_rows)],
            load.at[i, m],
        )

    def entry_copy(m):
        return pltpu.make_async_copy(gathered.at[m, 1], entry.at[m], load.at[4, m])

    def leave_copy(m):
        return pltpu.make_async_copy(gathered.at[m, 0], leave.at[m], load.at[5, m])

    for i in range(4):
        for m in range(QUARTERS):
            square_copy(i, m).start()
    for m in range(QUARTERS):
        entry_copy(m).start()
        leave_copy(m).start()
    images[dp, mp] = image[...].astype(half)
    greet(dp, mp, dp_count, mp_count)
    greeted(dp_count, mp_count)

    image_gather = Gather(images.at[dp, mp], images, (image_sems, image_arrivals))
    image_gather.start()
    row_gather = Gather(own_rows, rows_all, (row_sems, row_arrivals))
    factor_gather = FactorGather(
        sums,
        factors,
        (factor_near, factor_near_in),
        (factor_line, factor_line_in),
        (factor_mate, factor_mate_in),
        factor_keep,
    )

    def own_rows_copy():
        return pltpu.make_async_copy(own_rows, rows_all.at[dp, mp], own_keep)

    row = lax.broadcasted_iota(jnp.int32, (TEXT_WINDOW, TEXT_WINDOW), 0)
    column = lax.broadcasted_iota(jnp.int32, (TEXT_WINDOW, TEXT_WINDOW), 1)
    bias[...] = jnp.where((row // LEN == column // LEN) & (column <= row), 0.0, -1e30)
    first = lax.broadcasted_iota(jnp.int32, (TEXT_WINDOW, 128), 1) < HD

    unit, unused = hat(x[...].astype(jnp.float32))
    normed[...] = (unit * g1[...] + s1[...]).astype(half)
    for m in range(QUARTERS):
        square_copy(0, m).wait()
    q[...] = ((dot_nt(normed[...], squares[0]) + b_q[...]) * SCALE).astype(half)
    for m in range(QUARTERS):
        square_copy(1, m).wait()
    k[...] = dot_nt(normed[...], squares[1]).astype(half)
    for m in range(QUARTERS):
        square_copy(2, m).wait()
    v[...] = (dot_nt(normed[...], squares[2]) + b_v[...]).astype(half)

    def doubled(part):
        none = jnp.zeros_like(part)
        return jnp.concatenate([jnp.where(first, part, none), jnp.where(first, none, part)])

    def probabilities(both, keys):
        scores = dot_nt(both, keys) + jnp.concatenate([bias[...], bias[...]])
        weights = jnp.exp(scores - jnp.max(scores, axis=-1, keepdims=True))
        return weights * (1.0 / jnp.sum(weights, axis=-1, keepdims=True))

    def merge(heads):
        return jnp.where(first, heads[:TEXT_WINDOW], heads[TEXT_WINDOW:])

    @pl.loop(0, rows_count // TEXT_WINDOW)
    def _(w):
        rows = pl.ds(pl.multiple_of(w * TEXT_WINDOW, TEXT_WINDOW), TEXT_WINDOW)
        for h in range(HEADS // 2):
            lanes = pl.ds(128 * h, 128)
            probs = probabilities(doubled(q[rows, lanes]), k[rows, lanes]).astype(half)
            mixed[rows, lanes] = merge(dot(probs, v[rows, lanes])).astype(half)

    image_gather.forward(1, dp_count)
    for m in range(QUARTERS):
        square_copy(3, m).wait()
    middle[...] = x[...].astype(jnp.float32) + dot(mixed[...], squares[3]) + b_o[...]
    unit, unused = hat(middle[...])
    normed_two[...] = (unit * g2[...] + s2[...]).astype(half)
    owner = lax.broadcasted_iota(jnp.int32, (own_count, rows_count), 1) // LEN
    pool = jnp.where(owner == lax.broadcasted_iota(jnp.int32, (own_count, rows_count), 0), 1.0, 0.0)
    pool = pool.astype(half)
    work[...] = middle[...] + b_p[...]
    for m in range(QUARTERS):
        if m == 2:
            image_gather.forward_last()
        entry_copy(m).wait()
        leave_copy(m).wait()
        hidden = dot(normed_two[...], entry[m]) + packed[pl.ds(4 + m, 1), :]
        pre[m] = hidden
        active = gelu(hidden).astype(half)
        sums[m] = dot(pool, active).astype(half)
        work[...] += dot(active, leave[m])
    factor_gather.start()
    text_out[...] = work[...].astype(half)
    output = split(work[...])
    pooled = (dot(pool, output[:rows_count]) + dot(pool, output[rows_count:])) * (1.0 / LEN)

    image_gather.arrive()
    text_unit = normalize(pooled)
    everyone = image_mask.shape[1]
    width = LOSS_WIDTH
    multiplier = jnp.exp(params[pl.ds(7, 1), pl.ds(0, 1)])
    text_half = text_unit.astype(half)
    tiles = everyone // 128
    group_count = width // (mp_count * own_count)
    sections = [pl.ds(c * width, width) for c in range(everyone // width)]

    def images_of(c):
        return images[pl.ds(c * group_count, group_count)].reshape(width, D)

    def hits_of(c):
        place = lax.broadcasted_iota(jnp.int32, (own_count, width), 1) + c * width
        return jnp.where(place.astype(jnp.float32) == own_pair, 1.0, 0.0)

    row_total = text_hits = hit_logit = jnp.zeros((own_count, 1), jnp.float32)
    for c, lanes in enumerate(sections):
        logits[:, lanes] = dot_nt(text_half, images_of(c)) * multiplier
        hits = hits_of(c)
        weights = jnp.exp(logits[:, lanes])
        row_total += jnp.sum(weights * image_mask[:, lanes], axis=1, keepdims=True)
        text_hits += jnp.sum(hits * image_mask[:, lanes], axis=1, keepdims=True)
        hit_logit += jnp.sum(hits * logits[:, lanes], axis=1, keepdims=True)
        column_part = jnp.sum(weights * own_text, axis=0, keepdims=True)
        owner_part = jnp.sum(hits * own_text, axis=0, keepdims=True)
        for i in range(width // 128):
            piece = slice(128 * i, 128 * i + 128)
            value[pl.ds(c * width // 128 + i, 1), :] = column_part[:, piece]
            value[pl.ds(tiles + c * width // 128 + i, 1), :] = owner_part[:, piece]
    spread = Spread(value, near, far, column_send, column_receive)
    spread.start_near()
    safe_row = jnp.where(row_total > 0, row_total, 1.0)
    text_weight = own_text * text_hits
    total_part = total_of(0.5 * text_weight * jnp.log(safe_row) - text_weight * hit_logit)
    spread.wait_near()
    group = near[0]
    for i in range(1, mp_count):
        group = group + near[i]
    far[dp] = group
    spread.start_far()
    text_grad = jnp.zeros((own_count, D), jnp.float32)
    temp_part = column_loss = pairs = jnp.zeros((1, 1), jnp.float32)
    for c, lanes in enumerate(sections):
        row_weights = jnp.exp(logits[:, lanes]) * image_mask[:, lanes]
        row_grad = 0.5 * text_weight * (row_weights / safe_row - hits_of(c))
        temp_part += total_of(row_grad * logits[:, lanes])
        text_grad += dot((multiplier * row_grad).astype(half), images_of(c))
    spread.wait_far()
    spread.wait_near_sends()
    value[...] = far[0]

    @pl.loop(1, dp_count)
    def _(i):
        value[...] += far[i]

    def line_of(start):
        return jnp.concatenate([value[pl.ds(start + i, 1), :] for i in range(width // 128)], axis=1)

    for c, lanes in enumerate(sections):
        column_total = line_of(c * width // 128)
        image_weight = image_mask[:, lanes] * line_of(tiles + c * width // 128)
        safe_column = jnp.where(column_total > 0, column_total, 1.0)
        column_weights = jnp.exp(logits[:, lanes]) * own_text
        column_grad = 0.5 * image_weight * (column_weights / safe_column - hits_of(c))
        temp_part += total_of(column_grad * logits[:, lanes])
        column_loss += total_of(0.5 * image_weight * jnp.log(safe_column))
        pairs += total_of(image_weight)
        text_grad += dot((multiplier * column_grad).astype(half), images_of(c))
    lane = lax.broadcasted_iota(jnp.int32, (8, D), 1)
    plain[...] = jnp.where(lane == 0, column_loss, jnp.where(lane == 1, pairs, 0.0))
    vectors[pl.ds(8, 8), :] = jnp.where(lane == 0, total_part, jnp.where(lane == 1, temp_part, 0.0))

    inverse = lax.rsqrt(jnp.sum(pooled * pooled, axis=-1, keepdims=True) + 1e-06)
    caption_grad = (1.0 / LEN) * inverse * (
        text_grad - text_unit * jnp.sum(text_unit * text_grad, axis=-1, keepdims=True)
    )
    vectors[pl.ds(5, 1), :] = LEN * jnp.sum(caption_grad, axis=0, keepdims=True)
    spot = lax.broadcasted_iota(jnp.int32, (rows_count, own_count), 0) // LEN
    repeat = jnp.where(
        spot == lax.broadcasted_iota(jnp.int32, (rows_count, own_count), 1), 1.0, 0.0
    ).astype(half)
    caption_half = caption_grad.astype(half)
    own_rows[...] = caption_half
    factor_gather.spread()
    own_rows_copy().start()
    row_gather.start()
    grad_rows = dot(repeat, caption_half).astype(half)

    def stage_copies(piece):
        slot = piece % 3
        if piece < 4:
            return [
                pltpu.make_async_copy(
                    stage.at[slot],
                    stack.at[piece // 2, piece % 2, pl.ds(0, D)],
                    stage_sem.at[slot, 0],
                )
            ]
        place = D + (3, 0, 1, 2)[piece - 4] * part_rows
        return [
            pltpu.make_async_copy(
                stage.at[slot, pl.ds(m * part_rows, part_rows)],
                stack.at[m // 2, m % 2, pl.ds(place, part_rows)],
                stage_sem.at[slot, m],
            )
            for m in range(QUARTERS)
        ]

    def emit(piece, gradient):
        if piece >= 3:
            for copy in stage_copies(piece - 3):
                copy.wait()
        stage[piece % 3] = gradient.astype(half)
        for copy in stage_copies(piece):
            copy.start()

    work[...] = jnp.zeros_like(work)
    for m in range(QUARTERS):
        active_grad = dot_nt(grad_rows, leave[m])
        hidden_grad = active_grad * gelu_slope(pre[m])
        hidden_half = hidden_grad.astype(half)
        vectors[pl.ds(9 + m, 1), :] = jnp.sum(
            hidden_half.astype(jnp.float32), axis=0, keepdims=True
        )
        emit(m, dot_tn(normed_two[...], hidden_half))
        work[...] += dot_nt(hidden_half, entry[m])
    unit, inverse = hat(middle[...])
    grad = work[...]
    vectors[pl.ds(3, 1), :] = jnp.sum(grad * unit, axis=0, keepdims=True)
    vectors[pl.ds(4, 1), :] = jnp.sum(grad, axis=0, keepdims=True)
    caption_parts = split(caption_grad)
    token_grad = dot(repeat, caption_parts[:own_count]) + dot(repeat, caption_parts[own_count:])
    middle_grad = token_grad + hat_back(unit, inverse, grad * g2[...])
    middle[...] = middle_grad
    vectors[pl.ds(2, 1), :] = jnp.sum(middle_grad, axis=0, keepdims=True)
    attn_grad = middle_grad.astype(half)
    factor_gather.forward(1, (dp_count // 2 + 1) // 2)
    emit(4, dot_tn(mixed[...], attn_grad))
    mixed_grad[...] = dot_nt(attn_grad, squares[3]).astype(half)

    @pl.loop(0, rows_count // TEXT_WINDOW)
    def _(w):
        rows = pl.ds(pl.multiple_of(w * TEXT_WINDOW, TEXT_WINDOW), TEXT_WINDOW)
        for h in range(HEADS // 2):
            lanes = pl.ds(128 * h, 128)
            queries, keys, values = doubled(q[rows, lanes]), k[rows, lanes], v[rows, lanes]
            probs = probabilities(queries, keys)
            outer = doubled(mixed_grad[rows, lanes])
            probs_grad = dot_nt(outer, values)
            v[rows, lanes] = dot_tn(probs.astype(half), outer).astype(half)
            inner = jnp.sum(probs * probs_grad, axis=-1, keepdims=True)
            score_grad = (probs * (probs_grad - inner)).astype(half)
            q[rows, lanes] = (merge(dot(score_grad, keys)) * SCALE).astype(half)
            k[rows, lanes] = dot_tn(score_grad, queries).astype(half)

    factor_gather.forward((dp_count // 2 + 1) // 2, dp_count // 2)
    vectors[pl.ds(6, 1), :] = jnp.sum(q[...].astype(jnp.float32), axis=0, keepdims=True)
    vectors[pl.ds(7, 1), :] = jnp.sum(v[...].astype(jnp.float32), axis=0, keepdims=True)
    for i, part in enumerate([q, k, v]):
        emit(5 + i, dot_tn(part[...], normed[...]))
    row_gather.forward(1, dp_count)
    work[...] = (
        dot(q[...], squares[0]) + dot(k[...], squares[1]) + dot(v[...], squares[2])
    )
    unit, inverse = hat(x[...].astype(jnp.float32))
    grad = work[...]
    vectors[pl.ds(0, 1), :] = jnp.sum(grad * unit, axis=0, keepdims=True)
    vectors[pl.ds(1, 1), :] = jnp.sum(grad, axis=0, keepdims=True)
    in_grad[...] = middle[...] + hat_back(unit, inverse, grad * g1[...])

    row_gather.forward_last()
    for piece in range(5, 8):
        for copy in stage_copies(piece):
            copy.wait()
    spread.wait_far_sends()
    own_rows_copy().wait()
    factor_gather.finish()
    row_gather.arrive()
    row_gather.wait_sends()
    image_gather.wait_sends()


def text_layer(dp_count, mp_count, operands, gathered):
    half = jnp.bfloat16
    vmem, any_space = pl.BlockSpec(memory_space=pltpu.VMEM), pl.BlockSpec(memory_space=pl.ANY)
    rows_count, own_count = operands[0].shape[0], operands[1].shape[0]
    lines = 2 * dp_count * mp_count * own_count // 128
    rows = pltpu.VMEM((rows_count, D), half)
    wide = pltpu.VMEM((rows_count, D), jnp.float32)
    matrices = pltpu.VMEM((QUARTERS, D, D), half)
    kinds, few = pltpu.SemaphoreType.DMA((4, dp_count)), pltpu.SemaphoreType.DMA((QUARTERS,))
    line = pltpu.SemaphoreType.DMA((dp_count // 2,))
    everyone = jax.ShapeDtypeStruct((dp_count, mp_count, own_count, D), half)
    column = pltpu.SemaphoreType.DMA((mp_count + dp_count,))
    return pl.pallas_call(
        text_kernel,
        out_shape=(
            jax.ShapeDtypeStruct((rows_count, D), half),
            jax.ShapeDtypeStruct((rows_count, D), jnp.float32),
            jax.ShapeDtypeStruct((2, 2, 2 * D, D), half),
            jax.ShapeDtypeStruct((16, D), jnp.float32),
            jax.ShapeDtypeStruct((8, D), jnp.float32),
            everyone,
            everyone,
        ),
        in_specs=[vmem] * len(operands) + [any_space],
        out_specs=(vmem, vmem, any_space, vmem, vmem, any_space, any_space),
        scratch_shapes=[
            matrices,
            matrices,
            matrices,
            pltpu.SemaphoreType.DMA((6, QUARTERS)),
            pltpu.VMEM((dp_count, mp_count, own_count, D), half),
            kinds,
            kinds,
            kinds,
            kinds,
            pltpu.VMEM((own_count, D), half),
            pltpu.SemaphoreType.DMA,
            few,
            few,
            line,
            line,
            line,
            line,
            pltpu.SemaphoreType.DMA,
        ]
        + [rows] * 5
        + [
            wide,
            rows,
            pltpu.VMEM((QUARTERS, rows_count, D), jnp.float32),
            pltpu.VMEM((QUARTERS, own_count, D), half),
        ]
        + [
            pltpu.VMEM((TEXT_WINDOW, TEXT_WINDOW), jnp.float32),
            pltpu.VMEM((3, D, D), half),
            pltpu.SemaphoreType.DMA((3, QUARTERS)),
            pltpu.VMEM((own_count, lines * 64), jnp.float32),
            pltpu.VMEM((lines, 128), jnp.float32),
            pltpu.VMEM((mp_count, lines, 128), jnp.float32),
            pltpu.VMEM((dp_count, lines, 128), jnp.float32),
            column,
            column,
        ],
        compiler_params=pltpu.CompilerParams(
            collective_id=2, has_side_effects=True, vmem_limit_bytes=67043328
        ),
        name="text_layer",
    )(*operands, gathered)


def body(
    sentence_entry_words,
    sentence_present_marks,
    picture_present_marks,
    matched_picture_positions,
    stored_picture_patches,
    log_logit_multiplier,
    leading_standardizer_stretch,
    leading_standardizer_shift,
    lookup_coefficients,
    lookup_offset,
    address_coefficients,
    content_coefficients,
    content_offset,
    mixer_exit_coefficients,
    mixer_exit_offset,
    trailing_standardizer_stretch,
    trailing_standardizer_shift,
    perceptron_entry_coefficients,
    perceptron_inner_offset,
    perceptron_exit_coefficients,
    perceptron_exit_offset,
    picture_lookup_coefficients,
    picture_address_coefficients,
    picture_content_coefficients,
    picture_mixer_exit,
    picture_perceptron_entry,
    picture_perceptron_exit,
):
    own_count = sentence_present_marks.shape[0]
    dp_count, mp_count = lax.axis_size("dp"), lax.axis_size("mp")
    rank = lax.axis_index("mp")
    squares = jnp.concatenate(
        [
            lookup_coefficients.T,
            address_coefficients.T,
            content_coefficients.T,
            mixer_exit_coefficients,
        ]
    )
    quarter = D // mp_count

    offset = lax.axis_index(("dp", "mp")) * own_count
    own_pair = lax.dynamic_slice_in_dim(matched_picture_positions, offset, own_count, 0)

    def placed(vector):
        size = vector.shape[0]
        place = jnp.arange(size * mp_count, dtype=jnp.int32) // size
        return jnp.where(place == rank, jnp.tile(vector, mp_count), 0.0)

    def padded(*parts):
        filled = sum(part.shape[0] for part in parts)
        return parts + (jnp.zeros((-filled % D,), jnp.float32),)

    small = jnp.concatenate(
        (
            leading_standardizer_stretch,
            leading_standardizer_shift,
            mixer_exit_offset,
            trailing_standardizer_stretch,
            trailing_standardizer_shift,
            perceptron_exit_offset,
        )
        + padded(sentence_present_marks.astype(jnp.float32), own_pair.astype(jnp.float32))
        + padded(log_logit_multiplier)
        + (placed(lookup_offset), placed(content_offset))
        + padded(placed(picture_present_marks.astype(jnp.float32)))
        + (perceptron_inner_offset, jnp.zeros((4 * D,), jnp.float32))
    ).reshape(16, D)
    image, gathered, packed, image_mask = image_layer(
        dp_count,
        mp_count,
        stored_picture_patches,
        (
            picture_lookup_coefficients,
            picture_address_coefficients,
            picture_content_coefficients,
            picture_mixer_exit,
            picture_perceptron_entry,
            picture_perceptron_exit,
        ),
        squares,
        perceptron_entry_coefficients,
        perceptron_exit_coefficients,
        small,
    )
    output, text_in_grad, stack, vectors, plain, factors, rows_all = text_layer(
        dp_count,
        mp_count,
        (sentence_entry_words, image, image_mask, small, packed),
        gathered,
    )
    w_proj_grad = dot_tn(factors.reshape(-1, D), rows_all.reshape(-1, D))
    own_grads, shared = gradient_sum(dp_count, stack, vectors)
    loss = jnp.reshape((shared[8, 0] + plain[0, 0]) / plain[0, 1], (1,))

    def rows_of(start, count):
        return own_grads[start : start + count].astype(jnp.float32)

    def own(vector):
        return lax.dynamic_slice_in_dim(vector, rank * quarter, quarter, 0)

    return (
        loss,
        output,
        text_in_grad,
        shared[8, 1:2],
        shared[0],
        shared[1],
        rows_of(D, quarter).T,
        own(shared[6]),
        rows_of(D + 1 * quarter, quarter).T,
        rows_of(D + 2 * quarter, quarter).T,
        own(shared[7]),
        rows_of(D + 3 * quarter, quarter),
        shared[2],
        shared[3],
        shared[4],
        rows_of(0, D),
        lax.dynamic_slice_in_dim(shared, 9 + rank, 1, 0)[0],
        w_proj_grad,
        shared[5],
    )


def solution(mesh):
    in_specs = (
        P(("dp", "mp"), None),
        P(("dp", "mp")),
        P(("dp", "mp")),
        P(),
        P(("dp", "mp"), None),
        P(),
        P(),
        P(),
        P(None, "mp"),
        P("mp"),
        P(None, "mp"),
        P(None, "mp"),
        P("mp"),
        P("mp", None),
        P(),
        P(),
        P(),
        P(None, "mp"),
        P("mp"),
        P("mp", None),
        P(),
        P(),
        P(),
        P(),
        P(),
        P(),
        P(),
    )
    out_specs = (
        P(),
        P(("dp", "mp"), None),
        P(("dp", "mp"), None),
        P(),
        P(),
        P(),
        P(None, "mp"),
        P("mp"),
        P(None, "mp"),
        P(None, "mp"),
        P("mp"),
        P("mp", None),
        P(),
        P(),
        P(),
        P(None, "mp"),
        P("mp"),
        P("mp", None),
        P(),
    )
    return jax.shard_map(body, mesh=mesh, in_specs=in_specs, out_specs=out_specs, check_vma=False)
```

```python
from functools import partial

import jax
import jax.numpy as jnp
from jax import lax
from jax.experimental import pallas as pl
from jax.experimental.pallas import tpu as pltpu
from jax.sharding import PartitionSpec as P

D = 768
HEADS = 12
HD = 64
LEN = 16
PATCHES = 50
SCALE = HD ** (-0.5)
BLOCK = 8 * PATCHES
WINDOW = 112
STEP = 96
QUARTERS = 4
TEXT_WINDOW = 128
LOSS_WIDTH = 1024


def normalize(pooled):
    return pooled * lax.rsqrt(jnp.sum(pooled * pooled, axis=-1, keepdims=True) + 1e-06)


def dot(left, right):
    return lax.dot_general(
        left, right, (((1,), (0,)), ((), ())), preferred_element_type=jnp.float32
    )


def dot_nt(left, right):
    return lax.dot_general(
        left, right, (((1,), (1,)), ((), ())), preferred_element_type=jnp.float32
    )


def dot_tn(left, right):
    return lax.dot_general(
        left, right, (((0,), (0,)), ((), ())), preferred_element_type=jnp.float32
    )


def centre(tensor):
    centred = tensor - jnp.mean(tensor, axis=-1, keepdims=True)
    return centred * lax.rsqrt(jnp.mean(centred * centred, axis=-1, keepdims=True) + 1e-06)


def gelu(v):
    return 0.5 * v * (1.0 + jnp.tanh(0.7978845608028654 * (v + 0.044715 * v * v * v)))


MESH = pl.DeviceIdType.MESH
ROWS = 64
LAG = 2


def bit_of(value, bit):
    return lax.rem(lax.div(value, bit), 2)


def peer(axis, bit):
    dp, mp = lax.axis_index("dp"), lax.axis_index("mp")
    if axis == "dp":
        return (dp + bit - 2 * bit * bit_of(dp, bit), mp)
    return (dp, mp + bit - 2 * bit * bit_of(mp, bit))


def doubling_bits(dp_count):
    bits, bit = [], 1
    while bit < dp_count:
        bits.append(("dp", bit))
        bit *= 2
    return bits


def gradient_sum_kernel(dp_count, stack, small, out, small_out, keep, first, second, *rest):
    dp_bits = doubling_bits(dp_count)
    levels = len(dp_bits)
    parts, (whole, small_in, small_sum, send, receive, load, store, small_send, small_receive) = (
        rest[:levels],
        rest[levels:],
    )
    bits = [("mp", 1), ("mp", 2)] + dp_bits
    peers = [peer(*b) for b in bits]
    low, high = bit_of(lax.axis_index("mp"), 1), bit_of(lax.axis_index("mp"), 2)
    own = [bit_of(lax.axis_index("dp"), bit) for _, bit in dp_bits]
    chunks = stack.shape[2] // ROWS
    barrier = pltpu.get_barrier_semaphore()
    for p in peers:
        pl.semaphore_signal(barrier, inc=1, device_id=p, device_id_type=MESH)
    pl.semaphore_wait(barrier, len(peers))

    sizes = []
    size = ROWS
    for _ in dp_bits:
        halve = size >= 32
        size = size // 2 if halve else size
        sizes.append((size, halve))

    def add(target, other):
        target[...] = (target[...].astype(jnp.float32) + other[...].astype(jnp.float32)).astype(
            jnp.bfloat16
        )

    def rows(c):
        return pl.ds(pl.multiple_of(c * ROWS, ROWS), ROWS)

    def copy(stage, c):
        if stage == 0:
            source, target, who = stack.at[:, 1 - low, rows(c)], first.at[c], 0
        elif stage == 1:
            source, target, who = first.at[c, 1 - high], second.at[c], 1
        elif stage < 2 + levels:
            i = stage - 2
            n, halve = sizes[i]
            before = second if i == 0 else parts[i - 1]
            source = before.at[c, pl.ds((1 - own[i]) * n, n)] if halve else before.at[c]
            target, who = parts[i].at[c], stage
        else:
            i = gathers[stage - 2 - levels]
            n = sizes[i][0]
            where = sum(
                own[j] * sizes[j][0] for j in range(i + 1) if sizes[j][1]
            )
            source = target = whole.at[c, pl.ds(where, n)]
            who = 2 + i
        return pltpu.make_async_remote_copy(
            src_ref=source,
            dst_ref=target,
            send_sem=send.at[stage, c],
            recv_sem=receive.at[stage, c],
            device_id=peers[who],
            device_id_type=MESH,
        )

    gathers = [i for i in reversed(range(levels)) if sizes[i][1]]
    stages = 2 + levels + len(gathers)

    def load_copy(c):
        return pltpu.make_async_copy(stack.at[:, low, rows(c)], keep.at[c], load.at[c])

    def store_copy(c):
        return pltpu.make_async_copy(whole.at[c], out.at[rows(c)], store.at[c])

    def finish(stage, c):
        copy(stage, c).wait_recv()
        if stage == 0:
            load_copy(c).wait()
            add(first.at[c], keep.at[c])
        elif stage == 1:
            add(second.at[c], first.at[c, high])
        elif stage < 2 + levels:
            i = stage - 2
            n, halve = sizes[i]
            before = second if i == 0 else parts[i - 1]
            source = before.at[c, pl.ds(pl.multiple_of(own[i] * n, n), n)] if halve else before.at[c]
            if i < levels - 1:
                add(parts[i].at[c], source)
            else:
                where = sum(own[j] * sizes[j][0] for j in range(levels) if sizes[j][1])
                whole.at[c, pl.ds(pl.multiple_of(where, n), n)][...] = (
                    parts[i].at[c][...].astype(jnp.float32) + source[...].astype(jnp.float32)
                ).astype(jnp.bfloat16)

    def small_copy(i):
        return pltpu.make_async_remote_copy(
            src_ref=small if i == 0 else small_sum.at[i - 1],
            dst_ref=small_in.at[i],
            send_sem=small_send.at[i],
            recv_sem=small_receive.at[i],
            device_id=peers[i],
            device_id_type=MESH,
        )

    small_copy(0).start()

    @pl.loop(0, chunks + LAG * stages)
    def _(t):
        for slot in range(stages + 1):
            c = t - LAG * slot

            @pl.when((c >= 0) & (c < chunks))
            def _():
                if slot == 0:
                    load_copy(c).start()
                else:
                    finish(slot - 1, c)
                if slot < stages:
                    copy(slot, c).start()
                else:
                    store_copy(c).start()

        for i in range(len(bits)):

            @pl.when(t == 2 * i + 1)
            def _():
                small_copy(i).wait_recv()
                total = (small if i == 0 else small_sum.at[i - 1])[...] + small_in[i]
                if i < len(bits) - 1:
                    small_sum[i] = total
                    small_copy(i + 1).start()
                else:
                    small_out[...] = total

    for i in range(len(bits)):
        small_copy(i).wait_send()

    @pl.loop(0, chunks)
    def _(c):
        for stage in range(stages):
            copy(stage, c).wait_send()
        store_copy(c).wait()


def gradient_sum(dp_count, stack, small):
    levels = len(doubling_bits(dp_count))
    chunks = stack.shape[2] // ROWS
    sizes, size, halvings = [], ROWS, 0
    for _ in range(levels):
        halvings += size >= 32
        size = size // 2 if size >= 32 else size
        sizes.append(size)
    stages = 2 + levels + halvings
    half = jnp.bfloat16
    return pl.pallas_call(
        partial(gradient_sum_kernel, dp_count),
        out_shape=(
            jax.ShapeDtypeStruct(stack.shape[2:], half),
            jax.ShapeDtypeStruct(small.shape, jnp.float32),
        ),
        in_specs=[pl.BlockSpec(memory_space=pl.ANY), pl.BlockSpec(memory_space=pltpu.VMEM)],
        out_specs=(pl.BlockSpec(memory_space=pl.ANY), pl.BlockSpec(memory_space=pltpu.VMEM)),
        scratch_shapes=[
            pltpu.VMEM((chunks, 2, ROWS, D), half),
            pltpu.VMEM((chunks, 2, ROWS, D), half),
            pltpu.VMEM((chunks, ROWS, D), half),
        ]
        + [pltpu.VMEM((chunks, n, D), half) for n in sizes]
        + [
            pltpu.VMEM((chunks, ROWS, D), half),
            pltpu.VMEM((levels + 2,) + small.shape, jnp.float32),
            pltpu.VMEM((levels + 1,) + small.shape, jnp.float32),
            pltpu.SemaphoreType.DMA((stages, chunks)),
            pltpu.SemaphoreType.DMA((stages, chunks)),
            pltpu.SemaphoreType.DMA((chunks,)),
            pltpu.SemaphoreType.DMA((chunks,)),
            pltpu.SemaphoreType.DMA((levels + 2,)),
            pltpu.SemaphoreType.DMA((levels + 2,)),
        ],
        compiler_params=pltpu.CompilerParams(
            collective_id=1, has_side_effects=True, vmem_limit_bytes=56 * 2**20
        ),
        name="gradient_sum",
    )(stack, small)


def other(mp, bit):
    return mp + bit - 2 * bit * bit_of(mp, bit)


def greet(dp, mp, dp_count, mp_count):
    barrier = pltpu.get_barrier_semaphore()
    for step in range(1, mp_count):
        pl.semaphore_signal(
            barrier, inc=1, device_id=(dp, lax.rem(mp + step, mp_count)), device_id_type=MESH
        )

    @pl.loop(1, dp_count)
    def _(step):
        pl.semaphore_signal(
            barrier, inc=1, device_id=(lax.rem(dp + step, dp_count), mp), device_id_type=MESH
        )


def greeted(dp_count, mp_count):
    pl.semaphore_wait(pltpu.get_barrier_semaphore(), mp_count + dp_count - 2)


class Spread:
    def __init__(self, value, near, far, send, receive):
        self.dp, self.mp = lax.axis_index("dp"), lax.axis_index("mp")
        self.dp_count, self.mp_count = far.shape[0], near.shape[0]
        self.value, self.near, self.far = value, near, far
        self.send, self.receive = send, receive

    def near_copy(self, step, sender):
        return pltpu.make_async_remote_copy(
            src_ref=self.value,
            dst_ref=self.near.at[sender],
            send_sem=self.send.at[step],
            recv_sem=self.receive.at[step],
            device_id=(self.dp, lax.rem(self.mp + step, self.mp_count)),
            device_id_type=MESH,
        )

    def far_copy(self, step, sender):
        return pltpu.make_async_remote_copy(
            src_ref=self.far.at[self.dp],
            dst_ref=self.far.at[sender],
            send_sem=self.send.at[self.mp_count + step],
            recv_sem=self.receive.at[self.mp_count + step],
            device_id=(lax.rem(self.dp + step, self.dp_count), self.mp),
            device_id_type=MESH,
        )

    def start_near(self):
        for step in range(1, self.mp_count):
            self.near_copy(step, self.mp).start()
        self.near[self.mp] = self.value[...]

    def wait_near(self):
        for step in range(1, self.mp_count):
            self.near_copy(step, lax.rem(self.mp + self.mp_count - step, self.mp_count)).wait_recv()

    def start_far(self):
        @pl.loop(1, self.dp_count)
        def _(step):
            self.far_copy(step, self.dp).start()

    def wait_far(self):
        @pl.loop(1, self.dp_count)
        def _(step):
            self.far_copy(
                step, lax.rem(self.dp + self.dp_count - step, self.dp_count)
            ).wait_recv()

    def wait_near_sends(self):
        for step in range(1, self.mp_count):
            self.near_copy(step, self.mp).wait_send()

    def wait_far_sends(self):
        @pl.loop(1, self.dp_count)
        def _(step):
            self.far_copy(step, self.dp).wait_send()


PIECE = 96
PIECES = 6


def image_kernel(
    x, wq, wk, wv, wo, we, wx, squares, entry, leave, small,
    out, gathered, packed, mask,
    bq, bk, bv, bo, be, bx, load, normed, q, k, v, mixed, middle, bias,
    own, own_load, own_store, send, receive, near, far, small_send, small_receive,
):
    step = pl.program_id(0)
    last = pl.num_programs(0) - 1
    dp, mp = lax.axis_index("dp"), lax.axis_index("mp")
    y_bit, z_bit = bit_of(dp, 1), bit_of(dp, 2)
    across, beside = (dp, other(mp, 2)), (dp, other(mp, 1))
    along, behind = (other(dp, 1), mp), (other(dp, 2), mp)
    pairs = [(wq, bq), (wk, bk), (wv, bv), (wo, bo), (we, be), (wx, bx)]
    spread = Spread(small.at[pl.ds(8, 8)], near, far, small_send, small_receive)

    def load_copy(i):
        return pltpu.make_async_copy(pairs[i][0], pairs[i][1], load.at[i])

    def own_copy(i):
        return pltpu.make_async_copy((leave, entry, squares)[i], own.at[i], own_load.at[i])

    def keep_copy():
        return pltpu.make_async_copy(own, gathered.at[mp], own_store)

    def travel(kind, c):
        if kind == 9:
            source, target, who = own.at[c], gathered.at[mp, c], beside
        else:
            quarter = (y_bit if kind in (0, 1, 2, 3, 6, 7) else 1 - y_bit) + 2 * (
                z_bit if kind in (0, 1, 2, 3, 4, 5) else 1 - z_bit
            )
            matrix = lax.div(c, PIECES // 3)
            start = lax.rem(c, PIECES // 3) * PIECE + quarter * (D // 4)
            rows = pl.ds(pl.multiple_of(start, PIECE), PIECE)
            if kind == 0:
                source, target = own.at[matrix, rows], gathered.at[mp, matrix, rows]
            else:
                source = target = gathered.at[other(mp, 2), matrix, rows]
            who = (across, along, behind, beside, beside, behind, beside, along, beside)[kind]
        return pltpu.make_async_remote_copy(
            src_ref=source,
            dst_ref=target,
            send_sem=send.at[kind, c],
            recv_sem=receive.at[kind, c],
            device_id=who,
            device_id_type=MESH,
        )

    def early_or_late(c, early, late):
        @pl.when(c < PIECES // 2)
        def _():
            early()

        @pl.when(c >= PIECES // 2)
        def _():
            late()

    def forward_first(c):
        travel(0, c).wait_recv()
        for kind in (1, 2, 3):
            travel(kind, c).start()

    def forward_second(c):
        travel(1, c).wait_recv()
        travel(4, c).start()
        travel(2, c).wait_recv()
        travel(6, c).start()
        early_or_late(c, travel(5, c).start, travel(7, c).start)

    def forward_third(c):
        early_or_late(c, travel(5, c).wait_recv, travel(7, c).wait_recv)
        travel(8, c).start()

    def pump(j):
        n = step * 4 + j

        for lag, forward in ((3, forward_first), (6, forward_second), (10, forward_third)):

            @pl.when((n >= lag) & (n < lag + PIECES))
            def _():
                forward(n - lag)

    @pl.when(step == 0)
    def _():
        for i in range(3):
            own_copy(i).start()
        for i in range(6):
            load_copy(i).start()
        greet(dp, mp, far.shape[0], near.shape[0])
        for p in range(4):
            row = lax.broadcasted_iota(jnp.int32, (WINDOW, WINDOW), 0) + STEP * p
            column = lax.broadcasted_iota(jnp.int32, (WINDOW, WINDOW), 1) + STEP * p
            bias[p] = jnp.where(row // PATCHES == column // PATCHES, 0.0, -1e30)

    def ready(i):
        @pl.when(step == 0)
        def _():
            load_copy(i).wait()

    z = x[...].astype(jnp.float32)
    normed[...] = centre(z).astype(jnp.bfloat16)
    ready(0)
    q[...] = (dot(normed[...], bq[...]) * SCALE).astype(jnp.bfloat16)

    @pl.when(step == 0)
    def _():
        greeted(far.shape[0], near.shape[0])
        spread.start_near()
        for i in range(3):
            own_copy(i).wait()

        @pl.loop(0, PIECES)
        def _(c):
            travel(0, c).start()

        for i in range(3):
            travel(9, i).start()
        keep_copy().start()

    ready(1)
    k[...] = dot(normed[...], bk[...]).astype(jnp.bfloat16)
    ready(2)
    v[...] = dot(normed[...], bv[...]).astype(jnp.bfloat16)
    pump(0)
    first = lax.broadcasted_iota(jnp.int32, (WINDOW, 128), 1) < HD

    @pl.when(step == 1)
    def _():
        spread.wait_near()
        group = near[0] + near[1]
        for m in range(2, near.shape[0]):
            group = group + near[m]
        packed[pl.ds(0, 4), :] = group[:4]
        for m in range(QUARTERS):
            packed[pl.ds(4 + m, 1), :] = near[m, pl.ds(3, 1), :]
        far[dp] = jnp.broadcast_to(group[2:3, :128], (8, 128))
        spread.start_far()

    for p in range(4):
        if p == 2:
            pump(1)
        rows = pl.ds(STEP * p, WINDOW)
        for h in range(HEADS // 2):
            lanes = pl.ds(128 * h, 128)
            part = q[rows, lanes]
            none = jnp.zeros_like(part)
            both = jnp.concatenate([jnp.where(first, part, none), jnp.where(first, none, part)])
            scores = dot_nt(both, k[rows, lanes])
            scores = scores + jnp.concatenate([bias[p], bias[p]])
            weights = jnp.exp(scores - jnp.max(scores, axis=-1, keepdims=True))
            probs = (weights * (1.0 / jnp.sum(weights, axis=-1, keepdims=True))).astype(jnp.bfloat16)
            heads = dot(probs, v[rows, lanes])
            merged = jnp.where(first, heads[:WINDOW], heads[WINDOW:]).astype(jnp.bfloat16)
            if p:
                edge = pl.ds(STEP * p, 16)
                late = lax.broadcasted_iota(jnp.int32, (16, 128), 0) >= 2 * PATCHES * p - STEP * p
                mixed[edge, lanes] = jnp.where(late, merged[:16], mixed[edge, lanes])
                mixed[pl.ds(STEP * p + 16, WINDOW - 16), lanes] = merged[16:]
            else:
                mixed[rows, lanes] = merged
    pump(2)
    ready(3)
    middle[...] = x[...].astype(jnp.float32) + dot(mixed[...], bo[...])
    normed[...] = centre(middle[...]).astype(jnp.bfloat16)
    ready(4)
    ready(5)
    for c in range(4):
        if c == 2:
            pump(3)
        part = pl.ds(c * D, D)
        active = gelu(dot(normed[...], be[:, part])).astype(jnp.bfloat16)
        middle[...] += dot(active, bx[part, :])

    total = middle[...]
    high = total.astype(jnp.bfloat16)
    low = (total - high.astype(jnp.float32)).astype(jnp.bfloat16)
    owner = lax.broadcasted_iota(jnp.int32, (8, BLOCK), 1) // PATCHES
    pool = jnp.where(owner == lax.broadcasted_iota(jnp.int32, (8, BLOCK), 0), 1.0, 0.0)
    pool = pool.astype(jnp.bfloat16)
    pooled = (dot(pool, high) + dot(pool, low)) * (1.0 / PATCHES)
    out[...] = normalize(pooled)

    @pl.when(step == last)
    def _():
        spread.wait_far()
        for d in range(far.shape[0]):
            mask[:, pl.ds(128 * d, 128)] = far[d, pl.ds(0, 1), :]
        spread.wait_near_sends()
        spread.wait_far_sends()
        keep_copy().wait()
        for i in range(3):
            travel(9, i).wait()

        @pl.loop(0, PIECES)
        def _(c):
            for kind in (3, 4, 6, 8):
                travel(kind, c).wait_recv()
            for kind in (0, 1, 2, 3, 4, 6, 8):
                travel(kind, c).wait_send()
            early_or_late(c, travel(5, c).wait_send, travel(7, c).wait_send)


def image_layer(dp_count, mp_count, tokens, frozen, squares, entry, leave, small):
    half = jnp.bfloat16
    any_space = pl.BlockSpec(memory_space=pl.ANY)
    blocks = tokens.shape[0] // BLOCK
    square = pltpu.VMEM((D, D), half)
    rows = pltpu.VMEM((BLOCK, D), half)
    kinds = pltpu.SemaphoreType.DMA((10, PIECES))
    return pl.pallas_call(
        image_kernel,
        grid=(blocks,),
        out_shape=(
            jax.ShapeDtypeStruct((blocks * 8, D), jnp.float32),
            jax.ShapeDtypeStruct((mp_count, 3, D, D), half),
            jax.ShapeDtypeStruct((8, D), jnp.float32),
            jax.ShapeDtypeStruct((1, dp_count * 128), jnp.float32),
        ),
        in_specs=[pl.BlockSpec((BLOCK, D), lambda i: (i, 0))]
        + [any_space] * 9
        + [pl.BlockSpec(memory_space=pltpu.VMEM)],
        out_specs=(
            pl.BlockSpec((8, D), lambda i: (i, 0)),
            any_space,
            pl.BlockSpec(memory_space=pltpu.VMEM),
            pl.BlockSpec(memory_space=pltpu.VMEM),
        ),
        scratch_shapes=[square] * 4
        + [
            pltpu.VMEM((D, 4 * D), half),
            pltpu.VMEM((4 * D, D), half),
            pltpu.SemaphoreType.DMA((6,)),
        ]
        + [rows] * 5
        + [
            pltpu.VMEM((BLOCK, D), jnp.float32),
            pltpu.VMEM((4, WINDOW, WINDOW), jnp.float32),
            pltpu.VMEM((3, D, D), half),
            pltpu.SemaphoreType.DMA((3,)),
            pltpu.SemaphoreType.DMA,
            kinds,
            kinds,
            pltpu.VMEM((mp_count, 8, D), jnp.float32),
            pltpu.VMEM((dp_count, 8, 128), jnp.float32),
            pltpu.SemaphoreType.DMA((mp_count + dp_count,)),
            pltpu.SemaphoreType.DMA((mp_count + dp_count,)),
        ],
        compiler_params=pltpu.CompilerParams(
            collective_id=3, has_side_effects=True, vmem_limit_bytes=56 * 2**20
        ),
        name="image_layer",
    )(tokens, *frozen, squares, entry, leave, small)


def gelu_slope(v):
    bend = jnp.tanh(0.7978845608028654 * (v + 0.044715 * v * v * v))
    inner = 0.7978845608028654 * (1.0 + 0.134145 * v * v)
    return 0.5 * (1.0 + bend) + 0.5 * v * (1.0 - bend * bend) * inner


def hat(tensor):
    centred = tensor - jnp.mean(tensor, axis=-1, keepdims=True)
    inverse = lax.rsqrt(jnp.mean(centred * centred, axis=-1, keepdims=True) + 1e-06)
    return centred * inverse, inverse


def hat_back(unit, inverse, grad):
    mean = jnp.mean(grad, axis=-1, keepdims=True)
    return inverse * (grad - mean - unit * jnp.mean(grad * unit, axis=-1, keepdims=True))


def split(v):
    high = v.astype(jnp.bfloat16)
    return jnp.concatenate([high, (v - high.astype(jnp.float32)).astype(jnp.bfloat16)])


def total_of(v):
    return jnp.sum(jnp.sum(v, axis=1, keepdims=True), axis=0, keepdims=True)


class Gather:
    def __init__(self, own, blocks, sems):
        self.dp, self.mp = lax.axis_index("dp"), lax.axis_index("mp")
        self.own, self.blocks, self.count = own, blocks, blocks.shape[0]
        self.sems = sems

    def copy(self, kind, step):
        who = lax.rem(self.dp + self.count - step, self.count)
        lane = other(self.mp, 2) if kind == 3 else self.mp
        target = (self.dp, other(self.mp, 2 if kind == 1 else 1))
        if kind == 0:
            who, target = self.dp, (lax.rem(self.dp + step, self.count), self.mp)
        home = kind == 0 or (kind < 3 and isinstance(step, int) and step == 0)
        block = self.blocks.at[who, lane]
        return pltpu.make_async_remote_copy(
            src_ref=self.own if home else block,
            dst_ref=block,
            send_sem=self.sems[0].at[kind, step],
            recv_sem=self.sems[1].at[kind, step],
            device_id=target,
            device_id_type=MESH,
        )

    def start(self):
        @pl.loop(1, self.count)
        def _(step):
            self.copy(0, step).start()

        self.copy(1, 0).start()
        self.copy(2, 0).start()

    def forward(self, low, high):
        @pl.loop(low, high)
        def _(step):
            self.copy(0, step).wait_recv()
            self.copy(1, step).start()
            self.copy(2, step).start()

    def forward_last(self):
        @pl.loop(0, self.count)
        def _(step):
            self.copy(1, step).wait_recv()
            self.copy(3, step).start()

    def arrive(self):
        @pl.loop(0, self.count)
        def _(step):
            self.copy(2, step).wait_recv()
            self.copy(3, step).wait_recv()

    def wait_sends(self):
        @pl.loop(1, self.count)
        def _(step):
            self.copy(0, step).wait_send()

        @pl.loop(0, self.count)
        def _(step):
            for kind in (1, 2, 3):
                self.copy(kind, step).wait_send()


class FactorGather:
    def __init__(self, sums, blocks, near, line, mate, keep):
        self.dp, self.mp = lax.axis_index("dp"), lax.axis_index("mp")
        self.sums, self.blocks = sums, blocks
        self.near, self.line, self.mate, self.keep = near, line, mate, keep
        self.count, self.half = blocks.shape[0], blocks.shape[0] // 2

    def near_copy(self, step):
        to = lax.rem(self.mp + step, QUARTERS)
        return pltpu.make_async_remote_copy(
            src_ref=self.sums.at[to],
            dst_ref=self.blocks.at[self.dp, self.mp],
            send_sem=self.near[0].at[step],
            recv_sem=self.near[1].at[step],
            device_id=(self.dp, to),
            device_id_type=MESH,
        )

    def keep_copy(self):
        return pltpu.make_async_copy(
            self.sums.at[self.mp], self.blocks.at[self.dp, self.mp], self.keep
        )

    def line_copy(self, step):
        return pltpu.make_async_remote_copy(
            src_ref=self.blocks.at[self.dp],
            dst_ref=self.blocks.at[self.dp],
            send_sem=self.line[0].at[step],
            recv_sem=self.line[1].at[step],
            device_id=(lax.rem(self.dp + 2 * step, self.count), self.mp),
            device_id_type=MESH,
        )

    def mate_copy(self, step):
        block = self.blocks.at[lax.rem(self.dp + self.count - 2 * step, self.count)]
        return pltpu.make_async_remote_copy(
            src_ref=block,
            dst_ref=block,
            send_sem=self.mate[0].at[step],
            recv_sem=self.mate[1].at[step],
            device_id=(other(self.dp, 1), self.mp),
            device_id_type=MESH,
        )

    def start(self):
        self.keep_copy().start()
        for step in range(1, QUARTERS):
            self.near_copy(step).start()

    def spread(self):
        self.keep_copy().wait()
        for step in range(1, QUARTERS):
            self.near_copy(step).wait_recv()

        @pl.loop(1, self.half)
        def _(step):
            self.line_copy(step).start()

        self.mate_copy(0).start()

    def forward(self, low, high):
        @pl.loop(low, high)
        def _(step):
            self.line_copy(step).wait_recv()
            self.mate_copy(step).start()

    def finish(self):
        @pl.loop(0, self.half)
        def _(step):
            self.mate_copy(step).wait()

        @pl.loop(1, self.half)
        def _(step):
            self.line_copy(step).wait_send()

        for step in range(1, QUARTERS):
            self.near_copy(step).wait_send()


def text_kernel(
    x, image, image_mask, params, packed, gathered,
    text_out, in_grad, stack, vectors, plain, factors, rows_all,
    squares, entry, leave, load, images, image_sems, image_arrivals, row_sems, row_arrivals,
    own_rows, own_keep, factor_near, factor_near_in, factor_line, factor_line_in, factor_mate,
    factor_mate_in, factor_keep, normed, q, k, v, mixed, middle, normed_two, pre, sums, bias,
    stage, stage_sem, logits, value, near, far, column_send, column_receive,
):
    work, mixed_grad = in_grad, normed_two
    g1, s1, b_o, g2, s2, b_p = [params.at[pl.ds(i, 1)] for i in range(6)]
    b_q, b_v = packed.at[pl.ds(0, 1)], packed.at[pl.ds(1, 1)]
    own_count = image.shape[0]
    own_line = jnp.broadcast_to(params[pl.ds(6, 1), pl.ds(0, 128)], (own_count, 128))
    line_lane = lax.broadcasted_iota(jnp.int32, (own_count, 128), 1)
    line_row = lax.broadcasted_iota(jnp.int32, (own_count, 128), 0)

    def standing(shift):
        return jnp.sum(jnp.where(line_lane == line_row + shift, own_line, 0.0), axis=1, keepdims=True)

    own_text, own_pair = standing(0), standing(own_count)
    dp, mp = lax.axis_index("dp"), lax.axis_index("mp")
    dp_count, mp_count = far.shape[0], near.shape[0]
    rows_count = x.shape[0]
    part_rows = D // QUARTERS
    half = jnp.bfloat16

    def square_copy(i, m):
        return pltpu.make_async_copy(
            gathered.at[m, 2, pl.ds(i * part_rows, part_rows)],
            squares.at[i, pl.ds(m * part_rows, part_rows)],
            load.at[i, m],
        )

    def entry_copy(m):
        return pltpu.make_async_copy(gathered.at[m, 1], entry.at[m], load.at[4, m])

    def leave_copy(m):
        return pltpu.make_async_copy(gathered.at[m, 0], leave.at[m], load.at[5, m])

    for i in range(4):
        for m in range(QUARTERS):
            square_copy(i, m).start()
    for m in range(QUARTERS):
        entry_copy(m).start()
        leave_copy(m).start()
    images[dp, mp] = image[...].astype(half)
    greet(dp, mp, dp_count, mp_count)
    greeted(dp_count, mp_count)

    image_gather = Gather(images.at[dp, mp], images, (image_sems, image_arrivals))
    image_gather.start()
    row_gather = Gather(own_rows, rows_all, (row_sems, row_arrivals))
    factor_gather = FactorGather(
        sums,
        factors,
        (factor_near, factor_near_in),
        (factor_line, factor_line_in),
        (factor_mate, factor_mate_in),
        factor_keep,
    )

    def own_rows_copy():
        return pltpu.make_async_copy(own_rows, rows_all.at[dp, mp], own_keep)

    row = lax.broadcasted_iota(jnp.int32, (TEXT_WINDOW, TEXT_WINDOW), 0)
    column = lax.broadcasted_iota(jnp.int32, (TEXT_WINDOW, TEXT_WINDOW), 1)
    bias[...] = jnp.where((row // LEN == column // LEN) & (column <= row), 0.0, -1e30)
    first = lax.broadcasted_iota(jnp.int32, (TEXT_WINDOW, 128), 1) < HD

    unit, unused = hat(x[...].astype(jnp.float32))
    normed[...] = (unit * g1[...] + s1[...]).astype(half)
    for m in range(QUARTERS):
        square_copy(0, m).wait()
    q[...] = ((dot_nt(normed[...], squares[0]) + b_q[...]) * SCALE).astype(half)
    for m in range(QUARTERS):
        square_copy(1, m).wait()
    k[...] = dot_nt(normed[...], squares[1]).astype(half)
    for m in range(QUARTERS):
        square_copy(2, m).wait()
    v[...] = (dot_nt(normed[...], squares[2]) + b_v[...]).astype(half)

    def doubled(part):
        none = jnp.zeros_like(part)
        return jnp.concatenate([jnp.where(first, part, none), jnp.where(first, none, part)])

    def probabilities(both, keys):
        scores = dot_nt(both, keys) + jnp.concatenate([bias[...], bias[...]])
        weights = jnp.exp(scores - jnp.max(scores, axis=-1, keepdims=True))
        return weights * (1.0 / jnp.sum(weights, axis=-1, keepdims=True))

    def merge(heads):
        return jnp.where(first, heads[:TEXT_WINDOW], heads[TEXT_WINDOW:])

    @pl.loop(0, rows_count // TEXT_WINDOW)
    def _(w):
        rows = pl.ds(pl.multiple_of(w * TEXT_WINDOW, TEXT_WINDOW), TEXT_WINDOW)
        for h in range(HEADS // 2):
            lanes = pl.ds(128 * h, 128)
            probs = probabilities(doubled(q[rows, lanes]), k[rows, lanes]).astype(half)
            mixed[rows, lanes] = merge(dot(probs, v[rows, lanes])).astype(half)

    image_gather.forward(1, dp_count)
    for m in range(QUARTERS):
        square_copy(3, m).wait()
    middle[...] = x[...].astype(jnp.float32) + dot(mixed[...], squares[3]) + b_o[...]
    unit, unused = hat(middle[...])
    normed_two[...] = (unit * g2[...] + s2[...]).astype(half)
    owner = lax.broadcasted_iota(jnp.int32, (own_count, rows_count), 1) // LEN
    pool = jnp.where(owner == lax.broadcasted_iota(jnp.int32, (own_count, rows_count), 0), 1.0, 0.0)
    pool = pool.astype(half)
    work[...] = middle[...] + b_p[...]

    @pl.loop(0, QUARTERS)
    def _(m):
        @pl.when(m == 2)
        def _():
            image_gather.forward_last()

        entry_copy(m).wait()
        leave_copy(m).wait()
        hidden = dot(normed_two[...], entry[m]) + packed[pl.ds(4 + m, 1), :]
        pre[m] = hidden
        active = gelu(hidden).astype(half)
        sums[m] = dot(pool, active).astype(half)
        work[...] += dot(active, leave[m])

    factor_gather.start()
    text_out[...] = work[...].astype(half)
    output = split(work[...])
    pooled = (dot(pool, output[:rows_count]) + dot(pool, output[rows_count:])) * (1.0 / LEN)

    image_gather.arrive()
    text_unit = normalize(pooled)
    everyone = image_mask.shape[1]
    width = LOSS_WIDTH
    multiplier = jnp.exp(params[pl.ds(7, 1), pl.ds(0, 1)])
    text_half = text_unit.astype(half)
    tiles = everyone // 128
    group_count = width // (mp_count * own_count)
    sections = [pl.ds(c * width, width) for c in range(everyone // width)]

    def images_of(c):
        return images[pl.ds(c * group_count, group_count)].reshape(width, D)

    def hits_of(c):
        place = lax.broadcasted_iota(jnp.int32, (own_count, width), 1) + c * width
        return jnp.where(place.astype(jnp.float32) == own_pair, 1.0, 0.0)

    row_total = text_hits = hit_logit = jnp.zeros((own_count, 1), jnp.float32)
    for c, lanes in enumerate(sections):
        logits[:, lanes] = dot_nt(text_half, images_of(c)) * multiplier
        hits = hits_of(c)
        weights = jnp.exp(logits[:, lanes])
        row_total += jnp.sum(weights * image_mask[:, lanes], axis=1, keepdims=True)
        text_hits += jnp.sum(hits * image_mask[:, lanes], axis=1, keepdims=True)
        hit_logit += jnp.sum(hits * logits[:, lanes], axis=1, keepdims=True)
        column_part = jnp.sum(weights * own_text, axis=0, keepdims=True)
        owner_part = jnp.sum(hits * own_text, axis=0, keepdims=True)
        for i in range(width // 128):
            piece = slice(128 * i, 128 * i + 128)
            value[pl.ds(c * width // 128 + i, 1), :] = column_part[:, piece]
            value[pl.ds(tiles + c * width // 128 + i, 1), :] = owner_part[:, piece]
    spread = Spread(value, near, far, column_send, column_receive)
    spread.start_near()
    safe_row = jnp.where(row_total > 0, row_total, 1.0)
    text_weight = own_text * text_hits
    total_part = total_of(0.5 * text_weight * jnp.log(safe_row) - text_weight * hit_logit)
    spread.wait_near()
    group = near[0]
    for i in range(1, mp_count):
        group = group + near[i]
    far[dp] = group
    spread.start_far()
    text_grad = jnp.zeros((own_count, D), jnp.float32)
    temp_part = column_loss = pairs = jnp.zeros((1, 1), jnp.float32)
    for c, lanes in enumerate(sections):
        row_weights = jnp.exp(logits[:, lanes]) * image_mask[:, lanes]
        row_grad = 0.5 * text_weight * (row_weights / safe_row - hits_of(c))
        temp_part += total_of(row_grad * logits[:, lanes])
        text_grad += dot((multiplier * row_grad).astype(half), images_of(c))
    spread.wait_far()
    spread.wait_near_sends()
    value[...] = far[0]

    @pl.loop(1, dp_count)
    def _(i):
        value[...] += far[i]

    def line_of(start):
        return jnp.concatenate([value[pl.ds(start + i, 1), :] for i in range(width // 128)], axis=1)

    for c, lanes in enumerate(sections):
        column_total = line_of(c * width // 128)
        image_weight = image_mask[:, lanes] * line_of(tiles + c * width // 128)
        safe_column = jnp.where(column_total > 0, column_total, 1.0)
        column_weights = jnp.exp(logits[:, lanes]) * own_text
        column_grad = 0.5 * image_weight * (column_weights / safe_column - hits_of(c))
        temp_part += total_of(column_grad * logits[:, lanes])
        column_loss += total_of(0.5 * image_weight * jnp.log(safe_column))
        pairs += total_of(image_weight)
        text_grad += dot((multiplier * column_grad).astype(half), images_of(c))
    lane = lax.broadcasted_iota(jnp.int32, (8, D), 1)
    plain[...] = jnp.where(lane == 0, column_loss, jnp.where(lane == 1, pairs, 0.0))
    vectors[pl.ds(8, 8), :] = jnp.where(lane == 0, total_part, jnp.where(lane == 1, temp_part, 0.0))

    inverse = lax.rsqrt(jnp.sum(pooled * pooled, axis=-1, keepdims=True) + 1e-06)
    caption_grad = (1.0 / LEN) * inverse * (
        text_grad - text_unit * jnp.sum(text_unit * text_grad, axis=-1, keepdims=True)
    )
    vectors[pl.ds(5, 1), :] = LEN * jnp.sum(caption_grad, axis=0, keepdims=True)
    spot = lax.broadcasted_iota(jnp.int32, (rows_count, own_count), 0) // LEN
    repeat = jnp.where(
        spot == lax.broadcasted_iota(jnp.int32, (rows_count, own_count), 1), 1.0, 0.0
    ).astype(half)
    caption_half = caption_grad.astype(half)
    own_rows[...] = caption_half
    factor_gather.spread()
    own_rows_copy().start()
    row_gather.start()
    grad_rows = dot(repeat, caption_half).astype(half)

    def stage_copies(piece):
        if not isinstance(piece, int) or piece < 4:
            slot = lax.rem(piece, 3)
            return [
                pltpu.make_async_copy(
                    stage.at[slot],
                    stack.at[lax.div(piece, 2), lax.rem(piece, 2), pl.ds(0, D)],
                    stage_sem.at[slot, 0],
                )
            ]
        slot = piece % 3
        place = D + (3, 0, 1, 2)[piece - 4] * part_rows
        return [
            pltpu.make_async_copy(
                stage.at[slot, pl.ds(m * part_rows, part_rows)],
                stack.at[m // 2, m % 2, pl.ds(place, part_rows)],
                stage_sem.at[slot, m],
            )
            for m in range(QUARTERS)
        ]

    def emit(piece, gradient):
        for copy in stage_copies(piece - 3):
            copy.wait()
        stage[piece % 3] = gradient.astype(half)
        for copy in stage_copies(piece):
            copy.start()

    work[...] = jnp.zeros_like(work)

    @pl.loop(0, QUARTERS)
    def _(m):
        active_grad = dot_nt(grad_rows, leave[m])
        hidden_grad = active_grad * gelu_slope(pre[m])
        hidden_half = hidden_grad.astype(half)
        vectors[pl.ds(9 + m, 1), :] = jnp.sum(
            hidden_half.astype(jnp.float32), axis=0, keepdims=True
        )

        @pl.when(m >= 3)
        def _():
            for copy in stage_copies(m - 3):
                copy.wait()

        stage[lax.rem(m, 3)] = dot_tn(normed_two[...], hidden_half).astype(half)
        for copy in stage_copies(m):
            copy.start()
        work[...] += dot_nt(hidden_half, entry[m])

    unit, inverse = hat(middle[...])
    grad = work[...]
    vectors[pl.ds(3, 1), :] = jnp.sum(grad * unit, axis=0, keepdims=True)
    vectors[pl.ds(4, 1), :] = jnp.sum(grad, axis=0, keepdims=True)
    caption_parts = split(caption_grad)
    token_grad = dot(repeat, caption_parts[:own_count]) + dot(repeat, caption_parts[own_count:])
    middle_grad = token_grad + hat_back(unit, inverse, grad * g2[...])
    middle[...] = middle_grad
    vectors[pl.ds(2, 1), :] = jnp.sum(middle_grad, axis=0, keepdims=True)
    attn_grad = middle_grad.astype(half)
    factor_gather.forward(1, (dp_count // 2 + 1) // 2)
    emit(4, dot_tn(mixed[...], attn_grad))
    mixed_grad[...] = dot_nt(attn_grad, squares[3]).astype(half)

    @pl.loop(0, rows_count // TEXT_WINDOW)
    def _(w):
        rows = pl.ds(pl.multiple_of(w * TEXT_WINDOW, TEXT_WINDOW), TEXT_WINDOW)
        for h in range(HEADS // 2):
            lanes = pl.ds(128 * h, 128)
            queries, keys, values = doubled(q[rows, lanes]), k[rows, lanes], v[rows, lanes]
            probs = probabilities(queries, keys)
            outer = doubled(mixed_grad[rows, lanes])
            probs_grad = dot_nt(outer, values)
            v[rows, lanes] = dot_tn(probs.astype(half), outer).astype(half)
            inner = jnp.sum(probs * probs_grad, axis=-1, keepdims=True)
            score_grad = (probs * (probs_grad - inner)).astype(half)
            q[rows, lanes] = (merge(dot(score_grad, keys)) * SCALE).astype(half)
            k[rows, lanes] = dot_tn(score_grad, queries).astype(half)

    factor_gather.forward((dp_count // 2 + 1) // 2, dp_count // 2)
    vectors[pl.ds(6, 1), :] = jnp.sum(q[...].astype(jnp.float32), axis=0, keepdims=True)
    vectors[pl.ds(7, 1), :] = jnp.sum(v[...].astype(jnp.float32), axis=0, keepdims=True)
    for i, part in enumerate([q, k, v]):
        emit(5 + i, dot_tn(part[...], normed[...]))
    row_gather.forward(1, dp_count)
    work[...] = (
        dot(q[...], squares[0]) + dot(k[...], squares[1]) + dot(v[...], squares[2])
    )
    unit, inverse = hat(x[...].astype(jnp.float32))
    grad = work[...]
    vectors[pl.ds(0, 1), :] = jnp.sum(grad * unit, axis=0, keepdims=True)
    vectors[pl.ds(1, 1), :] = jnp.sum(grad, axis=0, keepdims=True)
    in_grad[...] = middle[...] + hat_back(unit, inverse, grad * g1[...])

    row_gather.forward_last()
    for piece in range(5, 8):
        for copy in stage_copies(piece):
            copy.wait()
    spread.wait_far_sends()
    own_rows_copy().wait()
    factor_gather.finish()
    row_gather.arrive()
    row_gather.wait_sends()
    image_gather.wait_sends()


def text_layer(dp_count, mp_count, operands, gathered):
    half = jnp.bfloat16
    vmem, any_space = pl.BlockSpec(memory_space=pltpu.VMEM), pl.BlockSpec(memory_space=pl.ANY)
    rows_count, own_count = operands[0].shape[0], operands[1].shape[0]
    lines = 2 * dp_count * mp_count * own_count // 128
    rows = pltpu.VMEM((rows_count, D), half)
    wide = pltpu.VMEM((rows_count, D), jnp.float32)
    matrices = pltpu.VMEM((QUARTERS, D, D), half)
    kinds, few = pltpu.SemaphoreType.DMA((4, dp_count)), pltpu.SemaphoreType.DMA((QUARTERS,))
    line = pltpu.SemaphoreType.DMA((dp_count // 2,))
    everyone = jax.ShapeDtypeStruct((dp_count, mp_count, own_count, D), half)
    column = pltpu.SemaphoreType.DMA((mp_count + dp_count,))
    return pl.pallas_call(
        text_kernel,
        out_shape=(
            jax.ShapeDtypeStruct((rows_count, D), half),
            jax.ShapeDtypeStruct((rows_count, D), jnp.float32),
            jax.ShapeDtypeStruct((2, 2, 2 * D, D), half),
            jax.ShapeDtypeStruct((16, D), jnp.float32),
            jax.ShapeDtypeStruct((8, D), jnp.float32),
            everyone,
            everyone,
        ),
        in_specs=[vmem] * len(operands) + [any_space],
        out_specs=(vmem, vmem, any_space, vmem, vmem, any_space, any_space),
        scratch_shapes=[
            matrices,
            matrices,
            matrices,
            pltpu.SemaphoreType.DMA((6, QUARTERS)),
            pltpu.VMEM((dp_count, mp_count, own_count, D), half),
            kinds,
            kinds,
            kinds,
            kinds,
            pltpu.VMEM((own_count, D), half),
            pltpu.SemaphoreType.DMA,
            few,
            few,
            line,
            line,
            line,
            line,
            pltpu.SemaphoreType.DMA,
        ]
        + [rows] * 5
        + [
            wide,
            rows,
            pltpu.VMEM((QUARTERS, rows_count, D), jnp.float32),
            pltpu.VMEM((QUARTERS, own_count, D), half),
        ]
        + [
            pltpu.VMEM((TEXT_WINDOW, TEXT_WINDOW), jnp.float32),
            pltpu.VMEM((3, D, D), half),
            pltpu.SemaphoreType.DMA((3, QUARTERS)),
            pltpu.VMEM((own_count, lines * 64), jnp.float32),
            pltpu.VMEM((lines, 128), jnp.float32),
            pltpu.VMEM((mp_count, lines, 128), jnp.float32),
            pltpu.VMEM((dp_count, lines, 128), jnp.float32),
            column,
            column,
        ],
        compiler_params=pltpu.CompilerParams(
            collective_id=2, has_side_effects=True, vmem_limit_bytes=67043328
        ),
        name="text_layer",
    )(*operands, gathered)


def body(
    sentence_entry_words,
    sentence_present_marks,
    picture_present_marks,
    matched_picture_positions,
    stored_picture_patches,
    log_logit_multiplier,
    leading_standardizer_stretch,
    leading_standardizer_shift,
    lookup_coefficients,
    lookup_offset,
    address_coefficients,
    content_coefficients,
    content_offset,
    mixer_exit_coefficients,
    mixer_exit_offset,
    trailing_standardizer_stretch,
    trailing_standardizer_shift,
    perceptron_entry_coefficients,
    perceptron_inner_offset,
    perceptron_exit_coefficients,
    perceptron_exit_offset,
    picture_lookup_coefficients,
    picture_address_coefficients,
    picture_content_coefficients,
    picture_mixer_exit,
    picture_perceptron_entry,
    picture_perceptron_exit,
):
    own_count = sentence_present_marks.shape[0]
    dp_count, mp_count = lax.axis_size("dp"), lax.axis_size("mp")
    rank = lax.axis_index("mp")
    squares = jnp.concatenate(
        [
            lookup_coefficients.T,
            address_coefficients.T,
            content_coefficients.T,
            mixer_exit_coefficients,
        ]
    )
    quarter = D // mp_count

    offset = lax.axis_index(("dp", "mp")) * own_count
    own_pair = lax.dynamic_slice_in_dim(matched_picture_positions, offset, own_count, 0)

    def placed(vector):
        size = vector.shape[0]
        place = jnp.arange(size * mp_count, dtype=jnp.int32) // size
        return jnp.where(place == rank, jnp.tile(vector, mp_count), 0.0)

    def padded(*parts):
        filled = sum(part.shape[0] for part in parts)
        return parts + (jnp.zeros((-filled % D,), jnp.float32),)

    small = jnp.concatenate(
        (
            leading_standardizer_stretch,
            leading_standardizer_shift,
            mixer_exit_offset,
            trailing_standardizer_stretch,
            trailing_standardizer_shift,
            perceptron_exit_offset,
        )
        + padded(sentence_present_marks.astype(jnp.float32), own_pair.astype(jnp.float32))
        + padded(log_logit_multiplier)
        + (placed(lookup_offset), placed(content_offset))
        + padded(placed(picture_present_marks.astype(jnp.float32)))
        + (perceptron_inner_offset, jnp.zeros((4 * D,), jnp.float32))
    ).reshape(16, D)
    image, gathered, packed, image_mask = image_layer(
        dp_count,
        mp_count,
        stored_picture_patches,
        (
            picture_lookup_coefficients,
            picture_address_coefficients,
            picture_content_coefficients,
            picture_mixer_exit,
            picture_perceptron_entry,
            picture_perceptron_exit,
        ),
        squares,
        perceptron_entry_coefficients,
        perceptron_exit_coefficients,
        small,
    )
    output, text_in_grad, stack, vectors, plain, factors, rows_all = text_layer(
        dp_count,
        mp_count,
        (sentence_entry_words, image, image_mask, small, packed),
        gathered,
    )
    w_proj_grad = dot_tn(factors.reshape(-1, D), rows_all.reshape(-1, D))
    own_grads, shared = gradient_sum(dp_count, stack, vectors)
    loss = jnp.reshape((shared[8, 0] + plain[0, 0]) / plain[0, 1], (1,))

    def rows_of(start, count):
        return own_grads[start : start + count].astype(jnp.float32)

    def own(vector):
        return lax.dynamic_slice_in_dim(vector, rank * quarter, quarter, 0)

    return (
        loss,
        output,
        text_in_grad,
        shared[8, 1:2],
        shared[0],
        shared[1],
        rows_of(D, quarter).T,
        own(shared[6]),
        rows_of(D + 1 * quarter, quarter).T,
        rows_of(D + 2 * quarter, quarter).T,
        own(shared[7]),
        rows_of(D + 3 * quarter, quarter),
        shared[2],
        shared[3],
        shared[4],
        rows_of(0, D),
        lax.dynamic_slice_in_dim(shared, 9 + rank, 1, 0)[0],
        w_proj_grad,
        shared[5],
    )


def solution(mesh):
    in_specs = (
        P(("dp", "mp"), None),
        P(("dp", "mp")),
        P(("dp", "mp")),
        P(),
        P(("dp", "mp"), None),
        P(),
        P(),
        P(),
        P(None, "mp"),
        P("mp"),
        P(None, "mp"),
        P(None, "mp"),
        P("mp"),
        P("mp", None),
        P(),
        P(),
        P(),
        P(None, "mp"),
        P("mp"),
        P("mp", None),
        P(),
        P(),
        P(),
        P(),
        P(),
        P(),
        P(),
    )
    out_specs = (
        P(),
        P(("dp", "mp"), None),
        P(("dp", "mp"), None),
        P(),
        P(),
        P(),
        P(None, "mp"),
        P("mp"),
        P(None, "mp"),
        P(None, "mp"),
        P("mp"),
        P("mp", None),
        P(),
        P(),
        P(),
        P(None, "mp"),
        P("mp"),
        P("mp", None),
        P(),
    )
    return jax.shard_map(body, mesh=mesh, in_specs=in_specs, out_specs=out_specs, check_vma=False)
```

```python
from functools import partial

import jax
import jax.numpy as jnp
from jax import lax
from jax.experimental import pallas as pl
from jax.experimental.pallas import tpu as pltpu
from jax.sharding import PartitionSpec as P

D = 768
HEADS = 12
HD = 64
LEN = 16
PATCHES = 50
SCALE = HD ** (-0.5)
BLOCK = 8 * PATCHES
WINDOW = 112
STEP = 96
QUARTERS = 4
TEXT_WINDOW = 128
LOSS_WIDTH = 1024


def normalize(pooled):
    return pooled * lax.rsqrt(jnp.sum(pooled * pooled, axis=-1, keepdims=True) + 1e-06)


def dot(left, right):
    return lax.dot_general(
        left, right, (((1,), (0,)), ((), ())), preferred_element_type=jnp.float32
    )


def dot_nt(left, right):
    return lax.dot_general(
        left, right, (((1,), (1,)), ((), ())), preferred_element_type=jnp.float32
    )


def dot_tn(left, right):
    return lax.dot_general(
        left, right, (((0,), (0,)), ((), ())), preferred_element_type=jnp.float32
    )


def centre(tensor):
    centred = tensor - jnp.mean(tensor, axis=-1, keepdims=True)
    return centred * lax.rsqrt(jnp.mean(centred * centred, axis=-1, keepdims=True) + 1e-06)


def gelu(v):
    return 0.5 * v * (1.0 + jnp.tanh(0.7978845608028654 * (v + 0.044715 * v * v * v)))


MESH = pl.DeviceIdType.MESH
ROWS = 64
LAG = 2


def bit_of(value, bit):
    return lax.rem(lax.div(value, bit), 2)


def peer(axis, bit):
    dp, mp = lax.axis_index("dp"), lax.axis_index("mp")
    if axis == "dp":
        return (dp + bit - 2 * bit * bit_of(dp, bit), mp)
    return (dp, mp + bit - 2 * bit * bit_of(mp, bit))


def doubling_bits(dp_count):
    bits, bit = [], 1
    while bit < dp_count:
        bits.append(("dp", bit))
        bit *= 2
    return bits


def gradient_sum_kernel(dp_count, stack, small, out, small_out, keep, first, second, *rest):
    dp_bits = doubling_bits(dp_count)
    levels = len(dp_bits)
    parts, (whole, small_in, small_sum, send, receive, load, store, small_send, small_receive) = (
        rest[:levels],
        rest[levels:],
    )
    bits = [("mp", 1), ("mp", 2)] + dp_bits
    peers = [peer(*b) for b in bits]
    low, high = bit_of(lax.axis_index("mp"), 1), bit_of(lax.axis_index("mp"), 2)
    own = [bit_of(lax.axis_index("dp"), bit) for _, bit in dp_bits]
    chunks = stack.shape[2] // ROWS
    barrier = pltpu.get_barrier_semaphore()
    for p in peers:
        pl.semaphore_signal(barrier, inc=1, device_id=p, device_id_type=MESH)
    pl.semaphore_wait(barrier, len(peers))

    sizes = []
    size = ROWS
    for _ in dp_bits:
        halve = size >= 32
        size = size // 2 if halve else size
        sizes.append((size, halve))

    def add(target, other):
        target[...] = (target[...].astype(jnp.float32) + other[...].astype(jnp.float32)).astype(
            jnp.bfloat16
        )

    def rows(c):
        return pl.ds(pl.multiple_of(c * ROWS, ROWS), ROWS)

    def copy(stage, c):
        if stage == 0:
            source, target, who = stack.at[:, 1 - low, rows(c)], first.at[c], 0
        elif stage == 1:
            source, target, who = first.at[c, 1 - high], second.at[c], 1
        elif stage < 2 + levels:
            i = stage - 2
            n, halve = sizes[i]
            before = second if i == 0 else parts[i - 1]
            source = before.at[c, pl.ds((1 - own[i]) * n, n)] if halve else before.at[c]
            target, who = parts[i].at[c], stage
        else:
            i = gathers[stage - 2 - levels]
            n = sizes[i][0]
            where = sum(
                own[j] * sizes[j][0] for j in range(i + 1) if sizes[j][1]
            )
            source = target = whole.at[c, pl.ds(where, n)]
            who = 2 + i
        return pltpu.make_async_remote_copy(
            src_ref=source,
            dst_ref=target,
            send_sem=send.at[stage, c],
            recv_sem=receive.at[stage, c],
            device_id=peers[who],
            device_id_type=MESH,
        )

    gathers = [i for i in reversed(range(levels)) if sizes[i][1]]
    stages = 2 + levels + len(gathers)

    def load_copy(c):
        return pltpu.make_async_copy(stack.at[:, low, rows(c)], keep.at[c], load.at[c])

    def store_copy(c):
        return pltpu.make_async_copy(whole.at[c], out.at[rows(c)], store.at[c])

    def finish(stage, c):
        copy(stage, c).wait_recv()
        if stage == 0:
            load_copy(c).wait()
            add(first.at[c], keep.at[c])
        elif stage == 1:
            add(second.at[c], first.at[c, high])
        elif stage < 2 + levels:
            i = stage - 2
            n, halve = sizes[i]
            before = second if i == 0 else parts[i - 1]
            source = before.at[c, pl.ds(pl.multiple_of(own[i] * n, n), n)] if halve else before.at[c]
            if i < levels - 1:
                add(parts[i].at[c], source)
            else:
                where = sum(own[j] * sizes[j][0] for j in range(levels) if sizes[j][1])
                whole.at[c, pl.ds(pl.multiple_of(where, n), n)][...] = (
                    parts[i].at[c][...].astype(jnp.float32) + source[...].astype(jnp.float32)
                ).astype(jnp.bfloat16)

    def small_copy(i):
        return pltpu.make_async_remote_copy(
            src_ref=small if i == 0 else small_sum.at[i - 1],
            dst_ref=small_in.at[i],
            send_sem=small_send.at[i],
            recv_sem=small_receive.at[i],
            device_id=peers[i],
            device_id_type=MESH,
        )

    small_copy(0).start()

    @pl.loop(0, chunks + LAG * stages)
    def _(t):
        for slot in range(stages + 1):
            c = t - LAG * slot

            @pl.when((c >= 0) & (c < chunks))
            def _():
                if slot == 0:
                    load_copy(c).start()
                else:
                    finish(slot - 1, c)
                if slot < stages:
                    copy(slot, c).start()
                else:
                    store_copy(c).start()

        for i in range(len(bits)):

            @pl.when(t == 2 * i + 1)
            def _():
                small_copy(i).wait_recv()
                total = (small if i == 0 else small_sum.at[i - 1])[...] + small_in[i]
                if i < len(bits) - 1:
                    small_sum[i] = total
                    small_copy(i + 1).start()
                else:
                    small_out[...] = total

    for i in range(len(bits)):
        small_copy(i).wait_send()

    @pl.loop(0, chunks)
    def _(c):
        for stage in range(stages):
            copy(stage, c).wait_send()
        store_copy(c).wait()


def gradient_sum(dp_count, stack, small):
    levels = len(doubling_bits(dp_count))
    chunks = stack.shape[2] // ROWS
    sizes, size, halvings = [], ROWS, 0
    for _ in range(levels):
        halvings += size >= 32
        size = size // 2 if size >= 32 else size
        sizes.append(size)
    stages = 2 + levels + halvings
    half = jnp.bfloat16
    return pl.pallas_call(
        partial(gradient_sum_kernel, dp_count),
        out_shape=(
            jax.ShapeDtypeStruct(stack.shape[2:], half),
            jax.ShapeDtypeStruct(small.shape, jnp.float32),
        ),
        in_specs=[pl.BlockSpec(memory_space=pl.ANY), pl.BlockSpec(memory_space=pltpu.VMEM)],
        out_specs=(pl.BlockSpec(memory_space=pl.ANY), pl.BlockSpec(memory_space=pltpu.VMEM)),
        scratch_shapes=[
            pltpu.VMEM((chunks, 2, ROWS, D), half),
            pltpu.VMEM((chunks, 2, ROWS, D), half),
            pltpu.VMEM((chunks, ROWS, D), half),
        ]
        + [pltpu.VMEM((chunks, n, D), half) for n in sizes]
        + [
            pltpu.VMEM((chunks, ROWS, D), half),
            pltpu.VMEM((levels + 2,) + small.shape, jnp.float32),
            pltpu.VMEM((levels + 1,) + small.shape, jnp.float32),
            pltpu.SemaphoreType.DMA((stages, chunks)),
            pltpu.SemaphoreType.DMA((stages, chunks)),
            pltpu.SemaphoreType.DMA((chunks,)),
            pltpu.SemaphoreType.DMA((chunks,)),
            pltpu.SemaphoreType.DMA((levels + 2,)),
            pltpu.SemaphoreType.DMA((levels + 2,)),
        ],
        compiler_params=pltpu.CompilerParams(
            collective_id=1, has_side_effects=True, vmem_limit_bytes=56 * 2**20
        ),
        name="gradient_sum",
    )(stack, small)


def other(mp, bit):
    return mp + bit - 2 * bit * bit_of(mp, bit)


def greet(dp, mp, dp_count, mp_count):
    barrier = pltpu.get_barrier_semaphore()
    for step in range(1, mp_count):
        pl.semaphore_signal(
            barrier, inc=1, device_id=(dp, lax.rem(mp + step, mp_count)), device_id_type=MESH
        )

    @pl.loop(1, dp_count)
    def _(step):
        pl.semaphore_signal(
            barrier, inc=1, device_id=(lax.rem(dp + step, dp_count), mp), device_id_type=MESH
        )


def greeted(dp_count, mp_count):
    pl.semaphore_wait(pltpu.get_barrier_semaphore(), mp_count + dp_count - 2)


class Spread:
    def __init__(self, value, near, far, send, receive):
        self.dp, self.mp = lax.axis_index("dp"), lax.axis_index("mp")
        self.dp_count, self.mp_count = far.shape[0], near.shape[0]
        self.value, self.near, self.far = value, near, far
        self.send, self.receive = send, receive

    def near_copy(self, step, sender):
        return pltpu.make_async_remote_copy(
            src_ref=self.value,
            dst_ref=self.near.at[sender],
            send_sem=self.send.at[step],
            recv_sem=self.receive.at[step],
            device_id=(self.dp, lax.rem(self.mp + step, self.mp_count)),
            device_id_type=MESH,
        )

    def far_copy(self, step, sender):
        return pltpu.make_async_remote_copy(
            src_ref=self.far.at[self.dp],
            dst_ref=self.far.at[sender],
            send_sem=self.send.at[self.mp_count + step],
            recv_sem=self.receive.at[self.mp_count + step],
            device_id=(lax.rem(self.dp + step, self.dp_count), self.mp),
            device_id_type=MESH,
        )

    def start_near(self):
        for step in range(1, self.mp_count):
            self.near_copy(step, self.mp).start()
        self.near[self.mp] = self.value[...]

    def wait_near(self):
        for step in range(1, self.mp_count):
            self.near_copy(step, lax.rem(self.mp + self.mp_count - step, self.mp_count)).wait_recv()

    def start_far(self):
        @pl.loop(1, self.dp_count)
        def _(step):
            self.far_copy(step, self.dp).start()

    def wait_far(self):
        @pl.loop(1, self.dp_count)
        def _(step):
            self.far_copy(
                step, lax.rem(self.dp + self.dp_count - step, self.dp_count)
            ).wait_recv()

    def wait_near_sends(self):
        for step in range(1, self.mp_count):
            self.near_copy(step, self.mp).wait_send()

    def wait_far_sends(self):
        @pl.loop(1, self.dp_count)
        def _(step):
            self.far_copy(step, self.dp).wait_send()


PIECE = 96
PIECES = 6


def image_kernel(
    x, wq, wk, wv, wo, we, wx, squares, entry, leave, small,
    out, gathered, packed, mask,
    bq, bk, bv, bo, be, bx, load, normed, q, k, v, mixed, middle, bias,
    own, own_load, own_store, send, receive, near, far, small_send, small_receive,
):
    step = pl.program_id(0)
    last = pl.num_programs(0) - 1
    dp, mp = lax.axis_index("dp"), lax.axis_index("mp")
    y_bit, z_bit = bit_of(dp, 1), bit_of(dp, 2)
    across, beside = (dp, other(mp, 2)), (dp, other(mp, 1))
    along, behind = (other(dp, 1), mp), (other(dp, 2), mp)
    pairs = [(wq, bq), (wk, bk), (wv, bv), (wo, bo), (we, be), (wx, bx)]
    spread = Spread(small.at[pl.ds(8, 8)], near, far, small_send, small_receive)

    def load_copy(i):
        return pltpu.make_async_copy(pairs[i][0], pairs[i][1], load.at[i])

    def own_copy(i):
        return pltpu.make_async_copy((leave, entry, squares)[i], own.at[i], own_load.at[i])

    def keep_copy():
        return pltpu.make_async_copy(own, gathered.at[mp], own_store)

    def travel(kind, c):
        if kind == 9:
            source, target, who = own.at[c], gathered.at[mp, c], beside
        else:
            quarter = (y_bit if kind in (0, 1, 2, 3, 6, 7) else 1 - y_bit) + 2 * (
                z_bit if kind in (0, 1, 2, 3, 4, 5) else 1 - z_bit
            )
            matrix = lax.div(c, PIECES // 3)
            start = lax.rem(c, PIECES // 3) * PIECE + quarter * (D // 4)
            rows = pl.ds(pl.multiple_of(start, PIECE), PIECE)
            if kind == 0:
                source, target = own.at[matrix, rows], gathered.at[mp, matrix, rows]
            else:
                source = target = gathered.at[other(mp, 2), matrix, rows]
            who = (across, along, behind, beside, beside, behind, beside, along, beside)[kind]
        return pltpu.make_async_remote_copy(
            src_ref=source,
            dst_ref=target,
            send_sem=send.at[kind, c],
            recv_sem=receive.at[kind, c],
            device_id=who,
            device_id_type=MESH,
        )

    def early_or_late(c, early, late):
        @pl.when(c < PIECES // 2)
        def _():
            early()

        @pl.when(c >= PIECES // 2)
        def _():
            late()

    def forward_first(c):
        travel(0, c).wait_recv()
        for kind in (1, 2, 3):
            travel(kind, c).start()

    def forward_second(c):
        travel(1, c).wait_recv()
        travel(4, c).start()
        travel(2, c).wait_recv()
        travel(6, c).start()
        early_or_late(c, travel(5, c).start, travel(7, c).start)

    def forward_third(c):
        early_or_late(c, travel(5, c).wait_recv, travel(7, c).wait_recv)
        travel(8, c).start()

    def pump(j):
        n = step * 4 + j

        for lag, forward in ((3, forward_first), (6, forward_second), (10, forward_third)):

            @pl.when((n >= lag) & (n < lag + PIECES))
            def _():
                forward(n - lag)

    @pl.when(step == 0)
    def _():
        for i in range(3):
            own_copy(i).start()
        for i in range(6):
            load_copy(i).start()
        greet(dp, mp, far.shape[0], near.shape[0])
        for p in range(4):
            row = lax.broadcasted_iota(jnp.int32, (WINDOW, WINDOW), 0) + STEP * p
            column = lax.broadcasted_iota(jnp.int32, (WINDOW, WINDOW), 1) + STEP * p
            bias[p] = jnp.where(row // PATCHES == column // PATCHES, 0.0, -1e30)

    def ready(i):
        @pl.when(step == 0)
        def _():
            load_copy(i).wait()

    z = x[...].astype(jnp.float32)
    normed[...] = centre(z).astype(jnp.bfloat16)
    ready(0)
    q[...] = (dot(normed[...], bq[...]) * SCALE).astype(jnp.bfloat16)

    @pl.when(step == 0)
    def _():
        greeted(far.shape[0], near.shape[0])
        spread.start_near()
        for i in range(3):
            own_copy(i).wait()

        @pl.loop(0, PIECES)
        def _(c):
            travel(0, c).start()

        for i in range(3):
            travel(9, i).start()
        keep_copy().start()

    ready(1)
    k[...] = dot(normed[...], bk[...]).astype(jnp.bfloat16)
    ready(2)
    v[...] = dot(normed[...], bv[...]).astype(jnp.bfloat16)
    pump(0)
    first = lax.broadcasted_iota(jnp.int32, (WINDOW, 128), 1) < HD

    @pl.when(step == 1)
    def _():
        spread.wait_near()
        group = near[0] + near[1]
        for m in range(2, near.shape[0]):
            group = group + near[m]
        packed[pl.ds(0, 4), :] = group[:4]
        for m in range(QUARTERS):
            packed[pl.ds(4 + m, 1), :] = near[m, pl.ds(3, 1), :]
        far[dp] = jnp.broadcast_to(group[2:3, :128], (8, 128))
        spread.start_far()

    for p in range(4):
        if p == 2:
            pump(1)
        rows = pl.ds(STEP * p, WINDOW)
        for h in range(HEADS // 2):
            lanes = pl.ds(128 * h, 128)
            part = q[rows, lanes]
            none = jnp.zeros_like(part)
            both = jnp.concatenate([jnp.where(first, part, none), jnp.where(first, none, part)])
            scores = dot_nt(both, k[rows, lanes])
            scores = scores + jnp.concatenate([bias[p], bias[p]])
            weights = jnp.exp(scores - jnp.max(scores, axis=-1, keepdims=True))
            probs = (weights * (1.0 / jnp.sum(weights, axis=-1, keepdims=True))).astype(jnp.bfloat16)
            heads = dot(probs, v[rows, lanes])
            merged = jnp.where(first, heads[:WINDOW], heads[WINDOW:]).astype(jnp.bfloat16)
            if p:
                edge = pl.ds(STEP * p, 16)
                late = lax.broadcasted_iota(jnp.int32, (16, 128), 0) >= 2 * PATCHES * p - STEP * p
                mixed[edge, lanes] = jnp.where(late, merged[:16], mixed[edge, lanes])
                mixed[pl.ds(STEP * p + 16, WINDOW - 16), lanes] = merged[16:]
            else:
                mixed[rows, lanes] = merged
    pump(2)
    ready(3)
    middle[...] = x[...].astype(jnp.float32) + dot(mixed[...], bo[...])
    normed[...] = centre(middle[...]).astype(jnp.bfloat16)
    ready(4)
    ready(5)
    for c in range(4):
        if c == 2:
            pump(3)
        part = pl.ds(c * D, D)
        active = gelu(dot(normed[...], be[:, part])).astype(jnp.bfloat16)
        middle[...] += dot(active, bx[part, :])

    total = middle[...]
    high = total.astype(jnp.bfloat16)
    low = (total - high.astype(jnp.float32)).astype(jnp.bfloat16)
    owner = lax.broadcasted_iota(jnp.int32, (8, BLOCK), 1) // PATCHES
    pool = jnp.where(owner == lax.broadcasted_iota(jnp.int32, (8, BLOCK), 0), 1.0, 0.0)
    pool = pool.astype(jnp.bfloat16)
    pooled = (dot(pool, high) + dot(pool, low)) * (1.0 / PATCHES)
    out[...] = normalize(pooled)

    @pl.when(step == last)
    def _():
        spread.wait_far()
        for d in range(far.shape[0]):
            mask[:, pl.ds(128 * d, 128)] = far[d, pl.ds(0, 1), :]
        spread.wait_near_sends()
        spread.wait_far_sends()
        keep_copy().wait()
        for i in range(3):
            travel(9, i).wait()

        @pl.loop(0, PIECES)
        def _(c):
            for kind in (3, 4, 6, 8):
                travel(kind, c).wait_recv()
            for kind in (0, 1, 2, 3, 4, 6, 8):
                travel(kind, c).wait_send()
            early_or_late(c, travel(5, c).wait_send, travel(7, c).wait_send)


def image_layer(dp_count, mp_count, tokens, frozen, squares, entry, leave, small):
    half = jnp.bfloat16
    any_space = pl.BlockSpec(memory_space=pl.ANY)
    blocks = tokens.shape[0] // BLOCK
    square = pltpu.VMEM((D, D), half)
    rows = pltpu.VMEM((BLOCK, D), half)
    kinds = pltpu.SemaphoreType.DMA((10, PIECES))
    return pl.pallas_call(
        image_kernel,
        grid=(blocks,),
        out_shape=(
            jax.ShapeDtypeStruct((blocks * 8, D), jnp.float32),
            jax.ShapeDtypeStruct((mp_count, 3, D, D), half),
            jax.ShapeDtypeStruct((8, D), jnp.float32),
            jax.ShapeDtypeStruct((1, dp_count * 128), jnp.float32),
        ),
        in_specs=[pl.BlockSpec((BLOCK, D), lambda i: (i, 0))]
        + [any_space] * 9
        + [pl.BlockSpec(memory_space=pltpu.VMEM)],
        out_specs=(
            pl.BlockSpec((8, D), lambda i: (i, 0)),
            any_space,
            pl.BlockSpec(memory_space=pltpu.VMEM),
            pl.BlockSpec(memory_space=pltpu.VMEM),
        ),
        scratch_shapes=[square] * 4
        + [
            pltpu.VMEM((D, 4 * D), half),
            pltpu.VMEM((4 * D, D), half),
            pltpu.SemaphoreType.DMA((6,)),
        ]
        + [rows] * 5
        + [
            pltpu.VMEM((BLOCK, D), jnp.float32),
            pltpu.VMEM((4, WINDOW, WINDOW), jnp.float32),
            pltpu.VMEM((3, D, D), half),
            pltpu.SemaphoreType.DMA((3,)),
            pltpu.SemaphoreType.DMA,
            kinds,
            kinds,
            pltpu.VMEM((mp_count, 8, D), jnp.float32),
            pltpu.VMEM((dp_count, 8, 128), jnp.float32),
            pltpu.SemaphoreType.DMA((mp_count + dp_count,)),
            pltpu.SemaphoreType.DMA((mp_count + dp_count,)),
        ],
        compiler_params=pltpu.CompilerParams(
            collective_id=3, has_side_effects=True, vmem_limit_bytes=56 * 2**20
        ),
        name="image_layer",
    )(tokens, *frozen, squares, entry, leave, small)


def gelu_slope(v):
    bend = jnp.tanh(0.7978845608028654 * (v + 0.044715 * v * v * v))
    inner = 0.7978845608028654 * (1.0 + 0.134145 * v * v)
    return 0.5 * (1.0 + bend) + 0.5 * v * (1.0 - bend * bend) * inner


def hat(tensor):
    centred = tensor - jnp.mean(tensor, axis=-1, keepdims=True)
    inverse = lax.rsqrt(jnp.mean(centred * centred, axis=-1, keepdims=True) + 1e-06)
    return centred * inverse, inverse


def hat_back(unit, inverse, grad):
    mean = jnp.mean(grad, axis=-1, keepdims=True)
    return inverse * (grad - mean - unit * jnp.mean(grad * unit, axis=-1, keepdims=True))


def split(v):
    high = v.astype(jnp.bfloat16)
    return jnp.concatenate([high, (v - high.astype(jnp.float32)).astype(jnp.bfloat16)])


def total_of(v):
    return jnp.sum(jnp.sum(v, axis=1, keepdims=True), axis=0, keepdims=True)


class Gather:
    def __init__(self, own, blocks, sems):
        self.dp, self.mp = lax.axis_index("dp"), lax.axis_index("mp")
        self.own, self.blocks, self.count = own, blocks, blocks.shape[0]
        self.sems = sems

    def copy(self, kind, step):
        who = lax.rem(self.dp + self.count - step, self.count)
        lane = other(self.mp, 2) if kind == 3 else self.mp
        target = (self.dp, other(self.mp, 2 if kind == 1 else 1))
        if kind == 0:
            who, target = self.dp, (lax.rem(self.dp + step, self.count), self.mp)
        home = kind == 0 or (kind < 3 and isinstance(step, int) and step == 0)
        block = self.blocks.at[who, lane]
        return pltpu.make_async_remote_copy(
            src_ref=self.own if home else block,
            dst_ref=block,
            send_sem=self.sems[0].at[kind, step],
            recv_sem=self.sems[1].at[kind, step],
            device_id=target,
            device_id_type=MESH,
        )

    def start(self):
        @pl.loop(1, self.count)
        def _(step):
            self.copy(0, step).start()

        self.copy(1, 0).start()
        self.copy(2, 0).start()

    def forward(self, low, high):
        @pl.loop(low, high)
        def _(step):
            self.copy(0, step).wait_recv()
            self.copy(1, step).start()
            self.copy(2, step).start()

    def forward_last(self):
        @pl.loop(0, self.count)
        def _(step):
            self.copy(1, step).wait_recv()
            self.copy(3, step).start()

    def arrive(self):
        @pl.loop(0, self.count)
        def _(step):
            self.copy(2, step).wait_recv()
            self.copy(3, step).wait_recv()

    def wait_sends(self):
        @pl.loop(1, self.count)
        def _(step):
            self.copy(0, step).wait_send()

        @pl.loop(0, self.count)
        def _(step):
            for kind in (1, 2, 3):
                self.copy(kind, step).wait_send()


class FactorGather:
    def __init__(self, sums, blocks, near, line, mate, keep):
        self.dp, self.mp = lax.axis_index("dp"), lax.axis_index("mp")
        self.sums, self.blocks = sums, blocks
        self.near, self.line, self.mate, self.keep = near, line, mate, keep
        self.count, self.half = blocks.shape[0], blocks.shape[0] // 2

    def near_copy(self, step):
        to = lax.rem(self.mp + step, QUARTERS)
        return pltpu.make_async_remote_copy(
            src_ref=self.sums.at[to],
            dst_ref=self.blocks.at[self.dp, self.mp],
            send_sem=self.near[0].at[step],
            recv_sem=self.near[1].at[step],
            device_id=(self.dp, to),
            device_id_type=MESH,
        )

    def keep_copy(self):
        return pltpu.make_async_copy(
            self.sums.at[self.mp], self.blocks.at[self.dp, self.mp], self.keep
        )

    def line_copy(self, step):
        return pltpu.make_async_remote_copy(
            src_ref=self.blocks.at[self.dp],
            dst_ref=self.blocks.at[self.dp],
            send_sem=self.line[0].at[step],
            recv_sem=self.line[1].at[step],
            device_id=(lax.rem(self.dp + 2 * step, self.count), self.mp),
            device_id_type=MESH,
        )

    def mate_copy(self, step):
        block = self.blocks.at[lax.rem(self.dp + self.count - 2 * step, self.count)]
        return pltpu.make_async_remote_copy(
            src_ref=block,
            dst_ref=block,
            send_sem=self.mate[0].at[step],
            recv_sem=self.mate[1].at[step],
            device_id=(other(self.dp, 1), self.mp),
            device_id_type=MESH,
        )

    def start(self):
        self.keep_copy().start()
        for step in range(1, QUARTERS):
            self.near_copy(step).start()

    def spread(self):
        self.keep_copy().wait()
        for step in range(1, QUARTERS):
            self.near_copy(step).wait_recv()

        @pl.loop(1, self.half)
        def _(step):
            self.line_copy(step).start()

        self.mate_copy(0).start()

    def forward(self, low, high):
        @pl.loop(low, high)
        def _(step):
            self.line_copy(step).wait_recv()
            self.mate_copy(step).start()

    def finish(self):
        @pl.loop(0, self.half)
        def _(step):
            self.mate_copy(step).wait()

        @pl.loop(1, self.half)
        def _(step):
            self.line_copy(step).wait_send()

        for step in range(1, QUARTERS):
            self.near_copy(step).wait_send()


def text_kernel(
    x, image, image_mask, params, packed, gathered,
    text_out, in_grad, stack, vectors, plain, factors, rows_all,
    squares, entry, leave, load, images, image_sems, image_arrivals, row_sems, row_arrivals,
    own_rows, own_keep, factor_near, factor_near_in, factor_line, factor_line_in, factor_mate,
    factor_mate_in, factor_keep, normed, q, k, v, mixed, middle, normed_two, pre, sums, bias,
    stage, stage_sem, logits, value, near, far, column_send, column_receive,
):
    work, mixed_grad = in_grad, normed_two
    g1, s1, b_o, g2, s2, b_p = [params.at[pl.ds(i, 1)] for i in range(6)]
    b_q, b_v = packed.at[pl.ds(0, 1)], packed.at[pl.ds(1, 1)]
    own_count = image.shape[0]
    own_line = jnp.broadcast_to(params[pl.ds(6, 1), pl.ds(0, 128)], (own_count, 128))
    line_lane = lax.broadcasted_iota(jnp.int32, (own_count, 128), 1)
    line_row = lax.broadcasted_iota(jnp.int32, (own_count, 128), 0)

    def standing(shift):
        return jnp.sum(jnp.where(line_lane == line_row + shift, own_line, 0.0), axis=1, keepdims=True)

    own_text, own_pair = standing(0), standing(own_count)
    dp, mp = lax.axis_index("dp"), lax.axis_index("mp")
    dp_count, mp_count = far.shape[0], near.shape[0]
    rows_count = x.shape[0]
    part_rows = D // QUARTERS
    half = jnp.bfloat16

    def square_copy(i, m):
        return pltpu.make_async_copy(
            gathered.at[m, 2, pl.ds(i * part_rows, part_rows)],
            squares.at[i, pl.ds(m * part_rows, part_rows)],
            load.at[i, m],
        )

    def entry_copy(m):
        return pltpu.make_async_copy(gathered.at[m, 1], entry.at[m], load.at[4, m])

    def leave_copy(m):
        return pltpu.make_async_copy(gathered.at[m, 0], leave.at[m], load.at[5, m])

    for i in range(4):
        for m in range(QUARTERS):
            square_copy(i, m).start()
    for m in range(QUARTERS):
        entry_copy(m).start()
        leave_copy(m).start()
    images[dp, mp] = image[...].astype(half)
    greet(dp, mp, dp_count, mp_count)
    greeted(dp_count, mp_count)

    image_gather = Gather(images.at[dp, mp], images, (image_sems, image_arrivals))
    image_gather.start()
    row_gather = Gather(own_rows, rows_all, (row_sems, row_arrivals))
    factor_gather = FactorGather(
        sums,
        factors,
        (factor_near, factor_near_in),
        (factor_line, factor_line_in),
        (factor_mate, factor_mate_in),
        factor_keep,
    )

    def own_rows_copy():
        return pltpu.make_async_copy(own_rows, rows_all.at[dp, mp], own_keep)

    row = lax.broadcasted_iota(jnp.int32, (TEXT_WINDOW, TEXT_WINDOW), 0)
    column = lax.broadcasted_iota(jnp.int32, (TEXT_WINDOW, TEXT_WINDOW), 1)
    bias[...] = jnp.where((row // LEN == column // LEN) & (column <= row), 0.0, -1e30)
    first = lax.broadcasted_iota(jnp.int32, (TEXT_WINDOW, 128), 1) < HD

    unit, unused = hat(x[...].astype(jnp.float32))
    normed[...] = (unit * g1[...] + s1[...]).astype(half)
    for m in range(QUARTERS):
        square_copy(0, m).wait()
    q[...] = ((dot_nt(normed[...], squares[0]) + b_q[...]) * SCALE).astype(half)
    for m in range(QUARTERS):
        square_copy(1, m).wait()
    k[...] = dot_nt(normed[...], squares[1]).astype(half)
    for m in range(QUARTERS):
        square_copy(2, m).wait()
    v[...] = (dot_nt(normed[...], squares[2]) + b_v[...]).astype(half)

    def doubled(part):
        none = jnp.zeros_like(part)
        return jnp.concatenate([jnp.where(first, part, none), jnp.where(first, none, part)])

    def probabilities(both, keys):
        scores = dot_nt(both, keys) + jnp.concatenate([bias[...], bias[...]])
        weights = jnp.exp(scores - jnp.max(scores, axis=-1, keepdims=True))
        return weights * (1.0 / jnp.sum(weights, axis=-1, keepdims=True))

    def merge(heads):
        return jnp.where(first, heads[:TEXT_WINDOW], heads[TEXT_WINDOW:])

    @pl.loop(0, rows_count // TEXT_WINDOW)
    def _(w):
        rows = pl.ds(pl.multiple_of(w * TEXT_WINDOW, TEXT_WINDOW), TEXT_WINDOW)
        for h in range(HEADS // 2):
            lanes = pl.ds(128 * h, 128)
            probs = probabilities(doubled(q[rows, lanes]), k[rows, lanes]).astype(half)
            mixed[rows, lanes] = merge(dot(probs, v[rows, lanes])).astype(half)

    image_gather.forward(1, dp_count)
    for m in range(QUARTERS):
        square_copy(3, m).wait()
    middle[...] = x[...].astype(jnp.float32) + dot(mixed[...], squares[3]) + b_o[...]
    unit, unused = hat(middle[...])
    normed_two[...] = (unit * g2[...] + s2[...]).astype(half)
    owner = lax.broadcasted_iota(jnp.int32, (own_count, rows_count), 1) // LEN
    pool = jnp.where(owner == lax.broadcasted_iota(jnp.int32, (own_count, rows_count), 0), 1.0, 0.0)
    pool = pool.astype(half)
    work[...] = middle[...] + b_p[...]

    @pl.loop(0, QUARTERS // 2)
    def _(pair):
        @pl.when(pair == 1)
        def _():
            image_gather.forward_last()

        for m in (2 * pair, 2 * pair + 1):
            entry_copy(m).wait()
            leave_copy(m).wait()
            hidden = dot(normed_two[...], entry[m]) + packed[pl.ds(4 + m, 1), :]
            pre[m] = hidden
            active = gelu(hidden).astype(half)
            sums[m] = dot(pool, active).astype(half)
            work[...] += dot(active, leave[m])

    factor_gather.start()
    text_out[...] = work[...].astype(half)
    output = split(work[...])
    pooled = (dot(pool, output[:rows_count]) + dot(pool, output[rows_count:])) * (1.0 / LEN)

    image_gather.arrive()
    text_unit = normalize(pooled)
    everyone = image_mask.shape[1]
    width = LOSS_WIDTH
    multiplier = jnp.exp(params[pl.ds(7, 1), pl.ds(0, 1)])
    text_half = text_unit.astype(half)
    tiles = everyone // 128
    group_count = width // (mp_count * own_count)
    sections = [pl.ds(c * width, width) for c in range(everyone // width)]

    def images_of(c):
        return images[pl.ds(c * group_count, group_count)].reshape(width, D)

    def hits_of(c):
        place = lax.broadcasted_iota(jnp.int32, (own_count, width), 1) + c * width
        return jnp.where(place.astype(jnp.float32) == own_pair, 1.0, 0.0)

    row_total = text_hits = hit_logit = jnp.zeros((own_count, 1), jnp.float32)
    for c, lanes in enumerate(sections):
        logits[:, lanes] = dot_nt(text_half, images_of(c)) * multiplier
        hits = hits_of(c)
        weights = jnp.exp(logits[:, lanes])
        row_total += jnp.sum(weights * image_mask[:, lanes], axis=1, keepdims=True)
        text_hits += jnp.sum(hits * image_mask[:, lanes], axis=1, keepdims=True)
        hit_logit += jnp.sum(hits * logits[:, lanes], axis=1, keepdims=True)
        column_part = jnp.sum(weights * own_text, axis=0, keepdims=True)
        owner_part = jnp.sum(hits * own_text, axis=0, keepdims=True)
        for i in range(width // 128):
            piece = slice(128 * i, 128 * i + 128)
            value[pl.ds(c * width // 128 + i, 1), :] = column_part[:, piece]
            value[pl.ds(tiles + c * width // 128 + i, 1), :] = owner_part[:, piece]
    spread = Spread(value, near, far, column_send, column_receive)
    spread.start_near()
    safe_row = jnp.where(row_total > 0, row_total, 1.0)
    text_weight = own_text * text_hits
    total_part = total_of(0.5 * text_weight * jnp.log(safe_row) - text_weight * hit_logit)
    spread.wait_near()
    group = near[0]
    for i in range(1, mp_count):
        group = group + near[i]
    far[dp] = group
    spread.start_far()
    text_grad = jnp.zeros((own_count, D), jnp.float32)
    temp_part = column_loss = pairs = jnp.zeros((1, 1), jnp.float32)
    for c, lanes in enumerate(sections):
        row_weights = jnp.exp(logits[:, lanes]) * image_mask[:, lanes]
        row_grad = 0.5 * text_weight * (row_weights / safe_row - hits_of(c))
        temp_part += total_of(row_grad * logits[:, lanes])
        text_grad += dot((multiplier * row_grad).astype(half), images_of(c))
    spread.wait_far()
    spread.wait_near_sends()
    value[...] = far[0]

    @pl.loop(1, dp_count)
    def _(i):
        value[...] += far[i]

    def line_of(start):
        return jnp.concatenate([value[pl.ds(start + i, 1), :] for i in range(width // 128)], axis=1)

    for c, lanes in enumerate(sections):
        column_total = line_of(c * width // 128)
        image_weight = image_mask[:, lanes] * line_of(tiles + c * width // 128)
        safe_column = jnp.where(column_total > 0, column_total, 1.0)
        column_weights = jnp.exp(logits[:, lanes]) * own_text
        column_grad = 0.5 * image_weight * (column_weights / safe_column - hits_of(c))
        temp_part += total_of(column_grad * logits[:, lanes])
        column_loss += total_of(0.5 * image_weight * jnp.log(safe_column))
        pairs += total_of(image_weight)
        text_grad += dot((multiplier * column_grad).astype(half), images_of(c))
    lane = lax.broadcasted_iota(jnp.int32, (8, D), 1)
    plain[...] = jnp.where(lane == 0, column_loss, jnp.where(lane == 1, pairs, 0.0))
    vectors[pl.ds(8, 8), :] = jnp.where(lane == 0, total_part, jnp.where(lane == 1, temp_part, 0.0))

    inverse = lax.rsqrt(jnp.sum(pooled * pooled, axis=-1, keepdims=True) + 1e-06)
    caption_grad = (1.0 / LEN) * inverse * (
        text_grad - text_unit * jnp.sum(text_unit * text_grad, axis=-1, keepdims=True)
    )
    vectors[pl.ds(5, 1), :] = LEN * jnp.sum(caption_grad, axis=0, keepdims=True)
    spot = lax.broadcasted_iota(jnp.int32, (rows_count, own_count), 0) // LEN
    repeat = jnp.where(
        spot == lax.broadcasted_iota(jnp.int32, (rows_count, own_count), 1), 1.0, 0.0
    ).astype(half)
    caption_half = caption_grad.astype(half)
    own_rows[...] = caption_half
    factor_gather.spread()
    own_rows_copy().start()
    row_gather.start()
    grad_rows = dot(repeat, caption_half).astype(half)

    def stage_copies(piece):
        if not isinstance(piece, int) or piece < 4:
            slot = lax.rem(piece, 3)
            return [
                pltpu.make_async_copy(
                    stage.at[slot],
                    stack.at[lax.div(piece, 2), lax.rem(piece, 2), pl.ds(0, D)],
                    stage_sem.at[slot, 0],
                )
            ]
        slot = piece % 3
        place = D + (3, 0, 1, 2)[piece - 4] * part_rows
        return [
            pltpu.make_async_copy(
                stage.at[slot, pl.ds(m * part_rows, part_rows)],
                stack.at[m // 2, m % 2, pl.ds(place, part_rows)],
                stage_sem.at[slot, m],
            )
            for m in range(QUARTERS)
        ]

    def emit(piece, gradient):
        for copy in stage_copies(piece - 3):
            copy.wait()
        stage[piece % 3] = gradient.astype(half)
        for copy in stage_copies(piece):
            copy.start()

    work[...] = jnp.zeros_like(work)

    @pl.loop(0, QUARTERS)
    def _(m):
        active_grad = dot_nt(grad_rows, leave[m])
        hidden_grad = active_grad * gelu_slope(pre[m])
        hidden_half = hidden_grad.astype(half)
        vectors[pl.ds(9 + m, 1), :] = jnp.sum(
            hidden_half.astype(jnp.float32), axis=0, keepdims=True
        )

        @pl.when(m >= 3)
        def _():
            for copy in stage_copies(m - 3):
                copy.wait()

        stage[lax.rem(m, 3)] = dot_tn(normed_two[...], hidden_half).astype(half)
        for copy in stage_copies(m):
            copy.start()
        work[...] += dot_nt(hidden_half, entry[m])

    unit, inverse = hat(middle[...])
    grad = work[...]
    vectors[pl.ds(3, 1), :] = jnp.sum(grad * unit, axis=0, keepdims=True)
    vectors[pl.ds(4, 1), :] = jnp.sum(grad, axis=0, keepdims=True)
    caption_parts = split(caption_grad)
    token_grad = dot(repeat, caption_parts[:own_count]) + dot(repeat, caption_parts[own_count:])
    middle_grad = token_grad + hat_back(unit, inverse, grad * g2[...])
    middle[...] = middle_grad
    vectors[pl.ds(2, 1), :] = jnp.sum(middle_grad, axis=0, keepdims=True)
    attn_grad = middle_grad.astype(half)
    factor_gather.forward(1, (dp_count // 2 + 1) // 2)
    emit(4, dot_tn(mixed[...], attn_grad))
    mixed_grad[...] = dot_nt(attn_grad, squares[3]).astype(half)

    @pl.loop(0, rows_count // TEXT_WINDOW)
    def _(w):
        rows = pl.ds(pl.multiple_of(w * TEXT_WINDOW, TEXT_WINDOW), TEXT_WINDOW)
        for h in range(HEADS // 2):
            lanes = pl.ds(128 * h, 128)
            queries, keys, values = doubled(q[rows, lanes]), k[rows, lanes], v[rows, lanes]
            probs = probabilities(queries, keys)
            outer = doubled(mixed_grad[rows, lanes])
            probs_grad = dot_nt(outer, values)
            v[rows, lanes] = dot_tn(probs.astype(half), outer).astype(half)
            inner = jnp.sum(probs * probs_grad, axis=-1, keepdims=True)
            score_grad = (probs * (probs_grad - inner)).astype(half)
            q[rows, lanes] = (merge(dot(score_grad, keys)) * SCALE).astype(half)
            k[rows, lanes] = dot_tn(score_grad, queries).astype(half)

    factor_gather.forward((dp_count // 2 + 1) // 2, dp_count // 2)
    vectors[pl.ds(6, 1), :] = jnp.sum(q[...].astype(jnp.float32), axis=0, keepdims=True)
    vectors[pl.ds(7, 1), :] = jnp.sum(v[...].astype(jnp.float32), axis=0, keepdims=True)
    for i, part in enumerate([q, k, v]):
        emit(5 + i, dot_tn(part[...], normed[...]))
    row_gather.forward(1, dp_count)
    work[...] = (
        dot(q[...], squares[0]) + dot(k[...], squares[1]) + dot(v[...], squares[2])
    )
    unit, inverse = hat(x[...].astype(jnp.float32))
    grad = work[...]
    vectors[pl.ds(0, 1), :] = jnp.sum(grad * unit, axis=0, keepdims=True)
    vectors[pl.ds(1, 1), :] = jnp.sum(grad, axis=0, keepdims=True)
    in_grad[...] = middle[...] + hat_back(unit, inverse, grad * g1[...])

    row_gather.forward_last()
    for piece in range(5, 8):
        for copy in stage_copies(piece):
            copy.wait()
    spread.wait_far_sends()
    own_rows_copy().wait()
    factor_gather.finish()
    row_gather.arrive()
    row_gather.wait_sends()
    image_gather.wait_sends()


def text_layer(dp_count, mp_count, operands, gathered):
    half = jnp.bfloat16
    vmem, any_space = pl.BlockSpec(memory_space=pltpu.VMEM), pl.BlockSpec(memory_space=pl.ANY)
    rows_count, own_count = operands[0].shape[0], operands[1].shape[0]
    lines = 2 * dp_count * mp_count * own_count // 128
    rows = pltpu.VMEM((rows_count, D), half)
    wide = pltpu.VMEM((rows_count, D), jnp.float32)
    matrices = pltpu.VMEM((QUARTERS, D, D), half)
    kinds, few = pltpu.SemaphoreType.DMA((4, dp_count)), pltpu.SemaphoreType.DMA((QUARTERS,))
    line = pltpu.SemaphoreType.DMA((dp_count // 2,))
    everyone = jax.ShapeDtypeStruct((dp_count, mp_count, own_count, D), half)
    column = pltpu.SemaphoreType.DMA((mp_count + dp_count,))
    return pl.pallas_call(
        text_kernel,
        out_shape=(
            jax.ShapeDtypeStruct((rows_count, D), half),
            jax.ShapeDtypeStruct((rows_count, D), jnp.float32),
            jax.ShapeDtypeStruct((2, 2, 2 * D, D), half),
            jax.ShapeDtypeStruct((16, D), jnp.float32),
            jax.ShapeDtypeStruct((8, D), jnp.float32),
            everyone,
            everyone,
        ),
        in_specs=[vmem] * len(operands) + [any_space],
        out_specs=(vmem, vmem, any_space, vmem, vmem, any_space, any_space),
        scratch_shapes=[
            matrices,
            matrices,
            matrices,
            pltpu.SemaphoreType.DMA((6, QUARTERS)),
            pltpu.VMEM((dp_count, mp_count, own_count, D), half),
            kinds,
            kinds,
            kinds,
            kinds,
            pltpu.VMEM((own_count, D), half),
            pltpu.SemaphoreType.DMA,
            few,
            few,
            line,
            line,
            line,
            line,
            pltpu.SemaphoreType.DMA,
        ]
        + [rows] * 5
        + [
            wide,
            rows,
            pltpu.VMEM((QUARTERS, rows_count, D), jnp.float32),
            pltpu.VMEM((QUARTERS, own_count, D), half),
        ]
        + [
            pltpu.VMEM((TEXT_WINDOW, TEXT_WINDOW), jnp.float32),
            pltpu.VMEM((3, D, D), half),
            pltpu.SemaphoreType.DMA((3, QUARTERS)),
            pltpu.VMEM((own_count, lines * 64), jnp.float32),
            pltpu.VMEM((lines, 128), jnp.float32),
            pltpu.VMEM((mp_count, lines, 128), jnp.float32),
            pltpu.VMEM((dp_count, lines, 128), jnp.float32),
            column,
            column,
        ],
        compiler_params=pltpu.CompilerParams(
            collective_id=2, has_side_effects=True, vmem_limit_bytes=67043328
        ),
        name="text_layer",
    )(*operands, gathered)


def body(
    sentence_entry_words,
    sentence_present_marks,
    picture_present_marks,
    matched_picture_positions,
    stored_picture_patches,
    log_logit_multiplier,
    leading_standardizer_stretch,
    leading_standardizer_shift,
    lookup_coefficients,
    lookup_offset,
    address_coefficients,
    content_coefficients,
    content_offset,
    mixer_exit_coefficients,
    mixer_exit_offset,
    trailing_standardizer_stretch,
    trailing_standardizer_shift,
    perceptron_entry_coefficients,
    perceptron_inner_offset,
    perceptron_exit_coefficients,
    perceptron_exit_offset,
    picture_lookup_coefficients,
    picture_address_coefficients,
    picture_content_coefficients,
    picture_mixer_exit,
    picture_perceptron_entry,
    picture_perceptron_exit,
):
    own_count = sentence_present_marks.shape[0]
    dp_count, mp_count = lax.axis_size("dp"), lax.axis_size("mp")
    rank = lax.axis_index("mp")
    squares = jnp.concatenate(
        [
            lookup_coefficients.T,
            address_coefficients.T,
            content_coefficients.T,
            mixer_exit_coefficients,
        ]
    )
    quarter = D // mp_count

    offset = lax.axis_index(("dp", "mp")) * own_count
    own_pair = lax.dynamic_slice_in_dim(matched_picture_positions, offset, own_count, 0)

    def placed(vector):
        return jnp.concatenate([jnp.where(rank == m, vector, 0.0) for m in range(mp_count)])

    def padded(*parts):
        filled = sum(part.shape[0] for part in parts)
        return parts + (jnp.zeros((-filled % D,), jnp.float32),)

    small = jnp.concatenate(
        (
            leading_standardizer_stretch,
            leading_standardizer_shift,
            mixer_exit_offset,
            trailing_standardizer_stretch,
            trailing_standardizer_shift,
            perceptron_exit_offset,
        )
        + padded(sentence_present_marks.astype(jnp.float32), own_pair.astype(jnp.float32))
        + padded(log_logit_multiplier)
        + (placed(lookup_offset), placed(content_offset))
        + padded(placed(picture_present_marks.astype(jnp.float32)))
        + (perceptron_inner_offset, jnp.zeros((4 * D,), jnp.float32))
    ).reshape(16, D)
    image, gathered, packed, image_mask = image_layer(
        dp_count,
        mp_count,
        stored_picture_patches,
        (
            picture_lookup_coefficients,
            picture_address_coefficients,
            picture_content_coefficients,
            picture_mixer_exit,
            picture_perceptron_entry,
            picture_perceptron_exit,
        ),
        squares,
        perceptron_entry_coefficients,
        perceptron_exit_coefficients,
        small,
    )
    output, text_in_grad, stack, vectors, plain, factors, rows_all = text_layer(
        dp_count,
        mp_count,
        (sentence_entry_words, image, image_mask, small, packed),
        gathered,
    )
    w_proj_grad = dot_tn(factors.reshape(-1, D), rows_all.reshape(-1, D))
    own_grads, shared = gradient_sum(dp_count, stack, vectors)
    loss = jnp.reshape((shared[8, 0] + plain[0, 0]) / plain[0, 1], (1,))

    def rows_of(start, count):
        return own_grads[start : start + count].astype(jnp.float32)

    def own(vector):
        return lax.dynamic_slice_in_dim(vector, rank * quarter, quarter, 0)

    return (
        loss,
        output,
        text_in_grad,
        shared[8, 1:2],
        shared[0],
        shared[1],
        rows_of(D, quarter).T,
        own(shared[6]),
        rows_of(D + 1 * quarter, quarter).T,
        rows_of(D + 2 * quarter, quarter).T,
        own(shared[7]),
        rows_of(D + 3 * quarter, quarter),
        shared[2],
        shared[3],
        shared[4],
        rows_of(0, D),
        lax.dynamic_slice_in_dim(shared, 9 + rank, 1, 0)[0],
        w_proj_grad,
        shared[5],
    )


def solution(mesh):
    in_specs = (
        P(("dp", "mp"), None),
        P(("dp", "mp")),
        P(("dp", "mp")),
        P(),
        P(("dp", "mp"), None),
        P(),
        P(),
        P(),
        P(None, "mp"),
        P("mp"),
        P(None, "mp"),
        P(None, "mp"),
        P("mp"),
        P("mp", None),
        P(),
        P(),
        P(),
        P(None, "mp"),
        P("mp"),
        P("mp", None),
        P(),
        P(),
        P(),
        P(),
        P(),
        P(),
        P(),
    )
    out_specs = (
        P(),
        P(("dp", "mp"), None),
        P(("dp", "mp"), None),
        P(),
        P(),
        P(),
        P(None, "mp"),
        P("mp"),
        P(None, "mp"),
        P(None, "mp"),
        P("mp"),
        P("mp", None),
        P(),
        P(),
        P(),
        P(None, "mp"),
        P("mp"),
        P("mp", None),
        P(),
    )
    return jax.shard_map(body, mesh=mesh, in_specs=in_specs, out_specs=out_specs, check_vma=False)
```
